32 devices in a mesh: dp: 16 (over z, x, core), tensor: 2 (over y).
Axes of the slice: x: 2, y: 2, z: 4, core: 2. Of those that a mesh axis runs over, the one named last changes fastest.
Arguments:
- hidden: bfloat16 [2, 16384, 768], P(None, ('dp', 'tensor')), may hold values from -6 to 6
- lengths: int32 [2, 16], P(None, 'dp'), may hold values from 256 to 1024, as said below
- cotangent: bfloat16 [2, 16384, 768], P(None, ('dp', 'tensor')), may hold values from -6 to 6
- w_query: bfloat16 [768, 768], P('dp', 'tensor'), may hold values from -0.21875 to 0.21875
- w_key: bfloat16 [768, 768], P('dp', 'tensor'), may hold values from -0.21875 to 0.21875
- w_value: bfloat16 [768, 768], P('dp', 'tensor'), may hold values from -0.21875 to 0.21875
- w_out: bfloat16 [768, 768], P('dp', 'tensor'), may hold values from -1.5 to 1.5
- w_in: bfloat16 [768, 3072], P('dp', 'tensor'), may hold values from -0.21875 to 0.21875
- w_back: bfloat16 [768, 3072], P('dp', 'tensor'), may hold values from -0.109375 to 0.109375
- b_query: float32 [768], replicated, may hold values from -1.75 to 1.75
- b_value: float32 [768], replicated, may hold values from -0.3125 to 0.3125
- b_out: float32 [768], replicated, may hold values from -1.75 to 1.75
- b_in: float32 [3072], replicated, may hold values from -1.75 to 1.75
- b_back: float32 [768], replicated, may hold values from -1.75 to 1.75
- gain_one: float32 [768], replicated, may hold values from 0.5 to 1.5
- shift_one: float32 [768], replicated, may hold values from -1.75 to 1.75
- gain_two: float32 [768], replicated, may hold values from 0.5 to 1.5
- shift_two: float32 [768], replicated, may hold values from -1.75 to 1.75
Outputs:
- output: bfloat16 [2, 16384, 768], P(None, ('dp', 'tensor'))
- grad_hidden: bfloat16 [2, 16384, 768], P(None, ('dp', 'tensor'))
- grad_w_query: float32 [768, 768], P('dp', 'tensor')
- grad_w_key: float32 [768, 768], P('dp', 'tensor')
- grad_w_value: float32 [768, 768], P('dp', 'tensor')
- grad_w_out: float32 [768, 768], P('dp', 'tensor')
- grad_w_in: float32 [768, 3072], P('dp', 'tensor')
- grad_w_back: float32 [768, 3072], P('dp', 'tensor')
- grad_b_query: float32 [768], replicated
- grad_b_value: float32 [768], replicated
- grad_b_out: float32 [768], replicated
- grad_b_in: float32 [3072], replicated
- grad_b_back: float32 [768], replicated
- grad_gain_one: float32 [768], replicated
- grad_shift_one: float32 [768], replicated
- grad_gain_two: float32 [768], replicated
- grad_shift_two: float32 [768], replicated
The draws below stay inside these ranges and needn't reach their ends.
Inputs may be any that keep to these rules, and one draw needn't show every extreme that they name: `lengths`: the count of real tokens of each sequence; its other slots of 1024 are padding. Some sequence has exactly 1024 and some exactly 256.
All inputs are finite; a program needn't handle non-finite values.
Results may differ from the reference program's by a relative error of at most 0.017.
Values may be sent and summed in bfloat16 or wider, within the bound.
A program may use at most 192 MiB of HBM per device.

```python
import math
import jax
import jax.numpy as jnp
from jax import lax

D = 768
H = 12
DH = 64
FF = 3072
SEQ = 1024
MICRO = 2
GROUPS = 16
TOKENS = 16384


def draw_lengths(key, part):
    key_draw = jax.random.fold_in(key, 11)
    key_long = jax.random.fold_in(key, 12)
    key_short = jax.random.fold_in(key, 13)
    total_count = MICRO * GROUPS
    drawn = jax.random.randint(key_draw, (total_count,), SEQ // 4, SEQ + 1, dtype=jnp.int32)
    long_place = jax.random.randint(key_long, (), 0, total_count, dtype=jnp.int32)
    short_step = jax.random.randint(key_short, (), 1, total_count, dtype=jnp.int32)
    short_place = (long_place + short_step) % total_count
    drawn = drawn.at[long_place].set(SEQ)
    drawn = drawn.at[short_place].set(SEQ // 4)
    return drawn.reshape(MICRO, GROUPS).astype(jnp.int32)


def raised(array, stream_key, source, target, parts, factor):
    def block_of(axis_at):
        return (jnp.arange(array.shape[axis_at]) // (array.shape[axis_at] // parts)).reshape((-1,) + (1,) * (array.ndim - 1 - axis_at))

    near = jax.random.permutation(stream_key, parts)[block_of(target)]
    far = (block_of(target) + parts // 2) % parts
    return jnp.where((block_of(source) == near) | (block_of(source) == far), factor * array, array)


def block_scale(rng, shape, split, least, top_value):
    gain = 1.0
    for dim, parts in split:
        draws = jax.random.uniform(jax.random.fold_in(jax.random.fold_in(rng, 6), dim), (parts,), jnp.float32, least / len(split), top_value / len(split))
        gain = gain * jnp.repeat(jnp.exp(draws), shape[dim] // parts).reshape((-1,) + (1,) * (len(shape) - 1 - dim))
    return gain


def noise(rng, dims, scale, bound, split=(), held_as=jnp.bfloat16):
    values = scale * jax.random.normal(rng, dims, jnp.float32)
    if split:
        values = values * block_scale(rng, dims, split, -0.22, 0.18)
    return jnp.clip(values, -bound, bound).astype(held_as)


def heavy_noise(stream_key, extent, scale, bound, split, heavy, kind=jnp.bfloat16):
    values = scale * jax.random.normal(stream_key, extent, jnp.float32)
    if split:
        values = values * block_scale(stream_key, extent, split, -0.22, 0.18)
    return jnp.clip(raised(values, jax.random.fold_in(stream_key, 3), *heavy), -bound, bound).astype(kind)


def setup_inputs(seed: int = 0) -> dict:
    arg_keys = jax.random.split(jax.random.key(seed), 19)
    hidden = heavy_noise(arg_keys[0], (MICRO, TOKENS, D), 1.0, 6.0, ((1, 32),), (1, 2, 32, 2.75))
    lengths = draw_lengths(jax.random.fold_in(arg_keys[18], 71), 0)
    cotangent = heavy_noise(arg_keys[2], (MICRO, TOKENS, D), 1.0, 6.0, ((1, 32),), (1, 2, 32, 2.75))
    w_query = noise(arg_keys[3], (D, D), D ** -0.5, 0.21875, ((0, 16), (1, 2)))
    w_key = noise(arg_keys[4], (D, D), D ** -0.5, 0.21875, ((0, 16), (1, 2)))
    w_value = noise(arg_keys[5], (D, D), D ** -0.5, 0.21875, ((0, 16), (1, 2)))
    w_out = noise(arg_keys[6], (D, D), (D // 48) ** -0.5, 1.5, ((0, 16), (1, 2)))
    w_in = noise(arg_keys[7], (D, FF), D ** -0.5, 0.21875, ((0, 16), (1, 2)))
    w_back = noise(arg_keys[8], (D, FF), FF ** -0.5, 0.109375, ((0, 16), (1, 2)))
    b_query = noise(arg_keys[9], (D,), 0.3, 1.75, (), jnp.float32)
    b_value = noise(arg_keys[10], (D,), 0.05, 0.3125, (), jnp.float32)
    b_out = noise(arg_keys[11], (D,), 0.3, 1.75, (), jnp.float32)
    b_in = noise(arg_keys[12], (FF,), 0.3, 1.75, (), jnp.float32)
    b_back = noise(arg_keys[13], (D,), 0.3, 1.75, (), jnp.float32)
    gain_one = jnp.clip(1.0 + 0.1 * jax.random.normal(arg_keys[14], (D,), jnp.float32), 0.5, 1.5)
    shift_one = noise(arg_keys[15], (D,), 0.3, 1.75, (), jnp.float32)
    gain_two = jnp.clip(1.0 + 0.1 * jax.random.normal(arg_keys[16], (D,), jnp.float32), 0.5, 1.5)
    shift_two = noise(arg_keys[17], (D,), 0.3, 1.75, (), jnp.float32)
    return dict(hidden=hidden, lengths=lengths, cotangent=cotangent, w_query=w_query, w_key=w_key, w_value=w_value, w_out=w_out, w_in=w_in, w_back=w_back, b_query=b_query, b_value=b_value, b_out=b_out, b_in=b_in, b_back=b_back, gain_one=gain_one, shift_one=shift_one, gain_two=gain_two, shift_two=shift_two)


@jax.custom_vjp
def low(v):
    return lax.optimization_barrier(v.astype(jnp.bfloat16)).astype(jnp.float32)

@jax.custom_vjp
def low_back(v):
    return v

def low_keep(v):
    return (low(v), None)

def low_pass(kept, grad):
    return (grad,)

def back_keep(v):
    return (v, None)

def back_low(kept, grad):
    return (low(grad),)
low.defvjp(low_keep, low_pass)
low_back.defvjp(back_keep, back_low)

def layer_norm(values, gain_vec, shift_vec):
    center = values - lax.optimization_barrier(jnp.mean(values, axis=-1, keepdims=True))
    spread = lax.optimization_barrier(jnp.mean(center * center, axis=-1, keepdims=True))
    return center * lax.rsqrt(spread + 1e-05) * gain_vec + shift_vec

def matmul(left_side, right_side):
    return jnp.dot(left_side, right_side, precision=lax.Precision.HIGHEST, preferred_element_type=jnp.float32)

def layer(inputs, params, length):
    w_query, w_key, w_value, w_out, w_in, w_back, b_query, b_value, b_out, b_in, b_back, gain_one, shift_one, gain_two, shift_two = params
    seq_len = inputs.shape[0]
    query_rows = low(low_back(matmul(inputs, w_query) + b_query))
    key_rows = low(low_back(matmul(inputs, w_key)))
    value_rows = low(low_back(matmul(inputs, w_value) + b_value))
    query_heads = query_rows.reshape(seq_len, H, DH)
    key_heads = key_rows.reshape(seq_len, H, DH)
    value_heads = value_rows.reshape(seq_len, H, DH)
    raw_scores = jnp.einsum('qhd,khd->hqk', query_heads, key_heads, precision=lax.Precision.HIGHEST) * (1.0 / math.sqrt(DH))
    key_live = jnp.arange(seq_len, dtype=jnp.int32) < length
    scores = low_back(jnp.where(key_live[None, None, :], raw_scores, -1000000000.0))
    row_max = lax.optimization_barrier(jnp.max(scores, axis=-1, keepdims=True))
    exponent = jnp.exp(scores - row_max)
    soft_weights = low(exponent / lax.optimization_barrier(jnp.sum(exponent, axis=-1, keepdims=True)))
    attended = jnp.einsum('hqk,khd->qhd', soft_weights, value_heads, precision=lax.Precision.HIGHEST).reshape(seq_len, D)
    attended = low(low_back(attended))
    branch_one = low_back(matmul(attended, w_out.T))
    normed_one = layer_norm(inputs + branch_one + b_out, gain_one, shift_one)
    hidden_pre = low_back(matmul(low(normed_one), w_in) + b_in)
    active = low(jax.nn.gelu(hidden_pre, approximate=False))
    branch_two = low_back(matmul(active, w_back.T))
    return layer_norm(normed_one + branch_two + b_back, gain_two, shift_two)

def reference(hidden, lengths, cotangent, w_query, w_key, w_value, w_out, w_in, w_back, b_query, b_value, b_out, b_in, b_back, gain_one, shift_one, gain_two, shift_two):
    params = tuple((argument.astype(jnp.float32) for argument in (w_query, w_key, w_value, w_out, w_in, w_back, b_query, b_value, b_out, b_in, b_back, gain_one, shift_one, gain_two, shift_two)))
    inputs_all = hidden.astype(jnp.float32).reshape(MICRO * GROUPS, SEQ, D)
    grads_all = cotangent.astype(jnp.float32).reshape(MICRO * GROUPS, SEQ, D)
    seq_lengths = lengths.reshape(MICRO * GROUPS).astype(jnp.int32)
    positions = jnp.arange(SEQ, dtype=jnp.int32)

    def one_sequence(totals, packed):
        inputs, grad_out, length = packed
        row_live = (positions < length).astype(jnp.float32)

        def forward(values_in, weights):
            return layer(values_in, weights, length)
        result, pull_back = jax.vjp(forward, inputs, params)
        grad_inputs, grad_params = pull_back(grad_out * row_live[:, None])
        totals = jax.tree.map(jnp.add, totals, grad_params)
        return (totals, (result.astype(jnp.bfloat16), grad_inputs.astype(jnp.bfloat16)))
    zeros_init = tuple((jnp.zeros_like(argument) for argument in params))
    summed_grads, (results, grad_rows) = lax.scan(one_sequence, zeros_init, (inputs_all, grads_all, seq_lengths))
    output = results.reshape(MICRO, GROUPS * SEQ, D)
    grad_hidden = grad_rows.reshape(MICRO, GROUPS * SEQ, D)
    return (output, grad_hidden, summed_grads[0], summed_grads[1], summed_grads[2], summed_grads[3], summed_grads[4], summed_grads[5], summed_grads[6], summed_grads[7], summed_grads[8], summed_grads[9], summed_grads[10], summed_grads[11], summed_grads[12], summed_grads[13], summed_grads[14])
```

```python
import functools
import math

import jax
import jax.numpy as jnp
from jax import lax
from jax.experimental import pallas as pl
from jax.experimental.pallas import tpu as pltpu
from jax.sharding import PartitionSpec as P

F32, BF16 = jnp.float32, jnp.bfloat16
DH = 64

def nt(a, b): return lax.dot_general(a, b, (((1,), (1,)), ((), ())), preferred_element_type=F32)
def nn(a, b): return lax.dot_general(a, b, (((1,), (0,)), ((), ())), preferred_element_type=F32)
def tn(a, b): return lax.dot_general(a, b, (((0,), (0,)), ((), ())), preferred_element_type=F32)

def split3(v):
    hi = v.astype(BF16).astype(F32); r = v - hi
    mid = r.astype(BF16).astype(F32)
    return hi, mid, r - mid

def fwd_kernel(bq, len_ref, q_ref, k_ref, v_ref, o_ref, lse_ref):
    rows = q_ref.shape[0]
    n = len_ref[0]
    lane = lax.broadcasted_iota(jnp.int32, (1, 128), 1)
    krow = lax.broadcasted_iota(jnp.int32, (rows, 1), 0)
    kbias = jnp.where((krow + len_ref[1]) % rows < n, 0.0, -1e9)
    k = k_ref[...].astype(F32)
    v = v_ref[...]
    kas = []
    for h in range(2):
        own = lane // DH == h
        kas.append(jnp.where(own, k, jnp.where(lane == DH * (1 - h), kbias, 0.0)).astype(BF16))
    for qb in range(0, rows, bq):
        q = q_ref[qb : qb + bq].astype(F32)
        os_, ls = [], []
        for h in range(2):
            own = lane // DH == h
            qa = jnp.where(own, q, jnp.where(lane == DH * (1 - h), 1.0, 0.0)).astype(BF16)
            s = nt(qa, kas[h])
            m = jnp.max(s, axis=1, keepdims=True)
            p = jnp.exp(s - m)
            l = jnp.sum(p, axis=1, keepdims=True)
            os_.append(nn(p.astype(BF16), v) * (1.0 / l))
            ls.append(m + jnp.log(l))
        first = lane < DH
        o_ref[qb : qb + bq] = jnp.where(first, os_[0], os_[1]).astype(BF16)
        lse_ref[qb : qb + bq] = jnp.where(first, ls[1], ls[0])

def attend_forward(length, q, k, v, bq=256):
    rows, width = q.shape
    spec = pl.BlockSpec((rows, 128), lambda i: (0, i))
    return pl.pallas_call(functools.partial(fwd_kernel, bq), grid=(width // 128,),
        in_specs=[pl.BlockSpec(memory_space=pltpu.SMEM), spec, spec, spec], out_specs=[spec, spec],
        out_shape=[jax.ShapeDtypeStruct((rows, width), BF16), jax.ShapeDtypeStruct((rows, width), F32)],
        compiler_params=pltpu.CompilerParams(vmem_limit_bytes=56 << 20), name="attend_forward")(length, q, k, v)

def bwd_kernel(bk, mode, len_ref, q_ref, k_ref, v_ref, d_ref, o_ref, lse_ref, dq_ref, dk_ref, dv_ref, qa_s, ka_s, va_s, da_s, acc):
    rows = q_ref.shape[0]
    n = len_ref[0]
    lane = lax.broadcasted_iota(jnp.int32, (1, 128), 1)
    krow = lax.broadcasted_iota(jnp.int32, (rows, 1), 0)
    kbias = jnp.where((krow + len_ref[1]) % rows < n, 0.0, -1e9)
    d = d_ref[...].astype(F32)
    prod = d * o_ref[...].astype(F32)
    nl = -lse_ref[...]
    hi, mid, lo = split3(nl)
    for h in range(2):
        own = lane // DH == h
        sp = DH * (1 - h)
        pick = lambda a, b, c, e: jnp.where(lane == sp, a, jnp.where(lane == sp + 1, b, jnp.where(lane == sp + 2, c, jnp.where(lane == sp + 3, e, 0.0))))
        dlt = -jnp.sum(jnp.where(own, prod, 0.0), axis=1, keepdims=True)
        dh, dm, dl = split3(dlt)
        qa_s[h] = jnp.where(own, q_ref[...].astype(F32), pick(hi, mid, lo, 1.0)).astype(BF16)
        ka_s[h] = jnp.where(own, k_ref[...].astype(F32), pick(1.0, 1.0, 1.0, kbias)).astype(BF16)
        da_s[h] = jnp.where(own, d, pick(dh, dm, dl, 0.0)).astype(BF16)
        va_s[h] = jnp.where(own, v_ref[...].astype(F32), pick(1.0, 1.0, 1.0, 0.0)).astype(BF16)
    first = lane < DH
    for kb in range(0, rows, bk):
        dks, dvs, dqs = [], [], []
        for h in range(2):
            sT = nt(ka_s[h, kb : kb + bk], qa_s[h])
            p = jnp.exp(sT)
            dpT = nt(va_s[h, kb : kb + bk], da_s[h])
            ds = (p * dpT).astype(BF16)
            dvs.append(nn(p.astype(BF16), d_ref[...]))
            dks.append(nn(ds, q_ref[...]))
            if mode == 0:
                dqs.append(tn(ds, k_ref[kb : kb + bk]))
            else:
                dqs.append(tn(k_ref[kb : kb + bk], ds))
        dk_ref[kb : kb + bk] = jnp.where(first, dks[0], dks[1]).astype(BF16)
        dv_ref[kb : kb + bk] = jnp.where(first, dvs[0], dvs[1]).astype(BF16)
        if mode == 0:
            dq = jnp.where(first, dqs[0], dqs[1])
            if kb == 0: acc[...] = dq
            else: acc[...] += dq
        else:
            row = lax.broadcasted_iota(jnp.int32, (128, 1), 0)
            dq = jnp.where(row < DH, dqs[0], dqs[1])
            if kb == 0: acc[...] = dq
            else: acc[...] += dq
    dqv = acc[...] if mode == 0 else acc[...].T
    dq_ref[...] = (dqv * 0.125).astype(BF16)

def attend_backward(length, q, k, v, d, o, lse, bk=256, mode=0):
    rows, width = q.shape
    spec = pl.BlockSpec((rows, 128), lambda i: (0, i))
    aug = pltpu.VMEM((2, rows, 128), BF16)
    return pl.pallas_call(functools.partial(bwd_kernel, bk, mode), grid=(width // 128,),
        in_specs=[pl.BlockSpec(memory_space=pltpu.SMEM)] + [spec] * 6, out_specs=[spec] * 3,
        out_shape=[jax.ShapeDtypeStruct((rows, width), BF16)] * 3,
        scratch_shapes=[aug, aug, aug, aug, pltpu.VMEM((rows, 128) if mode == 0 else (128, rows), F32)],
        compiler_params=pltpu.CompilerParams(vmem_limit_bytes=56 << 20), name=f"attend_backward_{mode}_{bk}")(length, q, k, v, d, o, lse)

def norm_parts(v):
    c = v - jnp.mean(v, axis=-1, keepdims=True)
    r = lax.rsqrt(jnp.mean(c * c, axis=-1, keepdims=True) + 1e-5)
    return c * r, r

def norm_back(n, r, dyg):
    return r * (dyg - jnp.mean(dyg, axis=-1, keepdims=True) - n * jnp.mean(dyg * n, axis=-1, keepdims=True))

def colsum(v): return jnp.sum(v, axis=0, keepdims=True)

def mlp_kernel(chunk, len_ref, a_ref, h_ref, c_ref, wo_ref, wi_ref, wb_ref, vec_ref, bi_ref,
               out_ref, g1_ref, ga_ref, gwo_ref, gwi_ref, gwb_ref, small_ref, gbi_ref,
               acc_o, acc_i, acc_b, act, gp, b2, gn, btT, midT):
    step = pl.program_id(0)
    rows, inner = a_ref.shape[0], wi_ref.shape[1]
    b_out, b_back, gain_one, shift_one, gain_two, shift_two = [vec_ref[i : i + 1] for i in range(6)]
    @pl.when(step == 0)
    def _():
        acc_o[...] = jnp.zeros_like(acc_o); acc_i[...] = jnp.zeros_like(acc_i); acc_b[...] = jnp.zeros_like(acc_b)
        small_ref[...] = jnp.zeros_like(small_ref); gbi_ref[...] = jnp.zeros_like(gbi_ref)
    v1 = h_ref[...].astype(F32) + nt(a_ref[...], wo_ref[...]) + b_out
    n1, r1 = norm_parts(v1)
    normed = n1 * gain_one + shift_one
    mid = normed.astype(BF16)
    midT[...] = mid.T
    b2[...] = jnp.zeros_like(b2)
    def up(i, _):
        cols = pl.ds(pl.multiple_of(i * chunk, chunk), chunk)
        hp = nn(mid, wi_ref[:, cols]) + bi_ref[:, cols]
        half = 0.5 + 0.5 * lax.erf(hp * math.sqrt(0.5))
        a = (hp * half).astype(BF16)
        act[:, cols] = a
        gp[:, cols] = (half + hp * (jnp.exp(hp * hp * -0.5) * (1.0 / math.sqrt(2 * math.pi)))).astype(BF16)
        b2[...] += nt(a, wb_ref[:, cols])
        return 0
    lax.fori_loop(0, inner // chunk, up, 0)
    n2, r2 = norm_parts(normed + b2[...] + b_back)
    out_ref[...] = (n2 * gain_two + shift_two).astype(BF16)
    place = (step * rows + lax.broadcasted_iota(jnp.int32, (rows, 1), 0) + len_ref[1]) % (rows * pl.num_programs(0))
    go = c_ref[...].astype(F32) * jnp.where(place < len_ref[0], 1.0, 0.0)
    grad_two = norm_back(n2, r2, go * gain_two)
    back = grad_two.astype(BF16)
    btT[...] = back.T
    small_ref[1:2] += colsum(grad_two)
    small_ref[4:5] += colsum(go * n2)
    small_ref[5:6] += colsum(go)
    gn[...] = grad_two
    def down(i, _):
        cols = pl.ds(pl.multiple_of(i * chunk, chunk), chunk)
        gpre = nn(back, wb_ref[:, cols]) * gp[:, cols].astype(F32)
        gb = gpre.astype(BF16)
        gbi_ref[:, cols] += colsum(gb.astype(F32))
        acc_b[:, cols] += nn(btT[...], act[:, cols])
        acc_i[:, cols] += nn(midT[...], gb)
        gn[...] += nt(gb, wi_ref[:, cols])
        return 0
    lax.fori_loop(0, inner // chunk, down, 0)
    g = gn[...]
    grad_one = norm_back(n1, r1, g * gain_one)
    bo = grad_one.astype(BF16)
    small_ref[0:1] += colsum(grad_one)
    small_ref[2:3] += colsum(g * n1)
    small_ref[3:4] += colsum(g)
    g1_ref[...] = grad_one
    acc_o[...] += tn(bo, a_ref[...])
    ga_ref[...] = nn(bo, wo_ref[...]).astype(BF16)
    @pl.when(step == pl.num_programs(0) - 1)
    def _():
        gwo_ref[...] = acc_o[...].astype(BF16)
        gwi_ref[...] = acc_i[...].astype(BF16)
        gwb_ref[...] = acc_b[...].astype(BF16)

def mlp(length, a, h, c, wo, wi, wb, vec, bi, rows=256, chunk=1024):
    total, width = a.shape
    inner = wi.shape[1]
    row = pl.BlockSpec((rows, width), lambda i: (i, 0))
    def whole(s, **kw): return pl.BlockSpec(s, lambda i: (0, 0), pipeline_mode=pl.Buffered(1))
    S = jax.ShapeDtypeStruct
    V = pltpu.VMEM
    return pl.pallas_call(functools.partial(mlp_kernel, chunk), grid=(total // rows,),
        in_specs=[pl.BlockSpec(memory_space=pltpu.SMEM), row, row, row, whole((width, width)), whole((width, inner)), whole((width, inner)), whole((8, width)), whole((1, inner))],
        out_specs=[row, row, row, whole((width, width)), whole((width, inner)), whole((width, inner)), whole((8, width)), whole((1, inner))],
        out_shape=[S((total, width), BF16), S((total, width), F32), S((total, width), BF16), S((width, width), BF16), S((width, inner), BF16), S((width, inner), BF16), S((8, width), F32), S((1, inner), F32)],
        scratch_shapes=[V((width, width), F32), V((width, inner), F32), V((width, inner), F32), V((rows, inner), BF16), V((rows, inner), BF16), V((rows, width), F32), V((rows, width), F32), V((width, rows), BF16), V((width, rows), BF16)],
        compiler_params=pltpu.CompilerParams(vmem_limit_bytes=62 << 20), name=f"mlp_{rows}_{chunk}")(length, a, h, c, wo, wi, wb, vec, bi)


def per_device(
    hidden, lengths, cotangent, w_query, w_key, w_value, w_out, w_in, w_back,
    b_query, b_value, b_out, b_in, b_back, gain_one, shift_one, gain_two, shift_two,
):
    t = lax.axis_index("tensor")
    local = hidden.shape[1]
    width = b_query.shape[0]
    swap = [(0, 1), (1, 0)]

    def mine(a):
        return lax.dynamic_index_in_dim(a, t, 0, keepdims=False)

    def other(a):
        return lax.dynamic_index_in_dim(a, 1 - t, 0, keepdims=False)

    def gather(w):
        w = lax.all_gather(w, "dp", axis=0, tiled=True)
        return lax.all_gather(w, "tensor", axis=1, tiled=True)

    length = jnp.stack([mine(lengths)[0], t * local]).astype(jnp.int32)
    rows = jnp.concatenate([mine(hidden), lax.ppermute(other(hidden), "tensor", swap)], 0)
    cot = jnp.concatenate([mine(cotangent), lax.ppermute(other(cotangent), "tensor", swap)], 0)
    full_query, full_key, full_value, full_out, full_in, full_back = [gather(w) for w in (w_query, w_key, w_value, w_out, w_in, w_back)]
    query = ((nn(rows, full_query) + b_query) * 0.125).astype(BF16)
    key = nn(rows, full_key).astype(BF16)
    value = (nn(rows, full_value) + b_value).astype(BF16)
    attended, lse = attend_forward(length, query, key, value)
    vec = jnp.stack([b_out, b_back, gain_one, shift_one, gain_two, shift_two, b_out, b_out])
    out, grad_one, grad_attended, g_out, g_in, g_back, small, g_b_in = mlp(
        length, attended, rows, cot, full_out, full_in, full_back, vec, b_in[None]
    )
    d_query, d_key, d_value = attend_backward(length, query, key, value, grad_attended, attended, lse)
    grad_rows = (grad_one + nt(d_query, full_query) + nt(d_key, full_key) + nt(d_value, full_value)).astype(BF16)
    g_query, g_key, g_value = [tn(rows, d).astype(BF16) for d in (d_query, d_key, d_value)]

    def scatter(g):
        g = lax.psum_scatter(g, "dp", scatter_dimension=0, tiled=True)
        return lax.psum_scatter(g, "tensor", scatter_dimension=1, tiled=True).astype(F32)

    owned = [scatter(g) for g in (g_query, g_key, g_value, g_out, g_in, g_back)]
    sums = lax.psum(
        (jnp.sum(d_query.astype(F32), 0), jnp.sum(d_value.astype(F32), 0), small, g_b_in[0]), ("dp", "tensor")
    )

    def give(a):
        got = lax.ppermute(a[local:], "tensor", swap)
        first = t == 0
        return jnp.stack([jnp.where(first, a[:local], got), jnp.where(first, got, a[:local])], 0)

    s = sums[2]
    return (give(out), give(grad_rows), *owned, sums[0], sums[1], s[0], sums[3], s[1], s[2], s[3], s[4], s[5])


def solution(mesh):
    rows = P(None, ("dp", "tensor"), None)
    weight = P("dp", "tensor")
    return jax.shard_map(
        per_device, mesh=mesh,
        in_specs=(rows, P(None, "dp"), rows) + (weight,) * 6 + (P(),) * 9,
        out_specs=(rows, rows) + (weight,) * 6 + (P(),) * 9,
        check_vma=False,
    )
```

```python
import functools
import math

import jax
import jax.numpy as jnp
from jax import lax
from jax.experimental import pallas as pl
from jax.experimental.pallas import tpu as pltpu
from jax.sharding import PartitionSpec as P

F32, BF16 = jnp.float32, jnp.bfloat16
DH = 64
S = jax.ShapeDtypeStruct
HBM = pl.BlockSpec(memory_space=pl.ANY)
SMALL = pl.BlockSpec(memory_space=pltpu.SMEM)
DMA = pltpu.SemaphoreType.DMA


def nt(a, b):
    return lax.dot_general(a, b, (((1,), (1,)), ((), ())), preferred_element_type=F32)


def nn(a, b):
    return lax.dot_general(a, b, (((1,), (0,)), ((), ())), preferred_element_type=F32)


def tn(a, b):
    return lax.dot_general(a, b, (((0,), (0,)), ((), ())), preferred_element_type=F32)


def split3(v):
    hi = v.astype(BF16).astype(F32)
    rest = v - hi
    mid = rest.astype(BF16).astype(F32)
    return hi, mid, rest - mid


class Place:
    def __init__(self):
        dp, t = lax.axis_index("dp"), lax.axis_index("tensor")
        z, x, c = dp // 4, (dp // 2) % 2, dp % 2
        self.z, self.x, self.c, self.t = z, x, c, t
        self.above, self.below, self.far = (z + 1) % 4, (z + 3) % 4, (z + 2) % 4
        at = lambda z, x, c, t: ((z * 2 + x) * 2 + c, t)
        self.up, self.down = at(self.above, x, c, t), at(self.below, x, c, t)
        self.across, self.beside, self.twin = at(z, 1 - x, c, t), at(z, x, c, 1 - t), at(z, x, 1 - c, t)

    def greet(self):
        barrier = pltpu.get_barrier_semaphore()
        for peer in (self.up, self.down, self.across, self.beside, self.twin):
            pl.semaphore_signal(barrier, inc=1, device_id=peer, device_id_type=pl.DeviceIdType.MESH)
        pl.semaphore_wait(barrier, 5)


def remote(src, dst, send, recv, peer):
    return pltpu.make_async_remote_copy(src, dst, send, recv, device_id=peer, device_id_type=pl.DeviceIdType.MESH)


def gather_stages(place, order, shard, full, first, count, send, recv, local):
    z, x, c, t = place.z, place.x, place.c, place.t
    lanes = pl.ds(first, count)
    part = count // 256 * 128
    low, high = pl.ds(first, part), pl.ds(first + part, count - part)
    own = full.at[t, z, x, c, :, lanes]
    here = shard.at[:, lanes]
    def move(i, view, peer, src=None):
        return remote(view if src is None else src, view, send.at[i], recv.at[i], peer)
    keep = pltpu.make_async_copy(here, own, local)
    everything = move(6, full.at[:, :, :, c, :, lanes], place.twin)
    if order[0] == "z":
        first_up, first_down = move(0, own, place.up, here), move(1, own, place.down, here)
        next_up = move(2, full.at[t, place.below, x, c, :, low], place.up)
        next_down = move(3, full.at[t, place.above, x, c, :, high], place.down)
        if order == "zxy":
            four, five = move(4, full.at[t, :, x, c, :, lanes], place.across), move(5, full.at[t, :, :, c, :, lanes], place.beside)
        else:
            four, five = move(4, full.at[t, :, x, c, :, lanes], place.beside), move(5, full.at[:, :, x, c, :, lanes], place.across)
        copies = [first_up, first_down, next_up, next_down, four, five, everything]
        def s0(): keep.start(); first_up.start(); first_down.start()
        def s1(): first_up.wait_recv(); next_up.start(); first_down.wait_recv(); next_down.start()
        def s2(): next_up.wait_recv(); next_down.wait_recv(); keep.wait(); four.start()
        def s3(): four.wait_recv(); five.start()
        def s4(): five.wait_recv(); everything.start()
    else:
        if order == "xyz":
            one, two = move(0, own, place.across, here), move(1, full.at[t, z, :, c, :, lanes], place.beside)
        else:
            one, two = move(0, own, place.beside, here), move(1, full.at[:, z, x, c, :, lanes], place.across)
        first_up, first_down = move(2, full.at[:, z, :, c, :, lanes], place.up), move(3, full.at[:, z, :, c, :, lanes], place.down)
        next_up = move(4, full.at[0, place.below, :, c, :, lanes], place.up)
        next_down = move(5, full.at[1, place.above, :, c, :, lanes], place.down)
        copies = [one, two, first_up, first_down, next_up, next_down, everything]
        def s0(): keep.start(); one.start()
        def s1(): one.wait_recv(); keep.wait(); two.start()
        def s2(): two.wait_recv(); first_up.start(); first_down.start()
        def s3(): first_up.wait_recv(); next_up.start(); first_down.wait_recv(); next_down.start()
        def s4(): next_up.wait_recv(); next_down.wait_recv(); everything.start()
    def s5():
        everything.wait_recv()
        for copy in copies: copy.wait_send()
    return [s0, s1, s2, s3, s4, s5]


def add_blocks(count, dst, *srcs):
    def body(i, _):
        ref = dst(i)
        total = ref[...].astype(F32)
        for s in srcs: total = total + s(i)[...].astype(F32)
        ref[...] = total.astype(ref.dtype)
        return 0
    lax.fori_loop(0, count, body, 0)


def reduce_scratch(order, rows, lanes):
    V = lambda *s: pltpu.VMEM(s + (rows, lanes), BF16)
    base = [V(2, 4, 2), V(2, 4, 2)]
    if order == "yxz": base += [V(4, 2), V(4), V(), V(2)]
    elif order == "xyz": base += [V(2, 4), V(4), V(), V(2)]
    else: base += [V(2, 2), V(2, 2, 2), V(2), V()]
    return base + [pltpu.SemaphoreType.DMA((7,)), pltpu.SemaphoreType.DMA((7,)), pltpu.SemaphoreType.DMA]


def reduce_stages(place, order, grad, first, count, out, scratch):
    held, r0, r1, r2, r3, r4, send, recv, local = scratch
    z, x, c, t = place.z, place.x, place.c, place.t
    lanes = pl.ds(first, count)
    part = count // 256 * 128
    low, high = pl.ds(0, part), pl.ds(part, count - part)
    load = pltpu.make_async_copy(grad.at[:, :, :, c, :, lanes], held, local)
    def move(i, src, dst, peer):
        return remote(src, dst, send.at[i], recv.at[i], peer)
    c0 = move(0, grad.at[:, :, :, 1 - c, :, lanes], r0, place.twin)
    at3 = lambda ref: (lambda i: ref.at[i // 8, (i // 2) % 4, i % 2])
    def s0(): load.start(); c0.start()
    if order[0] != "z":
        if order == "yxz":
            c1, c2 = move(1, held.at[1 - t], r1, place.beside), move(2, held.at[t, :, 1 - x], r2, place.across)
            def add1(): add_blocks(8, lambda i: held.at[t, i // 2, i % 2], lambda i: r1.at[i // 2, i % 2])
        else:
            c1, c2 = move(1, held.at[:, :, 1 - x], r1, place.across), move(2, held.at[1 - t, :, x], r2, place.beside)
            def add1(): add_blocks(8, lambda i: held.at[i // 4, i % 4, x], lambda i: r1.at[i // 4, i % 4])
        mine = lambda k: held.at[t, k, x]
        c3 = move(3, held.at[t, place.far, x, :, low], r3.at[:, low], place.up)
        c4 = move(4, held.at[t, place.far, x, :, high], r3.at[:, high], place.down)
        c5, c6 = move(5, mine(place.above), r4.at[0], place.up), move(6, mine(place.below), r4.at[1], place.down)
        def s1(): load.wait(); c0.wait_recv(); add_blocks(16, at3(held), at3(r0)); c1.start()
        def s2(): c1.wait_recv(); add1(); c2.start()
        def s3(): c2.wait_recv(); add_blocks(4, mine, lambda k: r2.at[k]); c3.start(); c4.start()
        def s4():
            c3.wait_recv()
            v = held.at[t, place.above, x, :, low]; v[...] = (v[...].astype(F32) + r3[:, low].astype(F32)).astype(BF16)
            c5.start()
            c4.wait_recv()
            v = held.at[t, place.below, x, :, high]; v[...] = (v[...].astype(F32) + r3[:, high].astype(F32)).astype(BF16)
            c6.start()
        def s5():
            c5.wait_recv(); c6.wait_recv()
            out[:, lanes] = mine(z)[...].astype(F32) + r4[0].astype(F32) + r4[1].astype(F32)
            for copy in (c0, c1, c2, c3, c4, c5, c6): copy.wait_send()
    else:
        c1, c2 = move(1, held.at[0, place.far], r1.at[0], place.up), move(2, held.at[1, place.far], r1.at[1], place.down)
        c3, c4 = move(3, held.at[:, place.above], r2.at[0], place.up), move(4, held.at[:, place.below], r2.at[1], place.down)
        if order == "zyx":
            c5, c6 = move(5, held.at[1 - t, z], r3, place.beside), move(6, held.at[t, z, 1 - x], r4, place.across)
            def add5(): add_blocks(2, lambda k: held.at[t, z, k], lambda k: r3.at[k])
        else:
            c5, c6 = move(5, held.at[:, z, 1 - x], r3, place.across), move(6, held.at[1 - t, z, x], r4, place.beside)
            def add5(): add_blocks(2, lambda k: held.at[k, z, x], lambda k: r3.at[k])
        def s1(): load.wait(); c0.wait_recv(); add_blocks(16, at3(held), at3(r0)); c1.start(); c2.start()
        def s2():
            c1.wait_recv(); add_blocks(2, lambda k: held.at[0, place.above, k], lambda k: r1.at[0, k]); c3.start()
            c2.wait_recv(); add_blocks(2, lambda k: held.at[1, place.below, k], lambda k: r1.at[1, k]); c4.start()
        def s3():
            c3.wait_recv(); c4.wait_recv()
            add_blocks(4, lambda k: held.at[k // 2, z, k % 2], lambda k: r2.at[0, k // 2, k % 2], lambda k: r2.at[1, k // 2, k % 2])
            c5.start()
        def s4(): c5.wait_recv(); add5(); c6.start()
        def s5():
            c6.wait_recv()
            out[:, lanes] = held[t, z, x].astype(F32) + r4[...].astype(F32)
            for copy in (c0, c1, c2, c3, c4, c5, c6): copy.wait_send()
    return [s0, s1, s2, s3, s4, s5]


def fold_stages(place, part, got, send, recv):
    flip = place.z % 2
    near = jax.tree.map(lambda u, d: u + flip * (d - u), place.up, place.down)
    next_ = jax.tree.map(lambda u, d: d + flip * (u - d), place.up, place.down)
    peers = (place.twin, place.across, place.beside, near, next_)
    copies = [remote(part, got.at[i], send.at[i], recv.at[i], peer) for i, peer in enumerate(peers)]
    def stage(i):
        def run():
            if i > 0:
                copies[i - 1].wait()
                part[...] = part[...] + got[i - 1]
            if i < 5:
                copies[i].start()
        return run
    return [stage(i) for i in range(6)]


def gather_sems(count):
    return [s for _ in range(count) for s in (DMA((7,)), DMA((7,)), DMA)]


def gather_plans(place, items, shards, fulls, sems):
    return [
        gather_stages(place, order, shards[w], fulls[w], first, count, *sems[3 * i : 3 * i + 3])
        for i, (w, first, count, order) in enumerate(items)
    ]


def reduce_plans(place, items, grads, outs, scratch):
    return [
        reduce_stages(place, order, grads[w], first, count, outs[w], scratch[9 * i : 9 * i + 9])
        for i, (w, first, count, order) in enumerate(items)
    ]


def swap_in(place, pair, rows, sems):
    local = pair.shape[1]
    keep = pltpu.make_async_copy(pair.at[place.t], rows.at[pl.ds(0, local)], sems.at[0])
    give = remote(pair.at[1 - place.t], rows.at[pl.ds(local, local)], sems.at[1], sems.at[2], place.beside)
    return keep, give


def swap_out(place, rows, pair, sems):
    local = pair.shape[1]
    keep = pltpu.make_async_copy(rows.at[pl.ds(0, local)], pair.at[place.t], sems.at[0])
    give = remote(rows.at[pl.ds(local, local)], pair.at[place.t], sems.at[1], sems.at[2], place.beside)
    return keep, give


ENTER_ITEMS = ((0, 0, 1, "xyz"), (1, 0, 1, "zxy"), (2, 0, 1, "zyx"))
REST_ITEMS = ((0, 0, 1, "zxy"), (1, 0, 2, "xyz"), (1, 1, 2, "zxy"), (2, 0, 2, "yxz"), (2, 1, 2, "zyx"))


def items_for(table, widths):
    return [(w, widths[w] // parts * i, widths[w] // parts, order) for w, i, parts, order in table]


def enter(hidden, shards):
    items = items_for(ENTER_ITEMS, [s.shape[1] for s in shards])
    n = len(shards)

    def kernel(*refs):
        pair, given, rows, fulls = refs[0], refs[1 : 1 + n], refs[1 + n], refs[2 + n : 2 + 2 * n]
        sems, swap = refs[2 + 2 * n : -1], refs[-1]
        place = Place()
        place.greet()
        keep, give = swap_in(place, pair, rows, swap)
        plans = gather_plans(place, items, given, fulls, sems)
        keep.start()
        give.start()
        for s in range(6):
            for plan in plans:
                plan[s]()
        keep.wait()
        give.wait()

    return pl.pallas_call(
        kernel,
        in_specs=[HBM] * (1 + n),
        out_specs=[HBM] * (1 + n),
        out_shape=[S((2 * hidden.shape[1], hidden.shape[2]), BF16)] + [S((2, 4, 2, 2) + s.shape, BF16) for s in shards],
        scratch_shapes=gather_sems(len(items)) + [DMA((3,))],
        compiler_params=pltpu.CompilerParams(collective_id=1, has_side_effects=True),
        name="enter",
    )(hidden, *shards)


def forward_pair(bq, len_ref, q_ref, k_ref, v_ref, o_ref, lse_ref):
    rows = q_ref.shape[0]
    n = len_ref[0]
    lane = lax.broadcasted_iota(jnp.int32, (1, 128), 1)
    krow = lax.broadcasted_iota(jnp.int32, (rows, 1), 0)
    kbias = jnp.where((krow + len_ref[1]) % rows < n, 0.0, -1e9)
    k = k_ref[...].astype(F32)
    v = v_ref[...]
    kas = []
    for h in range(2):
        own = lane // DH == h
        kas.append(jnp.where(own, k, jnp.where(lane == DH * (1 - h), kbias, 0.0)).astype(BF16))
    first = lane < DH

    def block(i, _):
        place = pl.ds(pl.multiple_of(i * bq, bq), bq)
        q = q_ref[place].astype(F32)
        os_, ls = [], []
        for h in range(2):
            own = lane // DH == h
            qa = jnp.where(own, q, jnp.where(lane == DH * (1 - h), 1.0, 0.0)).astype(BF16)
            s = nt(qa, kas[h])
            m = jnp.max(s, axis=1, keepdims=True)
            p = jnp.exp(s - m)
            l = jnp.sum(p, axis=1, keepdims=True)
            os_.append(nn(p.astype(BF16), v) * (1.0 / l))
            ls.append(m + jnp.log(l))
        o_ref[place] = jnp.where(first, os_[0], os_[1]).astype(BF16)
        lse_ref[place] = jnp.where(first, ls[1], ls[0])
        return 0

    for i in range(rows // bq):
        block(i, 0)


def attend_forward(length, q, k, v, comm=None, bq=256):
    rows, width = q.shape
    spec = pl.BlockSpec((rows, 128), lambda i: (0, i))
    out_shape = [S((rows, width), BF16), S((rows, width), F32)]
    cost = pl.CostEstimate(flops=4 * rows * rows * width, bytes_accessed=12 * rows * width, transcendentals=rows * rows * width // DH)
    if comm is None:
        return pl.pallas_call(
            functools.partial(forward_pair, bq),
            grid=(width // 128,),
            in_specs=[SMALL, spec, spec, spec],
            out_specs=[spec, spec],
            out_shape=out_shape,
            cost_estimate=cost,
            compiler_params=pltpu.CompilerParams(vmem_limit_bytes=56 << 20),
            name="attend_forward",
        )(length, q, k, v)
    pair, shards = comm
    n = len(shards)
    items = items_for(REST_ITEMS, [s.shape[1] for s in shards])

    def kernel(*refs):
        len_ref, q_ref, k_ref, v_ref, pair_ref = refs[:5]
        given, (o_ref, lse_ref, rows_ref), fulls = refs[5 : 5 + n], refs[5 + n : 8 + n], refs[8 + n : 8 + 2 * n]
        sems, swap = refs[8 + 2 * n : -1], refs[-1]
        step = pl.program_id(0)
        place = Place()
        keep, give = swap_in(place, pair_ref, rows_ref, swap)
        plans = gather_plans(place, items, given, fulls, sems)
        for s in range(5):
            @pl.when(step == s)
            def _():
                if s == 0:
                    place.greet()
                    keep.start()
                for plan in plans:
                    plan[s]()
                if s == 1:
                    give.start()
        forward_pair(bq, len_ref, q_ref, k_ref, v_ref, o_ref, lse_ref)
        @pl.when(step == pl.num_programs(0) - 1)
        def _():
            for plan in plans:
                plan[5]()
            keep.wait()
            give.wait()

    return pl.pallas_call(
        kernel,
        grid=(width // 128,),
        in_specs=[SMALL, spec, spec, spec] + [HBM] * (1 + n),
        out_specs=[spec, spec] + [HBM] * (1 + n),
        out_shape=out_shape + [S((rows, width), BF16)] + [S((2, 4, 2, 2) + s.shape, BF16) for s in shards],
        scratch_shapes=gather_sems(len(items)) + [DMA((3,))],
        cost_estimate=cost,
        compiler_params=pltpu.CompilerParams(collective_id=2, has_side_effects=True, vmem_limit_bytes=56 << 20),
        name="attend_forward",
    )(length, q, k, v, pair, *shards)


def backward_pair(bk, len_ref, q_ref, k_ref, v_ref, d_ref, o_ref, lse_ref, dq_ref, dk_ref, dv_ref, qa_s, ka_s, va_s, da_s, acc):
    rows = q_ref.shape[0]
    n = len_ref[0]
    lane = lax.broadcasted_iota(jnp.int32, (1, 128), 1)
    krow = lax.broadcasted_iota(jnp.int32, (rows, 1), 0)
    kbias = jnp.where((krow + len_ref[1]) % rows < n, 0.0, -1e9)
    d = d_ref[...].astype(F32)
    prod = d * o_ref[...].astype(F32)
    hi, mid, lo = split3(-lse_ref[...])
    for h in range(2):
        own = lane // DH == h
        sp = DH * (1 - h)
        def pick(a, b, c, e):
            return jnp.where(lane == sp, a, jnp.where(lane == sp + 1, b, jnp.where(lane == sp + 2, c, jnp.where(lane == sp + 3, e, 0.0))))
        dh, dm, dl = split3(-jnp.sum(jnp.where(own, prod, 0.0), axis=1, keepdims=True))
        qa_s[h] = jnp.where(own, q_ref[...].astype(F32), pick(hi, mid, lo, 1.0)).astype(BF16)
        ka_s[h] = jnp.where(own, k_ref[...].astype(F32), pick(1.0, 1.0, 1.0, kbias)).astype(BF16)
        da_s[h] = jnp.where(own, d, pick(dh, dm, dl, 0.0)).astype(BF16)
        va_s[h] = jnp.where(own, v_ref[...].astype(F32), pick(1.0, 1.0, 1.0, 0.0)).astype(BF16)
    first = lane < DH
    upper = lax.broadcasted_iota(jnp.int32, (128, 1), 0) < DH
    for kb in range(0, rows, bk):
        dks, dvs, dqs = [], [], []
        for h in range(2):
            p = jnp.exp(nt(ka_s[h, kb : kb + bk], qa_s[h]))
            ds = (p * nt(va_s[h, kb : kb + bk], da_s[h])).astype(BF16)
            dvs.append(nn(p.astype(BF16), d_ref[...]))
            dks.append(nn(ds, q_ref[...]))
            dqs.append(tn(k_ref[kb : kb + bk], ds))
        dk_ref[kb : kb + bk] = jnp.where(first, dks[0], dks[1]).astype(BF16)
        dv_ref[kb : kb + bk] = jnp.where(first, dvs[0], dvs[1]).astype(BF16)
        dq = jnp.where(upper, dqs[0], dqs[1])
        if kb == 0:
            acc[...] = dq
        else:
            acc[...] += dq
    dq_ref[...] = (acc[...].T * 0.125).astype(BF16)


def attend_backward(length, q, k, v, d, o, lse, comm=None, bk=256):
    rows, width = q.shape
    spec = pl.BlockSpec((rows, 128), lambda i: (0, i))
    aug = pltpu.VMEM((2, rows, 128), BF16)
    base = [aug, aug, aug, aug, pltpu.VMEM((128, rows), F32)]
    out_shape = [S((rows, width), BF16)] * 3
    cost = pl.CostEstimate(flops=10 * rows * rows * width, bytes_accessed=20 * rows * width, transcendentals=rows * rows * width // DH)
    if comm is None:
        return pl.pallas_call(
            functools.partial(backward_pair, bk),
            grid=(width // 128,),
            in_specs=[SMALL] + [spec] * 6,
            out_specs=[spec] * 3,
            out_shape=out_shape,
            scratch_shapes=base,
            cost_estimate=cost,
            compiler_params=pltpu.CompilerParams(vmem_limit_bytes=56 << 20),
            name="attend_backward",
        )(length, q, k, v, d, o, lse)
    out_rows, grads = comm
    n = len(grads)
    shards = [g.shape[4:] for g in grads]
    items = items_for(REST_ITEMS, [s[1] for s in shards])

    def kernel(*refs):
        main_in, (rows_ref,), given = refs[:7], refs[7:8], refs[8 : 8 + n]
        rest = refs[8 + n :]
        main_out, (pair_ref,), outs = rest[:3], rest[3:4], rest[4 : 4 + n]
        main_scratch, scratch, swap = rest[4 + n : 9 + n], rest[9 + n : -1], rest[-1]
        step = pl.program_id(0)
        place = Place()
        keep, give = swap_out(place, rows_ref, pair_ref, swap)
        plans = reduce_plans(place, items, given, outs, scratch)
        for s in range(5):
            @pl.when(step == s)
            def _():
                if s == 0:
                    place.greet()
                    keep.start()
                for plan in plans:
                    plan[s]()
                if s == 2:
                    give.start()
        backward_pair(bk, *main_in, *main_out, *main_scratch)
        @pl.when(step == pl.num_programs(0) - 1)
        def _():
            for plan in plans:
                plan[5]()
            keep.wait()
            give.wait()

    vm = [pl.BlockSpec(s, lambda i: (0, 0), pipeline_mode=pl.Buffered(1)) for s in shards]
    return pl.pallas_call(
        kernel,
        grid=(width // 128,),
        in_specs=[SMALL] + [spec] * 6 + [HBM] * (1 + n),
        out_specs=[spec] * 3 + [HBM] + vm,
        out_shape=out_shape + [S((2, rows // 2, width), BF16)] + [S(s, F32) for s in shards],
        scratch_shapes=base + [s for w, f, c, o in items for s in reduce_scratch(o, shards[w][0], c)] + [DMA((3,))],
        cost_estimate=cost,
        compiler_params=pltpu.CompilerParams(collective_id=3, has_side_effects=True, vmem_limit_bytes=60 << 20),
        name="attend_backward",
    )(length, q, k, v, d, o, lse, out_rows, *grads)


def norm_parts(v):
    c = v - jnp.mean(v, axis=-1, keepdims=True)
    r = lax.rsqrt(jnp.mean(c * c, axis=-1, keepdims=True) + 1e-5)
    return c * r, r


def norm_back(n, r, dyg):
    return r * (dyg - jnp.mean(dyg, axis=-1, keepdims=True) - n * jnp.mean(dyg * n, axis=-1, keepdims=True))


def colsum(v):
    return jnp.sum(v, axis=0, keepdims=True)


def mlp_kernel(chunk, len_ref, a_ref, h_ref, c_ref, wo_ref, wi_ref, wb_ref, vec_ref, bi_ref,
               out_ref, g1_ref, ga_ref, gwo_ref, gwi_ref, gwb_ref, small_ref, gbi_ref,
               acc_o, acc_i, acc_b, act, gp, b2, gn, btT, midT):
    step = pl.program_id(0)
    rows = a_ref.shape[0]
    half, inner = wo_ref.shape[2], wi_ref.shape[2]
    b_out, b_back, gain_one, shift_one, gain_two, shift_two = [vec_ref[i : i + 1] for i in range(6)]

    @pl.when(step == 0)
    def _():
        for ref in (acc_o, acc_i, acc_b, small_ref, gbi_ref):
            ref[...] = jnp.zeros_like(ref)

    v1 = h_ref[...].astype(F32) + (nt(a_ref[:, :half], wo_ref[0]) + nt(a_ref[:, half:], wo_ref[1])) + b_out
    n1, r1 = norm_parts(v1)
    normed = n1 * gain_one + shift_one
    mid = normed.astype(BF16)
    midT[...] = mid.T
    b2[...] = jnp.zeros_like(b2)

    def up(i, _):
        t = i // (inner // chunk)
        cols = pl.ds(pl.multiple_of(i % (inner // chunk) * chunk, chunk), chunk)
        hp = nn(mid, wi_ref[t, :, cols]) + bi_ref[t, :, cols]
        half_up = 0.5 + 0.5 * lax.erf(hp * math.sqrt(0.5))
        a = (hp * half_up).astype(BF16)
        act[t, :, cols] = a
        gp[t, :, cols] = (half_up + hp * (jnp.exp(hp * hp * -0.5) * (1.0 / math.sqrt(2 * math.pi)))).astype(BF16)
        b2[...] += nt(a, wb_ref[t, :, cols])
        return 0

    lax.fori_loop(0, 2 * inner // chunk, up, 0)
    n2, r2 = norm_parts(normed + b2[...] + b_back)
    out_ref[...] = (n2 * gain_two + shift_two).astype(BF16)
    place = (step * rows + lax.broadcasted_iota(jnp.int32, (rows, 1), 0) + len_ref[1]) % (rows * pl.num_programs(0))
    go = c_ref[...].astype(F32) * jnp.where(place < len_ref[0], 1.0, 0.0)
    grad_two = norm_back(n2, r2, go * gain_two)
    back = grad_two.astype(BF16)
    btT[...] = back.T
    small_ref[1:2] += colsum(grad_two)
    small_ref[4:5] += colsum(go * n2)
    small_ref[5:6] += colsum(go)
    gn[...] = grad_two

    def down(i, _):
        t = i // (inner // chunk)
        cols = pl.ds(pl.multiple_of(i % (inner // chunk) * chunk, chunk), chunk)
        gb = (nn(back, wb_ref[t, :, cols]) * gp[t, :, cols].astype(F32)).astype(BF16)
        gbi_ref[t, :, cols] += colsum(gb.astype(F32))
        acc_b[t, :, cols] += nn(btT[...], act[t, :, cols])
        acc_i[t, :, cols] += nn(midT[...], gb)
        gn[...] += nt(gb, wi_ref[t, :, cols])
        return 0

    lax.fori_loop(0, 2 * inner // chunk, down, 0)
    g = gn[...]
    grad_one = norm_back(n1, r1, g * gain_one)
    bo = grad_one.astype(BF16)
    small_ref[0:1] += colsum(grad_one)
    small_ref[2:3] += colsum(g * n1)
    small_ref[3:4] += colsum(g)
    g1_ref[...] = grad_one
    for t in range(2):
        cols = slice(t * half, (t + 1) * half)
        acc_o[t] += tn(bo, a_ref[:, cols])
        ga_ref[:, cols] = nn(bo, wo_ref[t]).astype(BF16)

    @pl.when(step == pl.num_programs(0) - 1)
    def _():
        gwo_ref[...] = acc_o[...].astype(BF16)
        gwi_ref[...] = acc_i[...].astype(BF16)
        gwb_ref[...] = acc_b[...].astype(BF16)


def mlp(length, a, h, c, wo, wi, wb, vec, bi, rows=256, chunk=768):
    total, width = a.shape
    row = pl.BlockSpec((rows, width), lambda i: (i, 0))
    def whole(s):
        return pl.BlockSpec(s, lambda i: (0,) * len(s), pipeline_mode=pl.Buffered(1))
    V = pltpu.VMEM
    inner = wi.shape[2]
    return pl.pallas_call(
        functools.partial(mlp_kernel, chunk),
        grid=(total // rows,),
        in_specs=[SMALL, row, row, row] + [whole(s.shape) for s in (wo, wi, wb, vec, bi)],
        out_specs=[row, row, row] + [whole(s.shape) for s in (wo, wi, wb, vec, bi)],
        out_shape=[S((total, width), BF16), S((total, width), F32), S((total, width), BF16)]
        + [S(s.shape, BF16) for s in (wo, wi, wb)] + [S(vec.shape, F32), S(bi.shape, F32)],
        scratch_shapes=[V(s.shape, F32) for s in (wo, wi, wb)]
        + [V((2, rows, inner), BF16), V((2, rows, inner), BF16), V((rows, width), F32), V((rows, width), F32), V((width, rows), BF16), V((width, rows), BF16)],
        cost_estimate=pl.CostEstimate(flops=total * width * (24 * inner + 6 * width), bytes_accessed=60 << 20, transcendentals=4 * total * inner),
        compiler_params=pltpu.CompilerParams(vmem_limit_bytes=62 << 20),
        name="mlp",
    )(length, a, h, c, wo, wi, wb, vec, bi)


def leave(grad_rows, small, grads):
    n = len(grads)
    shards = [g.shape[4:] for g in grads]
    items = items_for(ENTER_ITEMS, [s[1] for s in shards])
    rows, width = grad_rows.shape

    def kernel(*refs):
        rows_ref, small_ref, given = refs[0], refs[1], refs[2 : 2 + n]
        rest = refs[2 + n :]
        pair_ref, sum_ref, outs = rest[0], rest[1], rest[2 : 2 + n]
        part, got, fold_send, fold_recv, swap, scratch = rest[2 + n], rest[3 + n], rest[4 + n], rest[5 + n], rest[6 + n], rest[7 + n :]
        place = Place()
        part[...] = small_ref[...]
        place.greet()
        keep, give = swap_out(place, rows_ref, pair_ref, swap)
        plans = reduce_plans(place, items, given, outs, scratch) + [fold_stages(place, part, got, fold_send, fold_recv)]
        keep.start()
        for s in range(6):
            for plan in plans:
                plan[s]()
            if s == 0:
                give.start()
        sum_ref[...] = part[...]
        keep.wait()
        give.wait()

    vmem = pl.BlockSpec(memory_space=pltpu.VMEM)
    return pl.pallas_call(
        kernel,
        in_specs=[HBM, vmem] + [HBM] * n,
        out_specs=[HBM, vmem] + [vmem] * n,
        out_shape=[S((2, rows // 2, width), BF16), S(small.shape, F32)] + [S(s, F32) for s in shards],
        scratch_shapes=[pltpu.VMEM(small.shape, F32), pltpu.VMEM((5,) + small.shape, F32), DMA((5,)), DMA((5,)), DMA((3,))]
        + [s for w, f, c, o in items for s in reduce_scratch(o, shards[w][0], c)],
        compiler_params=pltpu.CompilerParams(collective_id=4, has_side_effects=True, vmem_limit_bytes=56 << 20),
        name="leave",
    )(grad_rows, small, *grads)


def per_device(
    hidden, lengths, cotangent, w_query, w_key, w_value, w_out, w_in, w_back,
    b_query, b_value, b_out, b_in, b_back, gain_one, shift_one, gain_two, shift_two,
):
    t = lax.axis_index("tensor")
    local = hidden.shape[1]
    width = b_query.shape[0]
    inner = b_in.shape[0]
    own_kernels = lax.axis_size("dp") == 16 and lax.axis_size("tensor") == 2
    swap = [(0, 1), (1, 0)]

    def mine(a):
        return lax.dynamic_index_in_dim(a, t, 0, keepdims=False)

    def take(a):
        other = lax.dynamic_index_in_dim(a, 1 - t, 0, keepdims=False)
        return jnp.concatenate([mine(a), lax.ppermute(other, "tensor", swap)], 0)

    def give(a):
        got = lax.ppermute(a[local:], "tensor", swap)
        first = t == 0
        return jnp.stack([jnp.where(first, a[:local], got), jnp.where(first, got, a[:local])], 0)

    def gather(w):
        return lax.all_gather(lax.all_gather(w, "dp", axis=0, tiled=True), "tensor", axis=0)

    def scatter(g):
        g = lax.psum_scatter(g, "dp", scatter_dimension=1, tiled=True)
        return lax.psum_scatter(g, "tensor", scatter_dimension=0, tiled=False).astype(F32)

    def flat(w):
        return w.reshape(2, width, -1)

    length = jnp.stack([mine(lengths)[0], t * local]).astype(jnp.int32)
    if own_kernels:
        rows, *near = enter(hidden, (w_query, w_key, w_value))
        full_query, full_key, full_value = [flat(w) for w in near]
    else:
        rows = take(hidden)
        full_query, full_key, full_value = [gather(w) for w in (w_query, w_key, w_value)]

    def project(w):
        return jnp.concatenate([nn(rows, w[0]), nn(rows, w[1])], 1)

    query = ((project(full_query) + b_query) * 0.125).astype(BF16)
    key = project(full_key).astype(BF16)
    value = (project(full_value) + b_value).astype(BF16)
    if own_kernels:
        attended, lse, cot, *rest = attend_forward(length, query, key, value, (cotangent, (w_out, w_in, w_back)))
        full_out, full_in, full_back = [flat(w) for w in rest]
    else:
        attended, lse = attend_forward(length, query, key, value)
        cot = take(cotangent)
        full_out, full_in, full_back = [gather(w) for w in (w_out, w_in, w_back)]
    vec = jnp.stack([b_out, b_back, gain_one, shift_one, gain_two, shift_two, b_out, b_out])
    out, grad_one, grad_attended, g_out, g_in, g_back, small, g_b_in = mlp(
        length, attended, rows, cot, full_out, full_in, full_back, vec, b_in.reshape(2, 1, inner // 2)
    )
    def split(g):
        return g.reshape(2, 4, 2, 2, -1, g.shape[-1])
    if own_kernels:
        d_query, d_key, d_value, output, *owned_rest = attend_backward(
            length, query, key, value, grad_attended, attended, lse, (out, [split(g) for g in (g_out, g_in, g_back)])
        )
    else:
        d_query, d_key, d_value = attend_backward(length, query, key, value, grad_attended, attended, lse)
        output = give(out)
        owned_rest = [scatter(g) for g in (g_out, g_in, g_back)]
    total = grad_one
    grads = []
    for d, w in ((d_query, full_query), (d_key, full_key), (d_value, full_value)):
        total = total + nt(d, jnp.concatenate([w[0], w[1]], 1))
        g = tn(rows, d).astype(BF16)
        grads.append(jnp.stack([g[:, : width // 2], g[:, width // 2 :]]))
    grad_rows = total.astype(BF16)
    small = jnp.concatenate([
        small, g_b_in.reshape(-1, width),
        jnp.sum(d_query.astype(F32), 0)[None], jnp.sum(d_value.astype(F32), 0)[None],
        jnp.zeros((2, width), F32),
    ])
    if own_kernels:
        grad_hidden, small, *owned = leave(grad_rows, small, [split(g) for g in grads])
    else:
        grad_hidden = give(grad_rows)
        owned = [scatter(g) for g in grads]
        small = lax.psum(small, ("dp", "tensor"))
    vb = 8 + inner // width
    return (
        output, grad_hidden, *owned, *owned_rest,
        small[vb], small[vb + 1], small[0], small[8:vb].reshape(inner), small[1], small[2], small[3], small[4], small[5],
    )


def solution(mesh):
    rows = P(None, ("dp", "tensor"), None)
    weight = P("dp", "tensor")
    return jax.shard_map(
        per_device,
        mesh=mesh,
        in_specs=(rows, P(None, "dp"), rows) + (weight,) * 6 + (P(),) * 9,
        out_specs=(rows, rows) + (weight,) * 6 + (P(),) * 9,
        check_vma=False,
    )
```

```python
import functools
import math

import jax
import jax.numpy as jnp
from jax import lax
from jax.experimental import pallas as pl
from jax.experimental.pallas import tpu as pltpu
from jax.sharding import PartitionSpec as P

F32, BF16 = jnp.float32, jnp.bfloat16
DH = 64
S = jax.ShapeDtypeStruct
HBM = pl.BlockSpec(memory_space=pl.ANY)
SMALL = pl.BlockSpec(memory_space=pltpu.SMEM)
DMA = pltpu.SemaphoreType.DMA


def nt(a, b):
    return lax.dot_general(a, b, (((1,), (1,)), ((), ())), preferred_element_type=F32)


def nn(a, b):
    return lax.dot_general(a, b, (((1,), (0,)), ((), ())), preferred_element_type=F32)


def tn(a, b):
    return lax.dot_general(a, b, (((0,), (0,)), ((), ())), preferred_element_type=F32)


def split3(v):
    hi = v.astype(BF16).astype(F32)
    rest = v - hi
    mid = rest.astype(BF16).astype(F32)
    return hi, mid, rest - mid


class Place:
    def __init__(self):
        dp, t = lax.axis_index("dp"), lax.axis_index("tensor")
        z, x, c = dp // 4, (dp // 2) % 2, dp % 2
        self.z, self.x, self.c, self.t = z, x, c, t
        self.above, self.below, self.far = (z + 1) % 4, (z + 3) % 4, (z + 2) % 4
        at = lambda z, x, c, t: ((z * 2 + x) * 2 + c, t)
        self.up, self.down = at(self.above, x, c, t), at(self.below, x, c, t)
        self.across, self.beside, self.twin = at(z, 1 - x, c, t), at(z, x, c, 1 - t), at(z, x, 1 - c, t)

    def greet(self):
        barrier = pltpu.get_barrier_semaphore()
        for peer in (self.up, self.down, self.across, self.beside, self.twin):
            pl.semaphore_signal(barrier, inc=1, device_id=peer, device_id_type=pl.DeviceIdType.MESH)
        pl.semaphore_wait(barrier, 5)


def remote(src, dst, send, recv, peer):
    return pltpu.make_async_remote_copy(src, dst, send, recv, device_id=peer, device_id_type=pl.DeviceIdType.MESH)


def gather_stages(place, order, shard, full, first, count, send, recv, local):
    z, x, c, t = place.z, place.x, place.c, place.t
    lanes = pl.ds(first, count)
    part = count // 256 * 128
    low, high = pl.ds(first, part), pl.ds(first + part, count - part)
    own = full.at[t, z, x, c, :, lanes]
    here = shard.at[:, lanes]
    def move(i, view, peer, src=None):
        return remote(view if src is None else src, view, send.at[i], recv.at[i], peer)
    keep = pltpu.make_async_copy(here, own, local)
    everything = move(6, full.at[:, :, :, c, :, lanes], place.twin)
    if order[0] == "z":
        first_up, first_down = move(0, own, place.up, here), move(1, own, place.down, here)
        next_up = move(2, full.at[t, place.below, x, c, :, low], place.up)
        next_down = move(3, full.at[t, place.above, x, c, :, high], place.down)
        if order == "zxy":
            four, five = move(4, full.at[t, :, x, c, :, lanes], place.across), move(5, full.at[t, :, :, c, :, lanes], place.beside)
        else:
            four, five = move(4, full.at[t, :, x, c, :, lanes], place.beside), move(5, full.at[:, :, x, c, :, lanes], place.across)
        copies = [first_up, first_down, next_up, next_down, four, five, everything]
        def s0(): keep.start(); first_up.start(); first_down.start()
        def s1(): first_up.wait_recv(); next_up.start(); first_down.wait_recv(); next_down.start()
        def s2(): next_up.wait_recv(); next_down.wait_recv(); keep.wait(); four.start()
        def s3(): four.wait_recv(); five.start()
        def s4(): five.wait_recv(); everything.start()
    else:
        if order == "xyz":
            one, two = move(0, own, place.across, here), move(1, full.at[t, z, :, c, :, lanes], place.beside)
        else:
            one, two = move(0, own, place.beside, here), move(1, full.at[:, z, x, c, :, lanes], place.across)
        first_up, first_down = move(2, full.at[:, z, :, c, :, lanes], place.up), move(3, full.at[:, z, :, c, :, lanes], place.down)
        next_up = move(4, full.at[0, place.below, :, c, :, lanes], place.up)
        next_down = move(5, full.at[1, place.above, :, c, :, lanes], place.down)
        copies = [one, two, first_up, first_down, next_up, next_down, everything]
        def s0(): keep.start(); one.start()
        def s1(): one.wait_recv(); keep.wait(); two.start()
        def s2(): two.wait_recv(); first_up.start(); first_down.start()
        def s3(): first_up.wait_recv(); next_up.start(); first_down.wait_recv(); next_down.start()
        def s4(): next_up.wait_recv(); next_down.wait_recv(); everything.start()
    def s5():
        everything.wait_recv()
        for copy in copies: copy.wait_send()
    return [s0, s1, s2, s3, s4, s5]


def add_blocks(count, dst, *srcs):
    def body(i, _):
        ref = dst(i)
        total = ref[...].astype(F32)
        for s in srcs: total = total + s(i)[...].astype(F32)
        ref[...] = total.astype(ref.dtype)
        return 0
    lax.fori_loop(0, count, body, 0)


def reduce_scratch(order, rows, lanes):
    V = lambda *s: pltpu.VMEM(s + (rows, lanes), BF16)
    base = [V(2, 4, 2), V(2, 4, 2)]
    if order == "yxz": base += [V(4, 2), V(4), V(), V(2)]
    elif order == "xyz": base += [V(2, 4), V(4), V(), V(2)]
    else: base += [V(2, 2), V(2, 2, 2), V(2), V()]
    return base + [pltpu.SemaphoreType.DMA((7,)), pltpu.SemaphoreType.DMA((7,)), pltpu.SemaphoreType.DMA]


def reduce_stages(place, order, grad, first, count, out, scratch):
    held, r0, r1, r2, r3, r4, send, recv, local = scratch
    z, x, c, t = place.z, place.x, place.c, place.t
    lanes = pl.ds(first, count)
    part = count // 256 * 128
    low, high = pl.ds(0, part), pl.ds(part, count - part)
    load = pltpu.make_async_copy(grad.at[:, :, :, c, :, lanes], held, local)
    def move(i, src, dst, peer):
        return remote(src, dst, send.at[i], recv.at[i], peer)
    c0 = move(0, grad.at[:, :, :, 1 - c, :, lanes], r0, place.twin)
    at3 = lambda ref: (lambda i: ref.at[i // 8, (i // 2) % 4, i % 2])
    def s0(): load.start(); c0.start()
    if order[0] != "z":
        if order == "yxz":
            c1, c2 = move(1, held.at[1 - t], r1, place.beside), move(2, held.at[t, :, 1 - x], r2, place.across)
            def add1(): add_blocks(8, lambda i: held.at[t, i // 2, i % 2], lambda i: r1.at[i // 2, i % 2])
        else:
            c1, c2 = move(1, held.at[:, :, 1 - x], r1, place.across), move(2, held.at[1 - t, :, x], r2, place.beside)
            def add1(): add_blocks(8, lambda i: held.at[i // 4, i % 4, x], lambda i: r1.at[i // 4, i % 4])
        mine = lambda k: held.at[t, k, x]
        c3 = move(3, held.at[t, place.far, x, :, low], r3.at[:, low], place.up)
        c4 = move(4, held.at[t, place.far, x, :, high], r3.at[:, high], place.down)
        c5, c6 = move(5, mine(place.above), r4.at[0], place.up), move(6, mine(place.below), r4.at[1], place.down)
        def s1(): load.wait(); c0.wait_recv(); add_blocks(16, at3(held), at3(r0)); c1.start()
        def s2(): c1.wait_recv(); add1(); c2.start()
        def s3(): c2.wait_recv(); add_blocks(4, mine, lambda k: r2.at[k]); c3.start(); c4.start()
        def s4():
            c3.wait_recv()
            v = held.at[t, place.above, x, :, low]; v[...] = (v[...].astype(F32) + r3[:, low].astype(F32)).astype(BF16)
            c5.start()
            c4.wait_recv()
            v = held.at[t, place.below, x, :, high]; v[...] = (v[...].astype(F32) + r3[:, high].astype(F32)).astype(BF16)
            c6.start()
        def s5():
            c5.wait_recv(); c6.wait_recv()
            out[:, lanes] = mine(z)[...].astype(F32) + r4[0].astype(F32) + r4[1].astype(F32)
            for copy in (c0, c1, c2, c3, c4, c5, c6): copy.wait_send()
    else:
        c1, c2 = move(1, held.at[0, place.far], r1.at[0], place.up), move(2, held.at[1, place.far], r1.at[1], place.down)
        c3, c4 = move(3, held.at[:, place.above], r2.at[0], place.up), move(4, held.at[:, place.below], r2.at[1], place.down)
        if order == "zyx":
            c5, c6 = move(5, held.at[1 - t, z], r3, place.beside), move(6, held.at[t, z, 1 - x], r4, place.across)
            def add5(): add_blocks(2, lambda k: held.at[t, z, k], lambda k: r3.at[k])
        else:
            c5, c6 = move(5, held.at[:, z, 1 - x], r3, place.across), move(6, held.at[1 - t, z, x], r4, place.beside)
            def add5(): add_blocks(2, lambda k: held.at[k, z, x], lambda k: r3.at[k])
        def s1(): load.wait(); c0.wait_recv(); add_blocks(16, at3(held), at3(r0)); c1.start(); c2.start()
        def s2():
            c1.wait_recv(); add_blocks(2, lambda k: held.at[0, place.above, k], lambda k: r1.at[0, k]); c3.start()
            c2.wait_recv(); add_blocks(2, lambda k: held.at[1, place.below, k], lambda k: r1.at[1, k]); c4.start()
        def s3():
            c3.wait_recv(); c4.wait_recv()
            add_blocks(4, lambda k: held.at[k // 2, z, k % 2], lambda k: r2.at[0, k // 2, k % 2], lambda k: r2.at[1, k // 2, k % 2])
            c5.start()
        def s4(): c5.wait_recv(); add5(); c6.start()
        def s5():
            c6.wait_recv()
            out[:, lanes] = held[t, z, x].astype(F32) + r4[...].astype(F32)
            for copy in (c0, c1, c2, c3, c4, c5, c6): copy.wait_send()
    return [s0, s1, s2, s3, s4, s5]


FRONT_ITEMS = {
    "q": (0, 0, 1, "zyx"),
    "k": (1, 0, 1, "zyx"),
    "v": (2, 0, 1, "yxz"),
    "o0": (3, 0, 1, "xyz"),
    "i0": (4, 0, 4, "xyz"),
    "i1": (4, 1, 4, "zxy"),
    "i2": (4, 2, 4, "zxy"),
    "i3": (4, 3, 4, "zxy"),
    "b0": (5, 0, 4, "zyx"),
    "b1": (5, 1, 4, "xyz"),
    "b2": (5, 2, 4, "zyx"),
    "b3": (5, 3, 4, "zyx"),
}
BACK_ITEMS = {
    "q": (0, 0, 1, "yxz"),
    "k": (1, 0, 1, "xyz"),
    "v": (2, 0, 1, "zxy"),
    "o0": (3, 0, 1, "zyx"),
    "i0": (4, 0, 4, "zxy"),
    "i1": (4, 1, 4, "xyz"),
    "i2": (4, 2, 4, "zyx"),
    "i3": (4, 3, 4, "zyx"),
    "b0": (5, 0, 4, "xyz"),
    "b1": (5, 1, 4, "xyz"),
    "b2": (5, 2, 4, "zxy"),
    "b3": (5, 3, 4, "yxz"),
}
FRONT_ORDER = (
    (("q", 0), ("v", 0), ("h1", 0), ("k", 0), ("v", 1), ("q", 1), ("b2", 0), ("k", 1), ("q", 2), ("v", 2), ("h1", 1), ("b2", 1), ("i1", 0), ("i0", 0), ("k", 2), ("i2", 0), ("b1", 0), ("h0", 0), ("h2", 0), ("h3", 0), ("o0", 0), ("i0", 1), ("q", 3), ("b1", 1), ("o0", 1), ("k", 3), ("v", 3), ("b3", 0), ("b2", 2), ("i1", 1), ("h0", 1), ("i2", 1), ("q", 4), ("v", 4), ("q", 5), ("h2", 1), ("b3", 1), ("i1", 2), ("i3", 0), ("v", 5), ("i2", 2), ("k", 4), ("b0", 0), ("b3", 2), ("h3", 1),),
    (("k", 5),),
    (),
    (("i1", 3), ("i0", 2), ("i2", 3), ("i3", 1), ("b0", 1), ("b1", 2), ("o0", 2), ("b2", 3),),
    (),
    (("b3", 3),),
    (("i0", 3), ("i3", 2), ("b0", 2), ("b2", 4),),
    (("i1", 4),),
    (("b2", 5),),
    (("i1", 5), ("b3", 4), ("i2", 4), ("b1", 3),),
    (("b3", 5), ("i3", 3), ("b0", 3),),
    (("i2", 5), ("o0", 3),),
    (("i0", 4),),
    (("i3", 4), ("b1", 4), ("i0", 5), ("b0", 4),),
    (("i3", 5), ("o0", 4),),
    (("b1", 5), ("b0", 5), ("o0", 5),),
)
BACK_ORDER = (
    (),
    (),
    (("b0", 0),),
    (("b0", 1),),
    (("i2", 0), ("i0", 0), ("i3", 0), ("b2", 0),),
    (("o0", 0), ("i2", 1), ("i0", 1), ("i3", 1), ("b0", 2), ("b2", 1),),
    (("o0", 1), ("b3", 0), ("i2", 2), ("b0", 3),),
    (("b1", 0), ("i1", 0), ("b3", 1), ("i0", 2), ("i3", 2),),
    (("b1", 1), ("i1", 1), ("o0", 2), ("b2", 2),),
    (("b3", 2),),
    (("b1", 2), ("i2", 3), ("b0", 4),),
    (),
    (("b1", 3), ("i1", 2), ("q", 0), ("b3", 3), ("i2", 4), ("i0", 3), ("i3", 3),),
    (("k", 0), ("q", 1), ("i1", 3), ("sm", 0), ("o0", 3), ("i2", 5), ("i0", 4), ("k", 1), ("sm", 1), ("i3", 4),),
    (("v", 0),),
    (("r2", 0), ("v", 1), ("b1", 4), ("q", 2), ("o0", 4), ("k", 2), ("i1", 4), ("b3", 4), ("sm", 2), ("i0", 5), ("r0", 0), ("i3", 5), ("v", 2), ("r2", 1), ("b2", 3), ("b1", 5), ("q", 3), ("o0", 5), ("r3", 0), ("k", 3), ("i1", 5), ("sm", 3), ("b3", 5), ("r1", 0), ("b0", 5), ("b2", 4),),
    (("r0", 1), ("v", 3), ("q", 4), ("k", 4), ("r3", 1), ("sm", 4), ("v", 4), ("q", 5), ("k", 5), ("r1", 1), ("sm", 5), ("b2", 5), ("v", 5),),
)


def fold_stages(place, part, got, send, recv):
    flip = place.z % 2
    near = jax.tree.map(lambda u, d: u + flip * (d - u), place.up, place.down)
    next_ = jax.tree.map(lambda u, d: d + flip * (u - d), place.up, place.down)
    peers = (place.twin, place.across, place.beside, near, next_)
    copies = [remote(part, got.at[i], send.at[i], recv.at[i], peer) for i, peer in enumerate(peers)]
    def stage(i):
        def run():
            if i > 0:
                copies[i - 1].wait()
                part[...] = part[...] + got[i - 1]
            if i < 5:
                copies[i].start()
        return run
    return [stage(i) for i in range(6)]


def swap(away, into, send, recv, peer, parts=4):
    size = away.shape[0] // parts
    plans = []
    for i in range(parts):
        r = pl.ds(i * size, size)
        give = remote(away.at[r], into.at[r], send.at[i], recv.at[i], peer)
        plans.append([give.start, give.wait])
    return plans


def whole(s):
    return pl.BlockSpec(s, lambda i: (0,) * len(s), pipeline_mode=pl.Buffered(1))


def forward_pair(bq, hook, len_ref, q_ref, k_ref, v_ref, o_ref, lse_ref):
    rows = q_ref.shape[0]
    n = len_ref[0]
    lane = lax.broadcasted_iota(jnp.int32, (1, 128), 1)
    krow = lax.broadcasted_iota(jnp.int32, (rows, 1), 0)
    kbias = jnp.where((krow + len_ref[1]) % rows < n, 0.0, -1e9)
    first = lane < DH
    for i in range(rows // bq):
        if i % (rows // bq // 2) == 0:
            hook(i * 2 * bq // rows)
            k = k_ref[...].astype(F32)
            v = v_ref[...]
            kas = []
            for h in range(2):
                own = lane // DH == h
                kas.append(jnp.where(own, k, jnp.where(lane == DH * (1 - h), kbias, 0.0)).astype(BF16))
        place = pl.ds(i * bq, bq)
        q = q_ref[place].astype(F32)
        os_, ls = [], []
        for h in range(2):
            own = lane // DH == h
            qa = jnp.where(own, q, jnp.where(lane == DH * (1 - h), 1.0, 0.0)).astype(BF16)
            s = nt(qa, kas[h])
            m = jnp.max(s, axis=1, keepdims=True)
            p = jnp.exp(s - m)
            l = jnp.sum(p, axis=1, keepdims=True)
            os_.append(nn(p.astype(BF16), v) * (1.0 / l))
            ls.append(m + jnp.log(l))
        o_ref[place] = jnp.where(first, os_[0], os_[1]).astype(BF16)
        lse_ref[place] = jnp.where(first, ls[1], ls[0])


def attend_forward(length, q, k, v, bq=256):
    rows, width = q.shape
    spec = pl.BlockSpec((rows, 128), lambda i: (0, i))
    return pl.pallas_call(
        functools.partial(forward_pair, bq, lambda i: None),
        grid=(width // 128,),
        in_specs=[SMALL, spec, spec, spec],
        out_specs=[spec, spec],
        out_shape=[S((rows, width), BF16), S((rows, width), F32)],
        compiler_params=pltpu.CompilerParams(vmem_limit_bytes=56 << 20),
        name="attend_forward",
    )(length, q, k, v)


def run(plans, events):
    for name, stage in events:
        plans[name][stage]()


def front(length, hidden, shards, b_query, b_value, bq=256):
    n = len(shards)
    rows, width = 2 * hidden.shape[1], hidden.shape[2]
    half, pairs = width // 2, width // 128
    items = [(name, w, shards[w].shape[1] // parts * i, shards[w].shape[1] // parts, order) for name, (w, i, parts, order) in FRONT_ITEMS.items()]

    def kernel(*refs):
        len_ref, pair_ref, given, bq_ref, bv_ref = refs[0], refs[1], refs[2 : 2 + n], refs[2 + n], refs[3 + n]
        refs = refs[4 + n :]
        o_ref, lse_ref, outs = refs[0], refs[1], refs[2 : 6 + n]
        refs = refs[6 + n :]
        rows_s, q_s, k_s, v_s, near, (send, recv, out_sem), sems = refs[0], refs[1], refs[2], refs[3], refs[4:7], refs[7:10], refs[10:]
        step = pl.program_id(0)
        place = Place()
        fulls = list(near) + list(outs[7:])
        local = rows // 2
        keep = pltpu.make_async_copy(pair_ref.at[place.t], rows_s.at[pl.ds(0, local)], out_sem.at[7])
        plans = {
            f"h{i}": plan
            for i, plan in enumerate(swap(pair_ref.at[1 - place.t], rows_s.at[pl.ds(local, local)], send, recv, place.beside))
        }
        for i, (name, w, at, count, order) in enumerate(items):
            plans[name] = gather_stages(place, order, given[w], fulls[w], at, count, *sems[3 * i : 3 * i + 3])
        stores = [pltpu.make_async_copy(src, dst, out_sem.at[i]) for i, (src, dst) in enumerate(zip((rows_s, q_s, k_s, v_s) + tuple(near), outs))]

        def project(full, dst, bias, scale):
            def block(i, _):
                r = pl.ds(pl.multiple_of(i * 256, 256), 256)
                for t in range(2):
                    v = nn(rows_s[r], full[t].reshape(width, half))
                    if bias is not None:
                        v = v + bias[:, t * half : (t + 1) * half]
                    dst[r, t * half : (t + 1) * half] = (v * scale).astype(BF16)
                return 0
            lax.fori_loop(0, rows // 256, block, 0)

        @pl.when(step == 0)
        def _():
            keep.start()
            place.greet()
            run(plans, FRONT_ORDER[0])
            keep.wait()
            project(near[0], q_s, bq_ref, 0.125)
            run(plans, FRONT_ORDER[1])
            project(near[1], k_s, None, 1.0)
            run(plans, FRONT_ORDER[2])
            project(near[2], v_s, bv_ref, 1.0)
            for store in stores:
                store.start()

        def hook(part):
            for i in range(pairs):
                @pl.when(step == 1 + i)
                def _():
                    run(plans, FRONT_ORDER[3 + 2 * i + part])

        @pl.when(step > 0)
        def _():
            cols = pl.ds(pl.multiple_of((step - 1) * 128, 128), 128)
            forward_pair(bq, hook, len_ref, q_s.at[:, cols], k_s.at[:, cols], v_s.at[:, cols], o_ref, lse_ref)

        @pl.when(step == pairs)
        def _():
            run(plans, FRONT_ORDER[3 + 2 * pairs])
            for store in stores:
                store.wait()

    spec = pl.BlockSpec((rows, 128), lambda i: (0, jnp.maximum(i - 1, 0)))
    flat = S((rows, width), BF16)
    full = [S((2, 4, 2, 2) + s.shape, BF16) for s in shards]
    V = pltpu.VMEM
    return pl.pallas_call(
        kernel,
        grid=(1 + pairs,),
        in_specs=[SMALL, HBM] + [HBM] * n + [whole((1, width))] * 2,
        out_specs=[spec, spec] + [HBM] * (4 + n),
        out_shape=[flat, S((rows, width), F32), flat, flat, flat, flat] + full,
        scratch_shapes=[V((rows, width), BF16)] * 4 + [V(f.shape, BF16) for f in full[:3]] + [DMA((4,)), DMA((4,)), DMA((8,))]
        + [s for _ in items for s in (DMA((7,)), DMA((7,)), DMA)],
        cost_estimate=pl.CostEstimate(flops=10 * rows * rows * width, bytes_accessed=40 << 20, transcendentals=rows * rows * 12),
        compiler_params=pltpu.CompilerParams(collective_id=1, has_side_effects=True, vmem_limit_bytes=56 << 20),
        name="front",
    )(length, hidden, *shards, b_query, b_value)


def backward_pair(bk, hook, len_ref, q_ref, k_ref, v_ref, d_ref, o_ref, lse_ref, dq_ref, dk_ref, dv_ref, qa_s, ka_s, va_s, da_s, acc):
    rows = q_ref.shape[0]
    n = len_ref[0]
    lane = lax.broadcasted_iota(jnp.int32, (1, 128), 1)
    krow = lax.broadcasted_iota(jnp.int32, (rows, 1), 0)
    kbias = jnp.where((krow + len_ref[1]) % rows < n, 0.0, -1e9)
    d = d_ref[...].astype(F32)
    prod = d * o_ref[...].astype(F32)
    hi, mid, lo = split3(-lse_ref[...])
    for h in range(2):
        own = lane // DH == h
        sp = DH * (1 - h)
        def pick(a, b, c, e):
            return jnp.where(lane == sp, a, jnp.where(lane == sp + 1, b, jnp.where(lane == sp + 2, c, jnp.where(lane == sp + 3, e, 0.0))))
        dh, dm, dl = split3(-jnp.sum(jnp.where(own, prod, 0.0), axis=1, keepdims=True))
        qa_s[h] = jnp.where(own, q_ref[...].astype(F32), pick(hi, mid, lo, 1.0)).astype(BF16)
        ka_s[h] = jnp.where(own, k_ref[...].astype(F32), pick(1.0, 1.0, 1.0, kbias)).astype(BF16)
        da_s[h] = jnp.where(own, d, pick(dh, dm, dl, 0.0)).astype(BF16)
        va_s[h] = jnp.where(own, v_ref[...].astype(F32), pick(1.0, 1.0, 1.0, 0.0)).astype(BF16)
    first = lane < DH
    upper = lax.broadcasted_iota(jnp.int32, (128, 1), 0) < DH
    for kb in range(0, rows, bk):
        if kb % (rows // 2) == 0:
            hook(kb * 2 // rows)
        dks, dvs, dqs = [], [], []
        for h in range(2):
            p = jnp.exp(nt(ka_s[h, kb : kb + bk], qa_s[h]))
            ds = (p * nt(va_s[h, kb : kb + bk], da_s[h])).astype(BF16)
            dvs.append(nn(p.astype(BF16), d_ref[...]))
            dks.append(nn(ds, q_ref[...]))
            dqs.append(tn(k_ref[kb : kb + bk], ds))
        dk_ref[kb : kb + bk] = jnp.where(first, dks[0], dks[1]).astype(BF16)
        dv_ref[kb : kb + bk] = jnp.where(first, dvs[0], dvs[1]).astype(BF16)
        dq = jnp.where(upper, dqs[0], dqs[1])
        if kb == 0:
            acc[...] = dq
        else:
            acc[...] += dq
    dq_ref[...] = (acc[...].T * 0.125).astype(BF16)


def pair_scratch(rows):
    aug = pltpu.VMEM((2, rows, 128), BF16)
    return [aug, aug, aug, aug, pltpu.VMEM((128, rows), F32)]


def attend_backward(length, q, k, v, d, o, lse, bk=256):
    rows, width = q.shape
    spec = pl.BlockSpec((rows, 128), lambda i: (0, i))
    return pl.pallas_call(
        functools.partial(backward_pair, bk, lambda i: None),
        grid=(width // 128,),
        in_specs=[SMALL] + [spec] * 6,
        out_specs=[spec] * 3,
        out_shape=[S((rows, width), BF16)] * 3,
        scratch_shapes=pair_scratch(rows),
        compiler_params=pltpu.CompilerParams(vmem_limit_bytes=56 << 20),
        name="attend_backward",
    )(length, q, k, v, d, o, lse)


def back(length, q, k, v, d, o, lse, rows_in, fulls, grad_one, small, grads, bk=256):
    n = len(grads)
    rows, width = q.shape
    half, pairs = width // 2, width // 128
    shards = [(grads[0].shape[4], half)] * 3 + [g.shape[4:] for g in grads]
    items = [(name, w, shards[w][1] // parts * i, shards[w][1] // parts, order) for name, (w, i, parts, order) in BACK_ITEMS.items()]
    vb = small.shape[0] - 4

    def kernel(*refs):
        main_in, rows_ref, full, one_ref, small_ref, given = refs[:7], refs[7], refs[8:11], refs[11], refs[12], refs[13 : 13 + n]
        refs = refs[13 + n :]
        pair_ref, sum_ref, outs = refs[0], refs[1], refs[2 : 5 + n]
        refs = refs[5 + n :]
        dq_s, dk_s, dv_s, rT, gr_s = refs[:5]
        own, part, got, fold_send, fold_recv, (send, recv, local_sem) = refs[5:8], refs[8], refs[9], refs[10], refs[11], refs[12:15]
        main_scratch, scratch = refs[15:20], refs[20:]
        step = pl.program_id(0)
        place = Place()
        local = rows // 2
        keep = pltpu.make_async_copy(gr_s.at[pl.ds(0, local)], pair_ref.at[place.t], local_sem)
        plans = {
            f"r{i}": plan
            for i, plan in enumerate(swap(gr_s.at[pl.ds(local, local)], pair_ref.at[place.t], send, recv, place.beside))
        }
        plans["sm"] = fold_stages(place, part, got, fold_send, fold_recv)
        sources = list(own) + list(given)
        for i, (name, w, at, count, order) in enumerate(items):
            plans[name] = reduce_stages(place, order, sources[w], at, count, outs[w], scratch[9 * i : 9 * i + 9])

        @pl.when(step == 0)
        def _():
            place.greet()

        def hook(j):
            for i in range(pairs):
                @pl.when(step == i)
                def _():
                    run(plans, BACK_ORDER[2 * i + j])

        @pl.when(step < pairs)
        def _():
            cols = pl.ds(pl.multiple_of(step * 128, 128), 128)
            backward_pair(bk, hook, *main_in, dq_s.at[:, cols], dk_s.at[:, cols], dv_s.at[:, cols], *main_scratch)

        @pl.when(step == pairs)
        def _():
            at = 2 * pairs
            rT[...] = rows_ref[...].T
            part[...] = small_ref[...]
            for i, d_s in enumerate((dq_s, dk_s, dv_s)):
                for t in range(2):
                    own[i][t] = nn(rT[...], d_s[:, t * half : (t + 1) * half]).astype(BF16).reshape(own[i].shape[1:])
                if i == 0:
                    part[vb : vb + 1] = colsum(dq_s[...].astype(F32))
                    part[vb + 1 : vb + 2] = colsum(dv_s[...].astype(F32))
                run(plans, BACK_ORDER[at + i])
            for j in (1, 0):
                def block(i, _):
                    r = pl.ds(pl.multiple_of(i * 256, 256), 256)
                    total = one_ref[r]
                    for d_s, w in zip((dq_s, dk_s, dv_s), full):
                        for t in range(2):
                            total = total + nt(d_s[r, t * half : (t + 1) * half], w[t])
                    gr_s[r] = total.astype(BF16)
                    return 0
                lax.fori_loop(j * (rows // 512), (j + 1) * (rows // 512), block, 0)
                if j == 0:
                    keep.start()
                run(plans, BACK_ORDER[at + 4 - j])
            keep.wait()
            sum_ref[...] = part[...]

    spec = pl.BlockSpec((rows, 128), lambda i: (0, jnp.minimum(i, pairs - 1)))
    V = pltpu.VMEM
    flat = V((rows, width), BF16)
    outs = [S(s, F32) for s in shards]
    return pl.pallas_call(
        kernel,
        grid=(pairs + 1,),
        in_specs=[SMALL] + [spec] * 6 + [whole((rows, width))] + [whole(f.shape) for f in fulls] + [whole((rows, width)), whole(small.shape)] + [HBM] * n,
        out_specs=[HBM, whole(small.shape)] + [whole(s) for s in shards],
        out_shape=[S((2, rows // 2, width), BF16), S(small.shape, F32)] + outs,
        scratch_shapes=[flat, flat, flat, V((width, rows), BF16), flat]
        + [V((2, 4, 2, 2) + shards[0], BF16)] * 3
        + [V(small.shape, F32), V((5,) + small.shape, F32), DMA((5,)), DMA((5,)), DMA((4,)), DMA((4,)), DMA]
        + pair_scratch(rows)
        + [s for _, w, f, c, o in items for s in reduce_scratch(o, shards[w][0], c)],
        cost_estimate=pl.CostEstimate(flops=20 * rows * rows * width, bytes_accessed=60 << 20, transcendentals=rows * rows * 12),
        compiler_params=pltpu.CompilerParams(collective_id=2, has_side_effects=True, vmem_limit_bytes=63 << 20),
        name="back",
    )(length, q, k, v, d, o, lse, rows_in, *fulls, grad_one, small, *grads)


def norm_parts(v):
    c = v - jnp.mean(v, axis=-1, keepdims=True)
    r = lax.rsqrt(jnp.mean(c * c, axis=-1, keepdims=True) + 1e-5)
    return c * r, r


def norm_back(n, r, dyg):
    return r * (dyg - jnp.mean(dyg, axis=-1, keepdims=True) - n * jnp.mean(dyg * n, axis=-1, keepdims=True))


def colsum(v):
    return jnp.sum(v, axis=0, keepdims=True)


def mlp_up_kernel(chunk, a_ref, h_ref, wo_ref, wi_ref, wb_ref, vec_ref, bi_ref, out_ref, mid_ref, v1_ref, v2_ref, act, gp, b2):
    half, inner = wo_ref.shape[2], wi_ref.shape[2]
    b_out, b_back, gain_one, shift_one, gain_two, shift_two = [vec_ref[i : i + 1] for i in range(6)]
    v1 = h_ref[...].astype(F32) + (nt(a_ref[:, :half], wo_ref[0]) + nt(a_ref[:, half:], wo_ref[1])) + b_out
    v1_ref[...] = v1
    n1, r1 = norm_parts(v1)
    normed = n1 * gain_one + shift_one
    mid = normed.astype(BF16)
    mid_ref[...] = mid
    b2[...] = normed + b_back

    def up(i, _):
        t = i // (inner // chunk)
        cols = pl.ds(pl.multiple_of(i % (inner // chunk) * chunk, chunk), chunk)
        hp = nn(mid, wi_ref[t, :, cols]) + bi_ref[t, :, cols]
        half_up = 0.5 + 0.5 * lax.erf(hp * math.sqrt(0.5))
        a = (hp * half_up).astype(BF16)
        act[t, :, cols] = a
        gp[t, :, cols] = (half_up + hp * (jnp.exp(hp * hp * -0.5) * (1.0 / math.sqrt(2 * math.pi)))).astype(BF16)
        b2[...] += nt(a, wb_ref[t, :, cols])
        return 0

    lax.fori_loop(0, 2 * inner // chunk, up, 0)
    v2_ref[...] = b2[...]
    n2, r2 = norm_parts(b2[...])
    out_ref[...] = (n2 * gain_two + shift_two).astype(BF16)


def mlp_up(a, h, wo, wi, wb, vec, bi, rows=256, chunk=768):
    total, width = a.shape
    inner = wi.shape[2]
    row = pl.BlockSpec((rows, width), lambda i: (i, 0))
    wide = pl.BlockSpec((2, rows, inner), lambda i: (0, i, 0))
    return pl.pallas_call(
        functools.partial(mlp_up_kernel, chunk),
        grid=(total // rows,),
        in_specs=[row, row] + [whole(s.shape) for s in (wo, wi, wb, vec, bi)],
        out_specs=[row, row, row, row, wide, wide],
        out_shape=[S((total, width), BF16), S((total, width), BF16), S((total, width), F32), S((total, width), F32), S((2, total, inner), BF16), S((2, total, inner), BF16)],
        scratch_shapes=[pltpu.VMEM((rows, width), F32)],
        cost_estimate=pl.CostEstimate(flops=total * width * (8 * inner + 2 * width), bytes_accessed=40 << 20, transcendentals=4 * total * inner),
        compiler_params=pltpu.CompilerParams(vmem_limit_bytes=60 << 20),
        name="mlp_up",
    )(a, h, wo, wi, wb, vec, bi)


def mlp_down_kernel(len_ref, a_ref, mid_ref, near_ref, far_ref, v1_ref, v2_ref, wo_ref, vec_ref, wi_ref, wb_ref, act_ref, gp_ref,
                    g1_ref, ga_ref, gwo_ref, gwi_ref, gwb_ref, small_ref, gbi_ref, back, btT, midT, gn):
    step = pl.program_id(0)
    rows, half, block = a_ref.shape[0], wo_ref.shape[2], 256
    b_out, b_back, gain_one, shift_one, gain_two, shift_two = [vec_ref[i : i + 1] for i in range(6)]

    @pl.when(step == 0)
    def _():
        small_ref[...] = jnp.zeros_like(small_ref)
        midT[...] = mid_ref[...].T
        for b in range(rows // block):
            r = slice(b * block, (b + 1) * block)
            n2, r2 = norm_parts(v2_ref[r])
            place = (b * block + lax.broadcasted_iota(jnp.int32, (block, 1), 0) + len_ref[1]) % rows
            c = (near_ref if b < rows // block // 2 else far_ref)[(b * block) % (rows // 2) : (b * block) % (rows // 2) + block]
            go = c.astype(F32) * jnp.where(place < len_ref[0], 1.0, 0.0)
            grad_two = norm_back(n2, r2, go * gain_two)
            bt = grad_two.astype(BF16)
            back[r] = bt
            btT[:, r] = bt.T
            gn[r] = grad_two
            small_ref[1:2] += colsum(grad_two)
            small_ref[4:5] += colsum(go * n2)
            small_ref[5:6] += colsum(go)

    gb = (nn(back[...], wb_ref[0]) * gp_ref[0].astype(F32)).astype(BF16)
    gbi_ref[0] = colsum(gb.astype(F32))
    gwb_ref[0] = nn(btT[...], act_ref[0]).astype(BF16)
    gwi_ref[0] = nn(midT[...], gb).astype(BF16)
    gn[...] += nt(gb, wi_ref[0])

    @pl.when(step == pl.num_programs(0) - 1)
    def _():
        for b in range(rows // block):
            r = slice(b * block, (b + 1) * block)
            g = gn[r]
            n1, r1 = norm_parts(v1_ref[r])
            grad_one = norm_back(n1, r1, g * gain_one)
            bo = grad_one.astype(BF16)
            back[r] = bo
            g1_ref[r] = grad_one
            small_ref[0:1] += colsum(grad_one)
            small_ref[2:3] += colsum(g * n1)
            small_ref[3:4] += colsum(g)
            for t in range(2):
                ga_ref[r, t * half : (t + 1) * half] = nn(bo, wo_ref[t]).astype(BF16)
        btT[...] = back[...].T
        for t in range(2):
            gwo_ref[t] = nn(btT[...], a_ref[:, t * half : (t + 1) * half]).astype(BF16)


def mlp_down(length, a, mid, near, far, v1, v2, wo, wi, wb, act, gp, vec, bi, chunk=512):
    rows, width = a.shape
    inner = wi.shape[2]
    m = inner // chunk
    tall = pl.BlockSpec((1, rows, chunk), lambda i: (i // m, 0, i % m))
    weight = pl.BlockSpec((1, width, chunk), lambda i: (i // m, 0, i % m))
    thin = pl.BlockSpec((1, 1, chunk), lambda i: (i // m, 0, i % m))
    V = pltpu.VMEM
    return pl.pallas_call(
        mlp_down_kernel,
        grid=(2 * m,),
        in_specs=[SMALL] + [whole(s.shape) for s in (a, mid, near, far, v1, v2, wo, vec)] + [weight, weight, tall, tall],
        out_specs=[whole((rows, width)), whole((rows, width)), whole(wo.shape), weight, weight, whole(vec.shape), thin],
        out_shape=[S((rows, width), F32), S((rows, width), BF16), S(wo.shape, BF16), S(wi.shape, BF16), S(wb.shape, BF16), S(vec.shape, F32), S(bi.shape, F32)],
        scratch_shapes=[V((rows, width), BF16), V((width, rows), BF16), V((width, rows), BF16), V((rows, width), F32)],
        cost_estimate=pl.CostEstimate(flops=rows * width * (16 * inner + 4 * width), bytes_accessed=60 << 20, transcendentals=0),
        compiler_params=pltpu.CompilerParams(vmem_limit_bytes=60 << 20),
        name="mlp_down",
    )(length, a, mid, near, far, v1, v2, wo, vec, wi, wb, act, gp)


def per_device(
    hidden, lengths, cotangent, w_query, w_key, w_value, w_out, w_in, w_back,
    b_query, b_value, b_out, b_in, b_back, gain_one, shift_one, gain_two, shift_two,
):
    t = lax.axis_index("tensor")
    local = hidden.shape[1]
    width = b_query.shape[0]
    inner = b_in.shape[0]
    own_kernels = lax.axis_size("dp") == 16 and lax.axis_size("tensor") == 2
    flip = [(0, 1), (1, 0)]

    def mine(a):
        return lax.dynamic_index_in_dim(a, t, 0, keepdims=False)

    def take(a):
        other = lax.dynamic_index_in_dim(a, 1 - t, 0, keepdims=False)
        return jnp.concatenate([mine(a), lax.ppermute(other, "tensor", flip)], 0)

    def give(a):
        got = lax.ppermute(a[local:], "tensor", flip)
        first = t == 0
        return jnp.stack([jnp.where(first, a[:local], got), jnp.where(first, got, a[:local])], 0)

    def gather(w):
        return lax.all_gather(lax.all_gather(w, "dp", axis=0, tiled=True), "tensor", axis=0)

    def scatter(g):
        g = lax.psum_scatter(g, "dp", scatter_dimension=1, tiled=True)
        return lax.psum_scatter(g, "tensor", scatter_dimension=0, tiled=False).astype(F32)

    def flat(w):
        return w.reshape(2, width, -1)

    length = jnp.stack([mine(lengths)[0], t * local]).astype(jnp.int32)
    shards = (w_query, w_key, w_value, w_out, w_in, w_back)
    if own_kernels:
        attended, lse, rows, query, key, value, *fulls = front(length, hidden, shards, b_query[None], b_value[None])
        fulls = [flat(w) for w in fulls]
        cotangent = lax.optimization_barrier((cotangent, attended))[0]
    else:
        rows = take(hidden)
        fulls = [gather(w) for w in shards]

        def project(w):
            return jnp.concatenate([nn(rows, w[0]), nn(rows, w[1])], 1)

        query = ((project(fulls[0]) + b_query) * 0.125).astype(BF16)
        key = project(fulls[1]).astype(BF16)
        value = (project(fulls[2]) + b_value).astype(BF16)
        attended, lse = attend_forward(length, query, key, value)
    full_query, full_key, full_value, full_out, full_in, full_back = fulls
    vec = jnp.stack([b_out, b_back, gain_one, shift_one, gain_two, shift_two, b_out, b_out])
    bi = b_in.reshape(2, 1, inner // 2)
    near_cot = mine(cotangent)
    far_cot = lax.ppermute(lax.dynamic_index_in_dim(cotangent, 1 - t, 0, keepdims=False), "tensor", flip)
    out, mid, v1, v2, act, gp = mlp_up(attended, rows, full_out, full_in, full_back, vec, bi)
    output = give(out)
    grad_one, grad_attended, g_out, g_in, g_back, small, g_b_in = mlp_down(
        length, attended, mid, near_cot, far_cot, v1, v2, full_out, full_in, full_back, act, gp, vec, bi
    )
    small = jnp.concatenate([small, g_b_in.reshape(-1, width), jnp.zeros((4, width), F32)])
    def split(g):
        return g.reshape(2, 4, 2, 2, -1, g.shape[-1])
    vb = 8 + inner // width
    if own_kernels:
        grad_hidden, small, *owned = back(
            length, query, key, value, grad_attended, attended, lse, rows, fulls[:3], grad_one, small, [split(g) for g in (g_out, g_in, g_back)]
        )
    else:
        d_query, d_key, d_value = attend_backward(length, query, key, value, grad_attended, attended, lse)
        total = grad_one
        grads = []
        for d, w in ((d_query, full_query), (d_key, full_key), (d_value, full_value)):
            total = total + nt(d, jnp.concatenate([w[0], w[1]], 1))
            g = tn(rows, d).astype(BF16)
            grads.append(jnp.stack([g[:, : width // 2], g[:, width // 2 :]]))
        small = small.at[vb].set(jnp.sum(d_query.astype(F32), 0)).at[vb + 1].set(jnp.sum(d_value.astype(F32), 0))
        grad_hidden = give(total.astype(BF16))
        owned = [scatter(g) for g in grads + [g_out, g_in, g_back]]
        small = lax.psum(small, ("dp", "tensor"))
    return (
        output, grad_hidden, *owned,
        small[vb], small[vb + 1], small[0], small[8:vb].reshape(inner), small[1], small[2], small[3], small[4], small[5],
    )


def solution(mesh):
    rows = P(None, ("dp", "tensor"), None)
    weight = P("dp", "tensor")
    return jax.shard_map(
        per_device,
        mesh=mesh,
        in_specs=(rows, P(None, "dp"), rows) + (weight,) * 6 + (P(),) * 9,
        out_specs=(rows, rows) + (weight,) * 6 + (P(),) * 9,
        check_vma=False,
    )
```

```python
import functools
import math

import jax
import jax.numpy as jnp
from jax import lax
from jax.experimental import pallas as pl
from jax.experimental.pallas import tpu as pltpu
from jax.sharding import PartitionSpec as P

F32, BF16 = jnp.float32, jnp.bfloat16
DH = 64
S = jax.ShapeDtypeStruct
HBM = pl.BlockSpec(memory_space=pl.ANY)
SMALL = pl.BlockSpec(memory_space=pltpu.SMEM)
DMA = pltpu.SemaphoreType.DMA


def nt(a, b):
    return lax.dot_general(a, b, (((1,), (1,)), ((), ())), preferred_element_type=F32)


def nn(a, b):
    return lax.dot_general(a, b, (((1,), (0,)), ((), ())), preferred_element_type=F32)


def tn(a, b):
    return lax.dot_general(a, b, (((0,), (0,)), ((), ())), preferred_element_type=F32)


def split3(v):
    hi = v.astype(BF16).astype(F32)
    rest = v - hi
    mid = rest.astype(BF16).astype(F32)
    return hi, mid, rest - mid


class Place:
    def __init__(self):
        dp, t = lax.axis_index("dp"), lax.axis_index("tensor")
        z, x, c = dp // 4, (dp // 2) % 2, dp % 2
        self.z, self.x, self.c, self.t = z, x, c, t
        self.above, self.below, self.far = (z + 1) % 4, (z + 3) % 4, (z + 2) % 4
        at = lambda z, x, c, t: ((z * 2 + x) * 2 + c, t)
        self.up, self.down = at(self.above, x, c, t), at(self.below, x, c, t)
        self.across, self.beside, self.twin = at(z, 1 - x, c, t), at(z, x, c, 1 - t), at(z, x, 1 - c, t)

    def greet(self):
        barrier = pltpu.get_barrier_semaphore()
        for peer in (self.up, self.down, self.across, self.beside, self.twin):
            pl.semaphore_signal(barrier, inc=1, device_id=peer, device_id_type=pl.DeviceIdType.MESH)
        pl.semaphore_wait(barrier, 5)


def remote(src, dst, send, recv, peer):
    return pltpu.make_async_remote_copy(src, dst, send, recv, device_id=peer, device_id_type=pl.DeviceIdType.MESH)


def gather_stages(place, order, shard, full, first, count, send, recv, local):
    z, x, c, t = place.z, place.x, place.c, place.t
    lanes = pl.ds(first, count)
    part = count // 256 * 128
    low, high = pl.ds(first, part), pl.ds(first + part, count - part)
    own = full.at[t, z, x, c, :, lanes]
    here = shard.at[:, lanes]
    def move(i, view, peer, src=None):
        return remote(view if src is None else src, view, send.at[i], recv.at[i], peer)
    keep = pltpu.make_async_copy(here, own, local)
    everything = move(6, full.at[:, :, :, c, :, lanes], place.twin)
    if order[0] == "z":
        first_up, first_down = move(0, own, place.up, here), move(1, own, place.down, here)
        next_up = move(2, full.at[t, place.below, x, c, :, low], place.up)
        next_down = move(3, full.at[t, place.above, x, c, :, high], place.down)
        if order == "zxy":
            four, five = move(4, full.at[t, :, x, c, :, lanes], place.across), move(5, full.at[t, :, :, c, :, lanes], place.beside)
        else:
            four, five = move(4, full.at[t, :, x, c, :, lanes], place.beside), move(5, full.at[:, :, x, c, :, lanes], place.across)
        copies = [first_up, first_down, next_up, next_down, four, five, everything]
        def s0(): keep.start(); first_up.start(); first_down.start()
        def s1(): first_up.wait_recv(); next_up.start(); first_down.wait_recv(); next_down.start()
        def s2(): next_up.wait_recv(); next_down.wait_recv(); keep.wait(); four.start()
        def s3(): four.wait_recv(); five.start()
        def s4(): five.wait_recv(); everything.start()
    else:
        if order == "xyz":
            one, two = move(0, own, place.across, here), move(1, full.at[t, z, :, c, :, lanes], place.beside)
        else:
            one, two = move(0, own, place.beside, here), move(1, full.at[:, z, x, c, :, lanes], place.across)
        first_up, first_down = move(2, full.at[:, z, :, c, :, lanes], place.up), move(3, full.at[:, z, :, c, :, lanes], place.down)
        next_up = move(4, full.at[0, place.below, :, c, :, lanes], place.up)
        next_down = move(5, full.at[1, place.above, :, c, :, lanes], place.down)
        copies = [one, two, first_up, first_down, next_up, next_down, everything]
        def s0(): keep.start(); one.start()
        def s1(): one.wait_recv(); keep.wait(); two.start()
        def s2(): two.wait_recv(); first_up.start(); first_down.start()
        def s3(): first_up.wait_recv(); next_up.start(); first_down.wait_recv(); next_down.start()
        def s4(): next_up.wait_recv(); next_down.wait_recv(); everything.start()
    def s5():
        everything.wait_recv()
        for copy in copies: copy.wait_send()
    return [s0, s1, s2, s3, s4, s5]


def add_blocks(count, dst, *srcs):
    def body(i, _):
        ref = dst(i)
        total = ref[...].astype(F32)
        for s in srcs: total = total + s(i)[...].astype(F32)
        ref[...] = total.astype(ref.dtype)
        return 0
    lax.fori_loop(0, count, body, 0)


def reduce_scratch(order, rows, lanes):
    V = lambda *s: pltpu.VMEM(s + (rows, lanes), BF16)
    base = [V(2, 4, 2), V(2, 4, 2)]
    if order == "yxz": base += [V(4, 2), V(4), V(), V(2)]
    elif order == "xyz": base += [V(2, 4), V(4), V(), V(2)]
    else: base += [V(2, 2), V(2, 2, 2), V(2), V()]
    return base + [pltpu.SemaphoreType.DMA((7,)), pltpu.SemaphoreType.DMA((7,)), pltpu.SemaphoreType.DMA]


def reduce_stages(place, order, grad, first, count, out, scratch):
    held, r0, r1, r2, r3, r4, send, recv, local = scratch
    z, x, c, t = place.z, place.x, place.c, place.t
    lanes = pl.ds(first, count)
    part = count // 256 * 128
    if part:
        low, high = (slice(None), pl.ds(0, part)), (slice(None), pl.ds(part, count - part))
    else:
        low, high = (pl.ds(0, 16), slice(None)), (pl.ds(16, held.shape[3] - 16), slice(None))
    load = pltpu.make_async_copy(grad.at[:, :, :, c, :, lanes], held, local)
    def move(i, src, dst, peer):
        return remote(src, dst, send.at[i], recv.at[i], peer)
    c0 = move(0, grad.at[:, :, :, 1 - c, :, lanes], r0, place.twin)
    at3 = lambda ref: (lambda i: ref.at[i // 8, (i // 2) % 4, i % 2])
    def s0(): load.start(); c0.start()
    if order[0] != "z":
        if order == "yxz":
            c1, c2 = move(1, held.at[1 - t], r1, place.beside), move(2, held.at[t, :, 1 - x], r2, place.across)
            def add1(): add_blocks(8, lambda i: held.at[t, i // 2, i % 2], lambda i: r1.at[i // 2, i % 2])
        else:
            c1, c2 = move(1, held.at[:, :, 1 - x], r1, place.across), move(2, held.at[1 - t, :, x], r2, place.beside)
            def add1(): add_blocks(8, lambda i: held.at[i // 4, i % 4, x], lambda i: r1.at[i // 4, i % 4])
        mine = lambda k: held.at[t, k, x]
        c3 = move(3, held.at[(t, place.far, x) + low], r3.at[low], place.up)
        c4 = move(4, held.at[(t, place.far, x) + high], r3.at[high], place.down)
        c5, c6 = move(5, mine(place.above), r4.at[0], place.up), move(6, mine(place.below), r4.at[1], place.down)
        def s1(): load.wait(); c0.wait_recv(); add_blocks(16, at3(held), at3(r0)); c1.start()
        def s2(): c1.wait_recv(); add1(); c2.start()
        def s3(): c2.wait_recv(); add_blocks(4, mine, lambda k: r2.at[k]); c3.start(); c4.start()
        def s4():
            c3.wait_recv()
            v = held.at[(t, place.above, x) + low]; v[...] = (v[...].astype(F32) + r3[low].astype(F32)).astype(BF16)
            c5.start()
            c4.wait_recv()
            v = held.at[(t, place.below, x) + high]; v[...] = (v[...].astype(F32) + r3[high].astype(F32)).astype(BF16)
            c6.start()
        def s5():
            c5.wait_recv(); c6.wait_recv()
            out[:, lanes] = mine(z)[...].astype(F32) + r4[0].astype(F32) + r4[1].astype(F32)
            for copy in (c0, c1, c2, c3, c4, c5, c6): copy.wait_send()
    else:
        c1, c2 = move(1, held.at[0, place.far], r1.at[0], place.up), move(2, held.at[1, place.far], r1.at[1], place.down)
        c3, c4 = move(3, held.at[:, place.above], r2.at[0], place.up), move(4, held.at[:, place.below], r2.at[1], place.down)
        if order == "zyx":
            c5, c6 = move(5, held.at[1 - t, z], r3, place.beside), move(6, held.at[t, z, 1 - x], r4, place.across)
            def add5(): add_blocks(2, lambda k: held.at[t, z, k], lambda k: r3.at[k])
        else:
            c5, c6 = move(5, held.at[:, z, 1 - x], r3, place.across), move(6, held.at[1 - t, z, x], r4, place.beside)
            def add5(): add_blocks(2, lambda k: held.at[k, z, x], lambda k: r3.at[k])
        def s1(): load.wait(); c0.wait_recv(); add_blocks(16, at3(held), at3(r0)); c1.start(); c2.start()
        def s2():
            c1.wait_recv(); add_blocks(2, lambda k: held.at[0, place.above, k], lambda k: r1.at[0, k]); c3.start()
            c2.wait_recv(); add_blocks(2, lambda k: held.at[1, place.below, k], lambda k: r1.at[1, k]); c4.start()
        def s3():
            c3.wait_recv(); c4.wait_recv()
            add_blocks(4, lambda k: held.at[k // 2, z, k % 2], lambda k: r2.at[0, k // 2, k % 2], lambda k: r2.at[1, k // 2, k % 2])
            c5.start()
        def s4(): c5.wait_recv(); add5(); c6.start()
        def s5():
            c6.wait_recv()
            out[:, lanes] = held[t, z, x].astype(F32) + r4[...].astype(F32)
            for copy in (c0, c1, c2, c3, c4, c5, c6): copy.wait_send()
    return [s0, s1, s2, s3, s4, s5]


FRONT_ITEMS = {
    "q": (0, 0, 1, "zyx"),
    "k": (1, 0, 1, "zyx"),
    "v": (2, 0, 1, "yxz"),
    "o0": (3, 0, 1, "xyz"),
    "i0": (4, 0, 2, "zxy"),
    "i1": (4, 1, 2, "xyz"),
    "b0": (5, 0, 4, "zyx"),
    "b1": (5, 1, 4, "zxy"),
    "b2": (5, 2, 4, "zyx"),
    "b3": (5, 3, 4, "zyx"),
}
BACK_ITEMS = {
    "m0": (0, 0, 1, "yxz"),
    "m1": (1, 0, 1, "yxz"),
    "mq": (2, 0, 3, "zyx"),
    "mk": (2, 1, 3, "xyz"),
    "mv": (2, 2, 3, "zyx"),
    "o0": (3, 0, 1, "xyz"),
    "i0": (4, 0, 2, "zxy"),
    "i1": (4, 1, 2, "yxz"),
    "b0": (5, 0, 2, "zxy"),
    "b1": (5, 1, 2, "xyz"),
}
FRONT_ORDER = (
    (("v", 0), ("q", 0), ("h1", 0), ("k", 0), ("b0", 0), ("v", 1), ("q", 1), ("k", 1), ("v", 2), ("b0", 1), ("i0", 0), ("q", 2), ("k", 2), ("h0", 0), ("i1", 0), ("b1", 0), ("o0", 0), ("h1", 1), ("b2", 0), ("b3", 0), ("q", 3), ("i1", 1), ("v", 3), ("o0", 1), ("b0", 2), ("k", 3), ("i0", 1), ("b1", 1), ("b2", 1), ("q", 4), ("b3", 1), ("h0", 1), ("q", 5),),
    (("v", 4), ("i0", 2), ("i1", 2), ("k", 4), ("b1", 2), ("b2", 2), ("o0", 2), ("b3", 2), ("v", 5), ("k", 5),),
    (),
    (("b0", 3),),
    (("b2", 3), ("i0", 3),),
    (("b1", 3), ("b3", 3),),
    (("i1", 3),),
    (),
    (("b0", 4),),
    (("o0", 3),),
    (("b2", 4), ("b0", 5), ("i0", 4),),
    (("i1", 4),),
    (("b2", 5), ("i0", 5), ("b3", 4), ("o0", 4),),
    (("i1", 5), ("b1", 4),),
    (("o0", 5), ("b3", 5),),
    (("b1", 5),),
)
BACK_ORDER = (
    (("b0", 0),),
    (),
    (("b0", 1),),
    (("i1", 0),),
    (("b0", 2), ("m0", 0), ("i1", 1), ("b1", 0), ("o0", 0),),
    (("m0", 1),),
    (("b1", 1), ("i0", 0), ("o0", 1),),
    (),
    (("b0", 3), ("i1", 2), ("i0", 1),),
    (("m0", 2), ("b1", 2), ("m1", 0),),
    (("i0", 2),),
    (("m1", 1), ("o0", 2), ("b0", 4), ("b1", 3),),
    (),
    (("i1", 3), ("m1", 2),),
    (("r1", 0), ("b0", 5), ("m0", 3), ("r0", 0), ("i1", 4), ("b1", 4), ("i0", 3), ("o0", 3), ("m1", 3),),
    (("mq", 0), ("m0", 4), ("mv", 0), ("i1", 5), ("mk", 0),),
    (("sm", 0), ("mq", 1), ("i0", 4), ("mv", 1), ("b1", 5), ("r1", 1), ("o0", 4), ("sm", 1), ("mk", 1), ("m1", 4), ("m0", 5), ("mq", 2), ("sm", 2), ("mv", 2), ("mk", 2), ("o0", 5), ("m1", 5), ("r0", 1), ("mq", 3), ("i0", 5), ("sm", 3), ("mv", 3), ("mk", 3), ("mq", 4), ("sm", 4), ("mk", 4), ("mv", 4), ("mq", 5), ("mv", 5), ("sm", 5), ("mk", 5),),
)


def fold_stages(place, part, got, send, recv):
    flip = place.z % 2
    near = jax.tree.map(lambda u, d: u + flip * (d - u), place.up, place.down)
    next_ = jax.tree.map(lambda u, d: d + flip * (u - d), place.up, place.down)
    peers = (place.twin, place.across, place.beside, near, next_)
    copies = [remote(part, got.at[i], send.at[i], recv.at[i], peer) for i, peer in enumerate(peers)]
    def stage(i):
        def run():
            if i > 0:
                copies[i - 1].wait()
                part[...] = part[...] + got[i - 1]
            if i < 5:
                copies[i].start()
        return run
    return [stage(i) for i in range(6)]


def swap(away, into, send, recv, peer, parts=2):
    size = away.shape[0] // parts
    plans = []
    for i in range(parts):
        r = pl.ds(i * size, size)
        give = remote(away.at[r], into.at[r], send.at[i], recv.at[i], peer)
        plans.append([give.start, give.wait])
    return plans


def whole(s):
    return pl.BlockSpec(s, lambda i: (0,) * len(s), pipeline_mode=pl.Buffered(1))


def live_rows(len_ref, rows):
    t = lax.axis_index("tensor")
    place = lax.broadcasted_iota(jnp.int32, (rows, 1), 0)
    return (place + t * (rows // 2)) % rows < len_ref[t, 0]


def forward_pair(bq, hook, len_ref, q_ref, k_ref, v_ref, o_ref, lse_ref):
    rows = q_ref.shape[0]
    lane = lax.broadcasted_iota(jnp.int32, (1, 128), 1)
    kbias = jnp.where(live_rows(len_ref, rows), 0.0, -1e9)
    first = lane < DH

    def block(i, _):
        hook(i, rows // bq)
        place = pl.ds(pl.multiple_of(i * bq, bq), bq)
        q = q_ref[place].astype(F32)
        k, v = k_ref[...].astype(F32), v_ref[...]
        os_, ls = [], []
        for h in range(2):
            own, spare = lane // DH == h, lane == DH * (1 - h)
            qa = jnp.where(own, q, jnp.where(spare, 1.0, 0.0)).astype(BF16)
            ka = jnp.where(own, k, jnp.where(spare, kbias, 0.0)).astype(BF16)
            s = nt(qa, ka)
            m = jnp.max(s, axis=1, keepdims=True)
            p = jnp.exp(s - m)
            l = jnp.sum(p, axis=1, keepdims=True)
            os_.append(nn(p.astype(BF16), v) * (1.0 / l))
            ls.append(m + jnp.log(l))
        o_ref[place] = jnp.where(first, os_[0], os_[1]).astype(BF16)
        lse_ref[place] = jnp.where(first, ls[1], ls[0])
        return 0

    lax.fori_loop(0, rows // bq, block, 0)


def attend_forward(length, q, k, v, bq=512):
    rows, width = q.shape
    spec = pl.BlockSpec((rows, 128), lambda i: (0, i))
    return pl.pallas_call(
        functools.partial(forward_pair, bq, lambda i, n: None),
        grid=(width // 128,),
        in_specs=[SMALL, spec, spec, spec],
        out_specs=[spec, spec],
        out_shape=[S((rows, width), BF16), S((rows, width), F32)],
        compiler_params=pltpu.CompilerParams(vmem_limit_bytes=56 << 20),
        name="attend_forward",
    )(length, q, k, v)


def run(plans, events):
    for name, stage in events:
        plans[name][stage]()


def front(length, hidden, shards, vec, bq=512):
    n = len(shards)
    rows, width = 2 * hidden.shape[1], hidden.shape[2]
    half, pairs = width // 2, width // 128
    items = [(name, w, shards[w].shape[1] // parts * i, shards[w].shape[1] // parts, order) for name, (w, i, parts, order) in FRONT_ITEMS.items()]

    def kernel(*refs):
        len_ref, pair_ref, given, vec_ref = refs[0], refs[1], refs[2 : 2 + n], refs[2 + n]
        refs = refs[3 + n :]
        o_ref, lse_ref, outs, far_outs, mixed = refs[0], refs[1], refs[2:6], refs[6 : 3 + n], refs[3 + n]
        refs = refs[4 + n :]
        rows_s, q_s, k_s, v_s, near, mix_s, (send, recv, out_sem), sems = refs[0], refs[1], refs[2], refs[3], refs[4:7], refs[7], refs[8:11], refs[11:]
        step = pl.program_id(0)
        place = Place()
        fulls = list(near) + list(far_outs)
        local = rows // 2
        keep = pltpu.make_async_copy(pair_ref.at[place.t], rows_s.at[pl.ds(0, local)], out_sem.at[4])
        plans = {
            f"h{i}": plan
            for i, plan in enumerate(swap(pair_ref.at[1 - place.t], rows_s.at[pl.ds(local, local)], send, recv, place.beside))
        }
        for i, (name, w, at, count, order) in enumerate(items):
            plans[name] = gather_stages(place, order, given[w], fulls[w], at, count, *sems[3 * i : 3 * i + 3])
        stores = [pltpu.make_async_copy(src, dst, out_sem.at[i]) for i, (src, dst) in enumerate(zip((rows_s, q_s, k_s, v_s), outs))]
        stores.append(pltpu.make_async_copy(mix_s, mixed, out_sem.at[5]))

        def turn(i):
            for t in range(2):
                w = near[i][t].reshape(width, half).T
                for j in range(pairs // 2):
                    mix_s[j, t, i * 128 : (i + 1) * 128] = w[j * 128 : (j + 1) * 128]

        def project(full, dst, bias, scale):
            def block(i, _):
                r = pl.ds(pl.multiple_of(i * 256, 256), 256)
                for t in range(2):
                    v = nn(rows_s[r], full[t].reshape(width, half))
                    if bias is not None:
                        v = v + bias[:, t * half : (t + 1) * half]
                    dst[r, t * half : (t + 1) * half] = (v * scale).astype(BF16)
                return 0
            lax.fori_loop(0, rows // 256, block, 0)

        @pl.when(step == 0)
        def _():
            keep.start()
            place.greet()
            run(plans, FRONT_ORDER[0])
            keep.wait()
            project(near[0], q_s, vec_ref[6:7], 0.125)
            run(plans, FRONT_ORDER[1])
            project(near[1], k_s, None, 1.0)
            run(plans, FRONT_ORDER[2])
            project(near[2], v_s, vec_ref[7:8], 1.0)
            for i in range(3):
                turn(i)
            for store in stores:
                store.start()

        def hook(block, blocks):
            for i in range(pairs):
                for part in range(2):
                    if FRONT_ORDER[3 + 2 * i + part]:
                        @pl.when((step == 1 + i) & (block == part * (blocks // 2)))
                        def _():
                            run(plans, FRONT_ORDER[3 + 2 * i + part])

        @pl.when(step > 0)
        def _():
            cols = pl.ds(pl.multiple_of((step - 1) * 128, 128), 128)
            forward_pair(bq, hook, len_ref, q_s.at[:, cols], k_s.at[:, cols], v_s.at[:, cols], o_ref, lse_ref)

        @pl.when(step == pairs)
        def _():
            run(plans, FRONT_ORDER[3 + 2 * pairs])
            for store in stores:
                store.wait()

    spec = pl.BlockSpec((rows, 128), lambda i: (0, jnp.maximum(i - 1, 0)))
    flat = S((rows, width), BF16)
    full = [S((2, 4, 2, 2) + s.shape, BF16) for s in shards]
    V = pltpu.VMEM
    return pl.pallas_call(
        kernel,
        grid=(1 + pairs,),
        in_specs=[SMALL, HBM] + [HBM] * n + [whole(vec.shape)],
        out_specs=[spec, spec] + [HBM] * (2 + n),
        out_shape=[flat, S((rows, width), F32), flat, flat, flat, flat] + full[3:] + [S((pairs // 2, 2, half, width), BF16)],
        scratch_shapes=[V((rows, width), BF16)] * 4 + [V(f.shape, BF16) for f in full[:3]] + [V((pairs // 2, 2, half, width), BF16), DMA((4,)), DMA((4,)), DMA((6,))]
        + [s for _ in items for s in (DMA((7,)), DMA((7,)), DMA)],
        cost_estimate=pl.CostEstimate(flops=10 * rows * rows * width, bytes_accessed=40 << 20, transcendentals=rows * rows * 12),
        compiler_params=pltpu.CompilerParams(collective_id=1, has_side_effects=True, vmem_limit_bytes=56 << 20),
        name="front",
    )(length, hidden, *shards, vec)


def backward_pair(bk, hook, len_ref, q_ref, k_ref, v_ref, d_ref, o_ref, lse_ref, dq_ref, dk_ref, dv_ref, qa_s, ka_s, va_s, da_s, acc):
    rows = q_ref.shape[0]
    lane = lax.broadcasted_iota(jnp.int32, (1, 128), 1)
    kbias = jnp.where(live_rows(len_ref, rows), 0.0, -1e9)
    d = d_ref[...].astype(F32)
    prod = d * o_ref[...].astype(F32)
    hi, mid, lo = split3(-lse_ref[...])
    for h in range(2):
        own = lane // DH == h
        sp = DH * (1 - h)
        def pick(a, b, c, e):
            return jnp.where(lane == sp, a, jnp.where(lane == sp + 1, b, jnp.where(lane == sp + 2, c, jnp.where(lane == sp + 3, e, 0.0))))
        dh, dm, dl = split3(-jnp.sum(jnp.where(own, prod, 0.0), axis=1, keepdims=True))
        qa_s[h] = jnp.where(own, q_ref[...].astype(F32), pick(hi, mid, lo, 1.0)).astype(BF16)
        ka_s[h] = jnp.where(own, k_ref[...].astype(F32), pick(1.0, 1.0, 1.0, kbias)).astype(BF16)
        da_s[h] = jnp.where(own, d, pick(dh, dm, dl, 0.0)).astype(BF16)
        va_s[h] = jnp.where(own, v_ref[...].astype(F32), pick(1.0, 1.0, 1.0, 0.0)).astype(BF16)
    first = lane < DH
    upper = lax.broadcasted_iota(jnp.int32, (128, 1), 0) < DH
    acc[...] = jnp.zeros_like(acc)

    def block(b, _):
        hook(b, rows // bk)
        r = pl.ds(b * bk, bk)
        dks, dvs, dqs = [], [], []
        for h in range(2):
            p = jnp.exp(nt(ka_s[h, r], qa_s[h]))
            ds = (p * nt(va_s[h, r], da_s[h])).astype(BF16)
            dvs.append(nn(p.astype(BF16), d_ref[...]))
            dks.append(nn(ds, q_ref[...]))
            dqs.append(tn(k_ref[r], ds))
        dk_ref[r] = jnp.where(first, dks[0], dks[1]).astype(BF16)
        dv_ref[r] = jnp.where(first, dvs[0], dvs[1]).astype(BF16)
        acc[...] += jnp.where(upper, dqs[0], dqs[1])
        return 0

    for b in range(rows // bk):
        block(b, 0)
    dq_ref[...] = (acc[...].T * 0.125).astype(BF16)


def pair_scratch(rows):
    aug = pltpu.VMEM((2, rows, 128), BF16)
    return [aug, aug, aug, aug, pltpu.VMEM((128, rows), F32)]


def attend_backward(length, q, k, v, d, o, lse, bk=512):
    rows, width = q.shape
    spec = pl.BlockSpec((rows, 128), lambda i: (0, i))
    return pl.pallas_call(
        functools.partial(backward_pair, bk, lambda i, n: None),
        grid=(width // 128,),
        in_specs=[SMALL] + [spec] * 6,
        out_specs=[spec] * 3,
        out_shape=[S((rows, width), BF16)] * 3,
        scratch_shapes=pair_scratch(rows),
        compiler_params=pltpu.CompilerParams(vmem_limit_bytes=56 << 20),
        name="attend_backward",
    )(length, q, k, v, d, o, lse)


def back(length, q, k, v, d, o, lse, rows_in, mixed, grad_one, small, grads, bk=512):
    n = len(grads)
    rows, width = q.shape
    half, pairs = width // 2, width // 128
    pieces = pairs // 2
    shards = [(grads[0].shape[4], half)] * pieces + [g.shape[4:] for g in grads]
    items = []
    for name, (w, i, parts, order) in BACK_ITEMS.items():
        items.append((name, w, shards[w][1] // parts * i, shards[w][1] // parts, order))
    vb = small.shape[0] - 4

    def kernel(*refs):
        main_in, rows_ref, mixed_ref, one_ref, small_ref, given = refs[:7], refs[7], refs[8], refs[9], refs[10], refs[11 : 11 + n]
        refs = refs[11 + n :]
        pair_ref, sum_ref, outs = refs[0], refs[1], refs[2 : 2 + pieces + n]
        refs = refs[2 + pieces + n :]
        cat, rT, total, gr_s, own = refs[:5]
        refs = refs[5:]
        part, got, fold_send, fold_recv, send, recv, local_sem = refs[:7]
        main_scratch, scratch = refs[7:12], refs[12:]
        step = pl.program_id(0)
        place = Place()
        local = rows // 2
        keep = pltpu.make_async_copy(gr_s.at[pl.ds(0, local)], pair_ref.at[place.t], local_sem)
        plans = {
            f"r{i}": plan
            for i, plan in enumerate(swap(gr_s.at[pl.ds(local, local)], pair_ref.at[place.t], send, recv, place.beside))
        }
        plans["sm"] = fold_stages(place, part, got, fold_send, fold_recv)
        sources = [own.at[p] for p in range(pieces)] + list(given)
        for i, (name, w, at, count, order) in enumerate(items):
            plans[name] = reduce_stages(place, order, sources[w], at, count, outs[w], scratch[9 * i : 9 * i + 9])

        @pl.when(step == 0)
        def _():
            place.greet()
            part[...] = small_ref[...]
            total[...] = one_ref[...]
            rT[...] = rows_ref[...].T

        def at(i, j):
            return 2 * i + j + i // 2

        def hook(block, blocks):
            for i in range(pairs):
                for j in range(2):
                    if BACK_ORDER[at(i, j)]:
                        if block == j * (blocks // 2):
                            @pl.when(step == i)
                            def _():
                                run(plans, BACK_ORDER[at(i, j)])

        t = step % 2
        backward_pair(bk, hook, *main_in, cat.at[t, :, pl.ds(0, 128)], cat.at[t, :, pl.ds(128, 128)], cat.at[t, :, pl.ds(256, 128)], *main_scratch)

        def gather_rows(p, first):
            r = slice(first, first + local)
            v = total[r] + (nn(cat[0, r], mixed_ref[p, 0]) + nn(cat[1, r], mixed_ref[p, 1]))
            total[r] = v
            gr_s[r] = v.astype(BF16)

        @pl.when(step % 2 == 1)
        def _():
            p = step // 2
            last = step == pairs - 1
            gather_rows(p, local)

            @pl.when(last)
            def _():
                run(plans, BACK_ORDER[-3])

            def weigh(t, _):
                own[p, t] = nn(rT[...], cat[t]).astype(BF16).reshape(own.shape[2:])
                sums = colsum(cat[t].astype(F32))
                lanes = pl.ds(pl.multiple_of(t * half + p * 128, 128), 128)
                part[vb : vb + 1, lanes] = sums[:, :128]
                part[vb + 1 : vb + 2, lanes] = sums[:, 256:]
                return 0
            weigh(0, 0)
            weigh(1, 0)
            for i in range(pieces - 1):
                @pl.when(step == 2 * i + 1)
                def _():
                    run(plans, BACK_ORDER[at(2 * i + 1, 2)])

            @pl.when(last)
            def _():
                run(plans, BACK_ORDER[-2])
            gather_rows(p, 0)

        @pl.when(step == pairs - 1)
        def _():
            keep.start()
            run(plans, BACK_ORDER[-1])
            sum_ref[...] = part[...]
            keep.wait()

    spec = pl.BlockSpec((rows, 128), lambda i: (0, i % 2 * (pairs // 2) + i // 2))
    V = pltpu.VMEM
    outs = [S(s, F32) for s in shards]
    return pl.pallas_call(
        kernel,
        grid=(pairs,),
        in_specs=[SMALL] + [spec] * 6 + [whole((rows, width)), whole(mixed.shape), whole((rows, width)), whole(small.shape)] + [HBM] * n,
        out_specs=[HBM, whole(small.shape)] + [whole(s) for s in shards],
        out_shape=[S((2, rows // 2, width), BF16), S(small.shape, F32)] + outs,
        scratch_shapes=[V((2, rows, half), BF16), V((width, rows), BF16), V((rows, width), F32), V((rows, width), BF16)]
        + [V((pieces, 2, 4, 2, 2) + shards[0], BF16)]
        + [V(small.shape, F32), V((5,) + small.shape, F32), DMA((5,)), DMA((5,)), DMA((4,)), DMA((4,)), DMA]
        + pair_scratch(rows)
        + [s for _, w, f, c, o in items for s in reduce_scratch(o, shards[w][0], c)],
        cost_estimate=pl.CostEstimate(flops=20 * rows * rows * width, bytes_accessed=60 << 20, transcendentals=rows * rows * 12),
        compiler_params=pltpu.CompilerParams(collective_id=2, has_side_effects=True, vmem_limit_bytes=63 << 20),
        name="back",
    )(length, q, k, v, d, o, lse, rows_in, mixed, grad_one, small, *grads)


def finish(near_out, came_out, grad_hidden, owned):
    local, width = near_out.shape
    pieces = 3

    def kernel(*refs):
        near_ref, came_ref, grad_ref = refs[:3]
        given, (out_ref, hid_ref), outs, sem = refs[3:9], refs[9:11], refs[11:17], refs[17]
        t = lax.axis_index("tensor")
        moves = [(near_ref, out_ref.at[t]), (came_ref, out_ref.at[1 - t]), (grad_ref, hid_ref)]
        moves += list(zip(given[pieces:], outs[3:]))
        for i in range(3):
            for p in range(pieces):
                moves.append((given[p].at[:, pl.ds(i * 128, 128)], outs[i].at[:, pl.ds(p * 128, 128)]))
        copies = [pltpu.make_async_copy(a, b, sem.at[i]) for i, (a, b) in enumerate(moves)]
        for copy in copies:
            copy.start()
        for copy in copies:
            copy.wait()

    return pl.pallas_call(
        kernel,
        in_specs=[pl.BlockSpec(memory_space=pltpu.VMEM)] * 9,
        out_specs=[HBM] * 8,
        out_shape=[S((2, local, width), BF16)] * 2 + [S(o.shape, F32) for o in owned],
        scratch_shapes=[DMA((15,))],
        name="finish",
    )(near_out, came_out, grad_hidden, *owned)


def norm_parts(v):
    c = v - jnp.mean(v, axis=-1, keepdims=True)
    r = lax.rsqrt(jnp.mean(c * c, axis=-1, keepdims=True) + 1e-5)
    return c * r, r


def norm_back(n, r, dyg):
    return r * (dyg - jnp.mean(dyg, axis=-1, keepdims=True) - n * jnp.mean(dyg * n, axis=-1, keepdims=True))


def colsum(v):
    return jnp.sum(v, axis=0, keepdims=True)


def mlp_up_kernel(chunk, a_ref, h_ref, wo_ref, wi_ref, wb_ref, vec_ref, bi_ref, near_ref, far_ref, mid_ref, v1_ref, v2_ref, act, gp, b2):
    half, inner = wo_ref.shape[2], wi_ref.shape[2]
    b_out, b_back, gain_one, shift_one, gain_two, shift_two = [vec_ref[i : i + 1] for i in range(6)]
    v1 = h_ref[...].astype(F32) + (nt(a_ref[:, :half], wo_ref[0]) + nt(a_ref[:, half:], wo_ref[1])) + b_out
    v1_ref[...] = v1
    n1, r1 = norm_parts(v1)
    normed = n1 * gain_one + shift_one
    mid = normed.astype(BF16)
    mid_ref[...] = mid
    b2[...] = normed + b_back

    def up(i, _):
        t = i // (inner // chunk)
        cols = pl.ds(pl.multiple_of(i % (inner // chunk) * chunk, chunk), chunk)
        hp = nn(mid, wi_ref[t, :, cols]) + bi_ref[t, :, cols]
        half_up = 0.5 + 0.5 * lax.erf(hp * math.sqrt(0.5))
        a = (hp * half_up).astype(BF16)
        act[t, :, cols] = a
        gp[t, :, cols] = (half_up + hp * (jnp.exp(hp * hp * -0.5) * (1.0 / math.sqrt(2 * math.pi)))).astype(BF16)
        b2[...] += nt(a, wb_ref[t, :, cols])
        return 0

    lax.fori_loop(0, 2 * inner // chunk, up, 0)
    v2_ref[...] = b2[...]
    n2, r2 = norm_parts(b2[...])
    out = (n2 * gain_two + shift_two).astype(BF16)
    step, steps = pl.program_id(0), pl.num_programs(0)

    @pl.when(step < steps // 2)
    def _():
        near_ref[...] = out

    @pl.when(step >= steps // 2)
    def _():
        far_ref[...] = out


def mlp_up(a, h, wo, wi, wb, vec, bi, rows=256, chunk=1536):
    total, width = a.shape
    inner = wi.shape[2]
    row = pl.BlockSpec((rows, width), lambda i: (i, 0))
    wide = pl.BlockSpec((2, rows, inner), lambda i: (0, i, 0))
    return pl.pallas_call(
        functools.partial(mlp_up_kernel, chunk),
        grid=(total // rows,),
        in_specs=[row, row] + [whole(s.shape) for s in (wo, wi, wb, vec, bi)],
        out_specs=[
            pl.BlockSpec((rows, width), lambda i: (jnp.minimum(i, total // rows // 2 - 1), 0)),
            pl.BlockSpec((rows, width), lambda i: (jnp.maximum(i - total // rows // 2, 0), 0)),
            row, row, row, wide, wide,
        ],
        out_shape=[S((total // 2, width), BF16), S((total // 2, width), BF16), S((total, width), BF16), S((total, width), F32), S((total, width), F32), S((2, total, inner), BF16), S((2, total, inner), BF16)],
        scratch_shapes=[pltpu.VMEM((rows, width), F32)],
        cost_estimate=pl.CostEstimate(flops=total * width * (8 * inner + 2 * width), bytes_accessed=40 << 20, transcendentals=4 * total * inner),
        compiler_params=pltpu.CompilerParams(vmem_limit_bytes=60 << 20),
        name="mlp_up",
    )(a, h, wo, wi, wb, vec, bi)


def mlp_down_kernel(len_ref, a_ref, mid_ref, cot_ref, far_ref, v1_ref, v2_ref, wo_ref, vec_ref, wi_ref, wb_ref, act_ref, gp_ref,
                    g1_ref, ga_ref, gwo_ref, gwi_ref, gwb_ref, small_ref, back, btT, midT, gn, sums_s):
    step = pl.program_id(0)
    rows, half, chunk, block = a_ref.shape[0], wo_ref.shape[2], wi_ref.shape[2], 256
    width = a_ref.shape[1]
    b_out, b_back, gain_one, shift_one, gain_two, shift_two = [vec_ref[i : i + 1] for i in range(6)]

    @pl.when(step == 0)
    def _():
        small_ref[...] = jnp.zeros_like(small_ref)
        midT[...] = mid_ref[...].T
        live = jnp.where(live_rows(len_ref, rows), 1.0, 0.0)
        near = cot_ref.at[lax.axis_index("tensor")]
        for b in range(rows // block):
            r = slice(b * block, (b + 1) * block)
            n2, r2 = norm_parts(v2_ref[r])
            at = (b * block) % (rows // 2)
            go = (near if b < rows // block // 2 else far_ref)[at : at + block].astype(F32) * live[r]
            grad_two = norm_back(n2, r2, go * gain_two)
            bt = grad_two.astype(BF16)
            back[r] = bt
            btT[:, r] = bt.T
            gn[r] = grad_two
            small_ref[1:2] += colsum(grad_two)
            small_ref[4:5] += colsum(go * n2)
            small_ref[5:6] += colsum(go)

    gb = (nn(back[...], wb_ref[0]) * gp_ref[0].astype(F32)).astype(BF16)
    sums = colsum(gb.astype(F32))
    gwb_ref[0] = nn(btT[...], act_ref[0]).astype(BF16)
    gwi_ref[0] = nn(midT[...], gb).astype(BF16)
    gn[...] += nt(gb, wi_ref[0])
    sums_s[...] = sums
    for j in range(half * 8 // chunk):
        @pl.when(step == j)
        def _():
            for at in range(j * chunk, (j + 1) * chunk, 128):
                small_ref[8 + at // width : 9 + at // width, at % width : at % width + 128] = sums_s[:, at - j * chunk : at - j * chunk + 128]

    @pl.when(step == pl.num_programs(0) - 1)
    def _():
        for b in range(rows // block):
            r = slice(b * block, (b + 1) * block)
            g = gn[r]
            n1, r1 = norm_parts(v1_ref[r])
            grad_one = norm_back(n1, r1, g * gain_one)
            bo = grad_one.astype(BF16)
            back[r] = bo
            g1_ref[r] = grad_one
            small_ref[0:1] += colsum(grad_one)
            small_ref[2:3] += colsum(g * n1)
            small_ref[3:4] += colsum(g)
            for t in range(2):
                ga_ref[r, t * half : (t + 1) * half] = nn(bo, wo_ref[t]).astype(BF16)
        btT[...] = back[...].T
        for t in range(2):
            gwo_ref[t] = nn(btT[...], a_ref[:, t * half : (t + 1) * half]).astype(BF16)


def mlp_down(length, a, mid, cot, far, v1, v2, wo, wi, wb, act, gp, vec, chunk=512):
    rows, width = a.shape
    inner = wi.shape[2]
    m = inner // chunk
    tall = pl.BlockSpec((1, rows, chunk), lambda i: (i // m, 0, i % m))
    weight = pl.BlockSpec((1, width, chunk), lambda i: (i // m, 0, i % m))
    V = pltpu.VMEM
    small = (12 + 2 * inner // width, width)
    return pl.pallas_call(
        mlp_down_kernel,
        grid=(2 * m,),
        in_specs=[SMALL] + [whole(s.shape) for s in (a, mid, cot, far, v1, v2, wo, vec)] + [weight, weight, tall, tall],
        out_specs=[whole((rows, width)), whole((rows, width)), whole(wo.shape), weight, weight, whole(small)],
        out_shape=[S((rows, width), F32), S((rows, width), BF16), S(wo.shape, BF16), S(wi.shape, BF16), S(wb.shape, BF16), S(small, F32)],
        scratch_shapes=[V((rows, width), BF16), V((width, rows), BF16), V((width, rows), BF16), V((rows, width), F32), V((1, chunk), F32)],
        cost_estimate=pl.CostEstimate(flops=rows * width * (16 * inner + 4 * width), bytes_accessed=60 << 20, transcendentals=0),
        compiler_params=pltpu.CompilerParams(vmem_limit_bytes=62 << 20),
        name="mlp_down",
    )(length, a, mid, cot, far, v1, v2, wo, vec, wi, wb, act, gp)


def per_device(
    hidden, lengths, cotangent, w_query, w_key, w_value, w_out, w_in, w_back,
    b_query, b_value, b_out, b_in, b_back, gain_one, shift_one, gain_two, shift_two,
):
    t = lax.axis_index("tensor")
    local = hidden.shape[1]
    width = b_query.shape[0]
    inner = b_in.shape[0]
    own_kernels = lax.axis_size("dp") == 16 and lax.axis_size("tensor") == 2
    flip = [(0, 1), (1, 0)]

    def mine(a):
        return lax.dynamic_index_in_dim(a, t, 0, keepdims=False)

    def take(a):
        other = lax.dynamic_index_in_dim(a, 1 - t, 0, keepdims=False)
        return jnp.concatenate([mine(a), lax.ppermute(other, "tensor", flip)], 0)

    def give(a):
        got = lax.ppermute(a[local:], "tensor", flip)
        first = t == 0
        return jnp.stack([jnp.where(first, a[:local], got), jnp.where(first, got, a[:local])], 0)

    def gather(w):
        return lax.all_gather(lax.all_gather(w, "dp", axis=0, tiled=True), "tensor", axis=0)

    def scatter(g):
        g = lax.psum_scatter(g, "dp", scatter_dimension=1, tiled=True)
        return lax.psum_scatter(g, "tensor", scatter_dimension=0, tiled=False).astype(F32)

    def flat(w):
        return w.reshape(2, width, -1)

    vec = jnp.stack([b_out, b_back, gain_one, shift_one, gain_two, shift_two, b_query, b_value])
    shards = (w_query, w_key, w_value, w_out, w_in, w_back)
    if own_kernels:
        attended, lse, rows, query, key, value, full_out, full_in, full_back, mixed = front(lengths, hidden, shards, vec)
        full_out, full_in, full_back = flat(full_out), flat(full_in), flat(full_back)
        late_cotangent = lax.optimization_barrier((cotangent, attended))[0]
    else:
        late_cotangent = cotangent
        rows = take(hidden)
        full_query, full_key, full_value, full_out, full_in, full_back = [gather(w) for w in shards]

        def project(w):
            return jnp.concatenate([nn(rows, w[0]), nn(rows, w[1])], 1)

        query = ((project(full_query) + b_query) * 0.125).astype(BF16)
        key = project(full_key).astype(BF16)
        value = (project(full_value) + b_value).astype(BF16)
        attended, lse = attend_forward(lengths, query, key, value)
    bi = b_in.reshape(2, 1, inner // 2)
    far_cot = lax.ppermute(lax.dynamic_index_in_dim(late_cotangent, 1 - t, 0, keepdims=False), "tensor", flip)
    near_out, far_out, mid, v1, v2, act, gp = mlp_up(attended, rows, full_out, full_in, full_back, vec, bi)
    came_out = lax.ppermute(far_out, "tensor", flip)
    grad_one, grad_attended, g_out, g_in, g_back, small = mlp_down(
        lengths, attended, mid, cotangent, far_cot, v1, v2, full_out, full_in, full_back, act, gp, vec
    )
    def split(g):
        return g.reshape(2, 4, 2, 2, -1, g.shape[-1])
    vb = 8 + inner // width
    if own_kernels:
        grad_hidden, small, *owned = back(
            lengths, query, key, value, grad_attended, attended, lse, rows, mixed, grad_one, small, [split(g) for g in (g_out, g_in, g_back)]
        )
        output, grad_hidden, *owned = finish(near_out, came_out, grad_hidden, owned)
    else:
        d_query, d_key, d_value = attend_backward(lengths, query, key, value, grad_attended, attended, lse)
        total = grad_one
        grads = []
        for d, w in ((d_query, full_query), (d_key, full_key), (d_value, full_value)):
            total = total + nt(d, jnp.concatenate([w[0], w[1]], 1))
            g = tn(rows, d).astype(BF16)
            grads.append(jnp.stack([g[:, : width // 2], g[:, width // 2 :]]))
        small = small.at[vb].set(jnp.sum(d_query.astype(F32), 0)).at[vb + 1].set(jnp.sum(d_value.astype(F32), 0))
        first = t == 0
        output = jnp.stack([jnp.where(first, near_out, came_out), jnp.where(first, came_out, near_out)], 0)
        grad_hidden = give(total.astype(BF16))
        owned = [scatter(g) for g in grads + [g_out, g_in, g_back]]
        small = lax.psum(small, ("dp", "tensor"))
    return (
        output, grad_hidden, *owned,
        small[vb], small[vb + 1], small[0], small[8:vb].reshape(inner), small[1], small[2], small[3], small[4], small[5],
    )


def solution(mesh):
    rows = P(None, ("dp", "tensor"), None)
    weight = P("dp", "tensor")
    return jax.shard_map(
        per_device,
        mesh=mesh,
        in_specs=(rows, P(None, "dp"), rows) + (weight,) * 6 + (P(),) * 9,
        out_specs=(rows, rows) + (weight,) * 6 + (P(),) * 9,
        check_vma=False,
    )
```

```python
import functools
import math

import jax
import jax.numpy as jnp
from jax import lax
from jax.experimental import pallas as pl
from jax.experimental.pallas import tpu as pltpu
from jax.sharding import PartitionSpec as P

F32, BF16 = jnp.float32, jnp.bfloat16
DH = 64
S = jax.ShapeDtypeStruct
HBM = pl.BlockSpec(memory_space=pl.ANY)
LENGTHS = pl.BlockSpec(memory_space=pltpu.VMEM)
DMA = pltpu.SemaphoreType.DMA


def nt(a, b):
    return lax.dot_general(a, b, (((1,), (1,)), ((), ())), preferred_element_type=F32)


def nn(a, b):
    return lax.dot_general(a, b, (((1,), (0,)), ((), ())), preferred_element_type=F32)


def tn(a, b):
    return lax.dot_general(a, b, (((0,), (0,)), ((), ())), preferred_element_type=F32)


def split3(v):
    hi = v.astype(BF16).astype(F32)
    rest = v - hi
    mid = rest.astype(BF16).astype(F32)
    return hi, mid, rest - mid


class Place:
    def __init__(self):
        dp, t = lax.axis_index("dp"), lax.axis_index("tensor")
        z, x, c = dp // 4, (dp // 2) % 2, dp % 2
        self.z, self.x, self.c, self.t = z, x, c, t
        self.above, self.below, self.far = (z + 1) % 4, (z + 3) % 4, (z + 2) % 4
        at = lambda z, x, c, t: ((z * 2 + x) * 2 + c, t)
        self.up, self.down = at(self.above, x, c, t), at(self.below, x, c, t)
        self.across, self.beside, self.twin = at(z, 1 - x, c, t), at(z, x, c, 1 - t), at(z, x, 1 - c, t)
        self.corner, self.opposite = at(z, 1 - x, c, 1 - t), at(self.far, x, c, t)
        self.near = (self.up, self.down, self.across, self.beside, self.twin)

    def greet(self, peers):
        barrier = pltpu.get_barrier_semaphore()
        for peer in peers:
            pl.semaphore_signal(barrier, inc=1, device_id=peer, device_id_type=pl.DeviceIdType.MESH)
        pl.semaphore_wait(barrier, len(peers))


def remote(src, dst, send, recv, peer):
    return pltpu.make_async_remote_copy(src, dst, send, recv, device_id=peer, device_id_type=pl.DeviceIdType.MESH)


def gather_stages(place, order, shard, full, first, count, send, recv, local):
    z, x, c, t = place.z, place.x, place.c, place.t
    lanes = pl.ds(first, count)
    part = count // 256 * 128
    low, high = pl.ds(first, part), pl.ds(first + part, count - part)
    own = full.at[t, z, x, c, :, lanes]
    here = shard.at[:, lanes]
    def move(i, view, peer, src=None):
        return remote(view if src is None else src, view, send.at[i], recv.at[i], peer)
    keep = pltpu.make_async_copy(here, own, local)
    everything = move(6, full.at[:, :, :, c, :, lanes], place.twin)
    if order[0] == "z":
        first_up, first_down = move(0, own, place.up, here), move(1, own, place.down, here)
        next_up = move(2, full.at[t, place.below, x, c, :, low], place.up)
        next_down = move(3, full.at[t, place.above, x, c, :, high], place.down)
        if order == "zxy":
            four, five = move(4, full.at[t, :, x, c, :, lanes], place.across), move(5, full.at[t, :, :, c, :, lanes], place.beside)
        else:
            four, five = move(4, full.at[t, :, x, c, :, lanes], place.beside), move(5, full.at[:, :, x, c, :, lanes], place.across)
        copies = [first_up, first_down, next_up, next_down, four, five, everything]
        def s0(): keep.start(); first_up.start(); first_down.start()
        def s1(): first_up.wait_recv(); next_up.start(); first_down.wait_recv(); next_down.start()
        def s2(): next_up.wait_recv(); next_down.wait_recv(); keep.wait(); four.start()
        def s3(): four.wait_recv(); five.start()
        def s4(): five.wait_recv(); everything.start()
    else:
        if order == "xyz":
            one, two = move(0, own, place.across, here), move(1, full.at[t, z, :, c, :, lanes], place.beside)
        else:
            one, two = move(0, own, place.beside, here), move(1, full.at[:, z, x, c, :, lanes], place.across)
        first_up, first_down = move(2, full.at[:, z, :, c, :, lanes], place.up), move(3, full.at[:, z, :, c, :, lanes], place.down)
        next_up = move(4, full.at[0, place.below, :, c, :, lanes], place.up)
        next_down = move(5, full.at[1, place.above, :, c, :, lanes], place.down)
        copies = [one, two, first_up, first_down, next_up, next_down, everything]
        def s0(): keep.start(); one.start()
        def s1(): one.wait_recv(); keep.wait(); two.start()
        def s2(): two.wait_recv(); first_up.start(); first_down.start()
        def s3(): first_up.wait_recv(); next_up.start(); first_down.wait_recv(); next_down.start()
        def s4(): next_up.wait_recv(); next_down.wait_recv(); everything.start()
    def s5():
        everything.wait_recv()
        for copy in copies: copy.wait_send()
    return [s0, s1, s2, s3, s4, s5]


def add_blocks(count, dst, *srcs):
    def body(i, _):
        ref = dst(i)
        total = ref[...].astype(F32)
        for s in srcs: total = total + s(i)[...].astype(F32)
        ref[...] = total.astype(ref.dtype)
        return 0
    lax.fori_loop(0, count, body, 0)


def reduce_scratch(order, rows, lanes):
    V = lambda *s: pltpu.VMEM(s + (rows, lanes), BF16)
    base = [V(2, 4, 2), V(2, 4, 2)]
    if order == "wide": base += [V(3, 4), V(3), V(), V()]
    elif order == "yxz": base += [V(4, 2), V(4), V(), V(2)]
    elif order == "xyz": base += [V(2, 4), V(4), V(), V(2)]
    else: base += [V(2, 2), V(2, 2, 2), V(2), V()]
    return base + [pltpu.SemaphoreType.DMA((7,)), pltpu.SemaphoreType.DMA((7,)), pltpu.SemaphoreType.DMA]


def wide_stages(place, load, c0, held, r0, r1, r2, out, lanes, move):
    z, x, t = place.z, place.x, place.t
    flat = [
        move(1, held.at[t, :, 1 - x], r1.at[0], place.across),
        move(2, held.at[1 - t, :, x], r1.at[1], place.beside),
        move(3, held.at[1 - t, :, 1 - x], r1.at[2], place.corner),
    ]
    tall = [
        move(4, held.at[t, place.above, x], r2.at[0], place.up),
        move(5, held.at[t, place.below, x], r2.at[1], place.down),
        move(6, held.at[t, place.far, x], r2.at[2], place.opposite),
    ]
    def block(ref): return lambda i: ref.at[i // 8, (i // 2) % 4, i % 2]
    def s0(): load.start(); c0.start()
    def s1():
        load.wait(); c0.wait_recv(); add_blocks(16, block(held), block(r0))
        for copy in flat: copy.start()
    def s2():
        for copy in flat: copy.wait_recv()
        add_blocks(4, lambda k: held.at[t, k, x], *[lambda k, i=i: r1.at[i, k] for i in range(3)])
        for copy in tall: copy.start()
    def s3():
        for copy in tall: copy.wait_recv()
        out[:, lanes] = (held[t, z, x].astype(F32) + r2[2].astype(F32)) + (r2[0].astype(F32) + r2[1].astype(F32))
        for copy in [c0] + flat + tall: copy.wait_send()
    return [s0, s1, s2, s3]


def reduce_stages(place, order, grad, first, count, out, scratch):
    held, r0, r1, r2, r3, r4, send, recv, local = scratch
    z, x, c, t = place.z, place.x, place.c, place.t
    lanes = pl.ds(first, count)
    part = count // 256 * 128
    if part:
        low, high = (slice(None), pl.ds(0, part)), (slice(None), pl.ds(part, count - part))
    else:
        low, high = (pl.ds(0, 16), slice(None)), (pl.ds(16, held.shape[3] - 16), slice(None))
    load = pltpu.make_async_copy(grad.at[:, :, :, c, :, lanes], held, local)
    def move(i, src, dst, peer):
        return remote(src, dst, send.at[i], recv.at[i], peer)
    c0 = move(0, grad.at[:, :, :, 1 - c, :, lanes], r0, place.twin)
    if order == "wide":
        return wide_stages(place, load, c0, held, r0, r1, r2, out, lanes, move)
    at3 = lambda ref: (lambda i: ref.at[i // 8, (i // 2) % 4, i % 2])
    def s0(): load.start(); c0.start()
    if order[0] != "z":
        if order == "yxz":
            c1, c2 = move(1, held.at[1 - t], r1, place.beside), move(2, held.at[t, :, 1 - x], r2, place.across)
            def add1(): add_blocks(8, lambda i: held.at[t, i // 2, i % 2], lambda i: r1.at[i // 2, i % 2])
        else:
            c1, c2 = move(1, held.at[:, :, 1 - x], r1, place.across), move(2, held.at[1 - t, :, x], r2, place.beside)
            def add1(): add_blocks(8, lambda i: held.at[i // 4, i % 4, x], lambda i: r1.at[i // 4, i % 4])
        mine = lambda k: held.at[t, k, x]
        c3 = move(3, held.at[(t, place.far, x) + low], r3.at[low], place.up)
        c4 = move(4, held.at[(t, place.far, x) + high], r3.at[high], place.down)
        c5, c6 = move(5, mine(place.above), r4.at[0], place.up), move(6, mine(place.below), r4.at[1], place.down)
        def s1(): load.wait(); c0.wait_recv(); add_blocks(16, at3(held), at3(r0)); c1.start()
        def s2(): c1.wait_recv(); add1(); c2.start()
        def s3(): c2.wait_recv(); add_blocks(4, mine, lambda k: r2.at[k]); c3.start(); c4.start()
        def s4():
            c3.wait_recv()
            v = held.at[(t, place.above, x) + low]; v[...] = (v[...].astype(F32) + r3[low].astype(F32)).astype(BF16)
            c5.start()
            c4.wait_recv()
            v = held.at[(t, place.below, x) + high]; v[...] = (v[...].astype(F32) + r3[high].astype(F32)).astype(BF16)
            c6.start()
        def s5():
            c5.wait_recv(); c6.wait_recv()
            out[:, lanes] = mine(z)[...].astype(F32) + r4[0].astype(F32) + r4[1].astype(F32)
            for copy in (c0, c1, c2, c3, c4, c5, c6): copy.wait_send()
    else:
        c1, c2 = move(1, held.at[0, place.far], r1.at[0], place.up), move(2, held.at[1, place.far], r1.at[1], place.down)
        c3, c4 = move(3, held.at[:, place.above], r2.at[0], place.up), move(4, held.at[:, place.below], r2.at[1], place.down)
        if order == "zyx":
            c5, c6 = move(5, held.at[1 - t, z], r3, place.beside), move(6, held.at[t, z, 1 - x], r4, place.across)
            def add5(): add_blocks(2, lambda k: held.at[t, z, k], lambda k: r3.at[k])
        else:
            c5, c6 = move(5, held.at[:, z, 1 - x], r3, place.across), move(6, held.at[1 - t, z, x], r4, place.beside)
            def add5(): add_blocks(2, lambda k: held.at[k, z, x], lambda k: r3.at[k])
        def s1(): load.wait(); c0.wait_recv(); add_blocks(16, at3(held), at3(r0)); c1.start(); c2.start()
        def s2():
            c1.wait_recv(); add_blocks(2, lambda k: held.at[0, place.above, k], lambda k: r1.at[0, k]); c3.start()
            c2.wait_recv(); add_blocks(2, lambda k: held.at[1, place.below, k], lambda k: r1.at[1, k]); c4.start()
        def s3():
            c3.wait_recv(); c4.wait_recv()
            add_blocks(4, lambda k: held.at[k // 2, z, k % 2], lambda k: r2.at[0, k // 2, k % 2], lambda k: r2.at[1, k // 2, k % 2])
            c5.start()
        def s4(): c5.wait_recv(); add5(); c6.start()
        def s5():
            c6.wait_recv()
            out[:, lanes] = held[t, z, x].astype(F32) + r4[...].astype(F32)
            for copy in (c0, c1, c2, c3, c4, c5, c6): copy.wait_send()
    return [s0, s1, s2, s3, s4, s5]


FRONT_ITEMS = {
    "q": (0, 0, 1, "zyx"),
    "k": (1, 0, 1, "zyx"),
    "v": (2, 0, 1, "yxz"),
    "o0": (3, 0, 1, "xyz"),
    "i0": (4, 0, 2, "zxy"),
    "i1": (4, 1, 2, "xyz"),
    "b0": (5, 0, 4, "zyx"),
    "b1": (5, 1, 4, "zxy"),
    "b2": (5, 2, 4, "zyx"),
    "b3": (5, 3, 4, "zyx"),
}
BACK_ITEMS = {
    "m0": (0, 0, 1, "xyz"),
    "m1": (1, 0, 1, "yxz"),
    "mq": (2, 0, 3, "zxy"),
    "mk": (2, 1, 3, "zxy"),
    "mv": (2, 2, 3, "yxz"),
    "o0": (3, 0, 1, "zxy"),
    "i0": (4, 0, 2, "zxy"),
    "i1": (4, 1, 2, "xyz"),
    "b0": (5, 0, 2, "yxz"),
    "b1": (5, 1, 2, "xyz"),
}
FRONT_ORDER = (
    (("v", 0), ("q", 0), ("h1", 0), ("k", 0), ("b0", 0), ("v", 1), ("q", 1), ("k", 1), ("v", 2), ("b0", 1), ("i0", 0), ("q", 2), ("k", 2), ("h0", 0), ("i1", 0), ("b1", 0), ("o0", 0), ("h1", 1), ("b2", 0), ("b3", 0), ("q", 3), ("i1", 1), ("v", 3), ("o0", 1), ("b0", 2), ("k", 3), ("i0", 1), ("b1", 1), ("b2", 1), ("q", 4), ("b3", 1), ("h0", 1), ("q", 5),),
    (("v", 4), ("i0", 2), ("i1", 2), ("k", 4), ("b1", 2), ("b2", 2), ("o0", 2), ("b3", 2), ("v", 5), ("k", 5),),
    (),
    (("b0", 3),),
    (("b2", 3), ("i0", 3),),
    (("b1", 3), ("b3", 3),),
    (("i1", 3),),
    (),
    (("b0", 4),),
    (("o0", 3),),
    (("b2", 4), ("b0", 5), ("i0", 4),),
    (("i1", 4),),
    (("b2", 5), ("i0", 5), ("b3", 4), ("o0", 4),),
    (("i1", 5), ("b1", 4),),
    (("o0", 5), ("b3", 5),),
    (("b1", 5),),
)
BACK_ORDER = (
    (("i0", 0), ("i1", 0), ("b1", 0),),
    (("b0", 0),),
    (("i0", 1), ("i1", 1),),
    (("b0", 1), ("b1", 1),),
    (("i0", 2), ("m0", 0),),
    (),
    (("i1", 2), ("m0", 1),),
    (("b0", 2), ("o0", 0),),
    (),
    (("o0", 1), ("i1", 3), ("i0", 3), ("b1", 2), ("m1", 0),),
    (),
    (("o0", 2), ("m1", 1), ("m0", 2),),
    (("b0", 3), ("i1", 4), ("b1", 3),),
    (("i0", 4),),
    (("b0", 4), ("r2", 0), ("o0", 3), ("i1", 5), ("m1", 2), ("m0", 3),),
    (("mv", 0), ("i0", 5), ("b1", 4), ("mq", 0), ("mk", 0), ("o0", 4),),
    (("b0", 5), ("m0", 4), ("mv", 1), ("r2", 1), ("sm", 0), ("mq", 1), ("mk", 1), ("m1", 3), ("r0", 0), ("o0", 5), ("b1", 5), ("sm", 1), ("m0", 5), ("mv", 2), ("mq", 2), ("r1", 0), ("r3", 0), ("mk", 2), ("m1", 4), ("r0", 1), ("mv", 3), ("mq", 3), ("sm", 2), ("mk", 3), ("mq", 4), ("m1", 5), ("mv", 4), ("r1", 1), ("mk", 4), ("sm", 3), ("mv", 5), ("r3", 1), ("mq", 5), ("mk", 5),),
)


def fold_stages(place, part, got, send, recv):
    peers = (place.twin, place.across, place.beside, place.corner, place.up, place.down, place.opposite)
    copies = [remote(part, got.at[i], send.at[i], recv.at[i], peer) for i, peer in enumerate(peers)]
    def hop(first, last, old):
        for copy in copies[old:first]: copy.wait()
        if first == 1: part[...] = part[...] + got[0]
        elif first == 4: part[...] = (part[...] + got[1]) + (got[2] + got[3])
        elif first == 7: part[...] = (part[...] + got[6]) + (got[4] + got[5])
        for copy in copies[first:last]: copy.start()
    return [lambda: hop(0, 1, 0), lambda: hop(1, 4, 0), lambda: hop(4, 7, 1), lambda: hop(7, 7, 4)]


def swap(away, into, send, recv, peer, parts):
    size = away.shape[0] // parts
    plans = []
    for i in range(parts):
        r = pl.ds(i * size, size)
        give = remote(away.at[r], into.at[r], send.at[i], recv.at[i], peer)
        plans.append([give.start, give.wait])
    return plans


def whole(s):
    return pl.BlockSpec(s, lambda i: (0,) * len(s), pipeline_mode=pl.Buffered(1))


def live_rows(len_ref, rows):
    t = lax.axis_index("tensor")
    place = lax.broadcasted_iota(jnp.int32, (rows, 1), 0)
    length = jnp.where(t == 0, len_ref[0:1], len_ref[1:2])
    return (place + t * (rows // 2)) % rows < length


def forward_pair(bq, hook, len_ref, q_ref, k_ref, v_ref, o_ref, lse_ref):
    rows = q_ref.shape[0]
    lane = lax.broadcasted_iota(jnp.int32, (1, 128), 1)
    kbias = jnp.where(live_rows(len_ref, rows), 0.0, -1e9)
    first = lane < DH

    def block(i, _):
        hook(i, rows // bq)
        place = pl.ds(pl.multiple_of(i * bq, bq), bq)
        q = q_ref[place].astype(F32)
        k, v = k_ref[...].astype(F32), v_ref[...]
        os_, ls = [], []
        for h in range(2):
            own, spare = lane // DH == h, lane == DH * (1 - h)
            qa = jnp.where(own, q, jnp.where(spare, 1.0, 0.0)).astype(BF16)
            ka = jnp.where(own, k, jnp.where(spare, kbias, 0.0)).astype(BF16)
            s = nt(qa, ka)
            m = jnp.max(s, axis=1, keepdims=True)
            p = jnp.exp(s - m)
            l = jnp.sum(p, axis=1, keepdims=True)
            os_.append(nn(p.astype(BF16), v) * (1.0 / l))
            ls.append(m + jnp.log(l))
        o_ref[place] = jnp.where(first, os_[0], os_[1]).astype(BF16)
        lse_ref[place] = jnp.where(first, ls[1], ls[0])
        return 0

    lax.fori_loop(0, rows // bq, block, 0)


def attend_forward(length, q, k, v, bq=512):
    rows, width = q.shape
    spec = pl.BlockSpec((rows, 128), lambda i: (0, i))
    return pl.pallas_call(
        functools.partial(forward_pair, bq, lambda i, n: None),
        grid=(width // 128,),
        in_specs=[LENGTHS, spec, spec, spec],
        out_specs=[spec, spec],
        out_shape=[S((rows, width), BF16), S((rows, width), F32)],
        compiler_params=pltpu.CompilerParams(vmem_limit_bytes=56 << 20),
        name="attend_forward",
    )(length, q, k, v)


def pieces_of(order, letter):
    return len({name for phase in order for name, _ in phase if name[0] == letter})


def run(plans, events):
    for name, stage in events:
        plans[name][stage]()


def front(length, hidden, shards, b_query, b_value, bq=512):
    n = len(shards)
    rows, width = 2 * hidden.shape[1], hidden.shape[2]
    half, pairs = width // 2, width // 128
    items = [(name, w, shards[w].shape[1] // parts * i, shards[w].shape[1] // parts, order) for name, (w, i, parts, order) in FRONT_ITEMS.items()]

    def kernel(*refs):
        len_ref, pair_ref, given, bq_ref, bv_ref = refs[0], refs[1], refs[2 : 2 + n], refs[2 + n], refs[3 + n]
        refs = refs[4 + n :]
        o_ref, lse_ref, outs, far_outs, mixed = refs[0], refs[1], refs[2:6], refs[6 : 3 + n], refs[3 + n]
        refs = refs[4 + n :]
        rows_s, q_s, k_s, v_s, near, mix_s, (send, recv, out_sem), sems = refs[0], refs[1], refs[2], refs[3], refs[4:7], refs[7], refs[8:11], refs[11:]
        step = pl.program_id(0)
        place = Place()
        fulls = list(near) + list(far_outs)
        local = rows // 2
        keep = pltpu.make_async_copy(pair_ref.at[place.t], rows_s.at[pl.ds(0, local)], out_sem.at[4])
        plans = {
            f"h{i}": plan
            for i, plan in enumerate(swap(pair_ref.at[1 - place.t], rows_s.at[pl.ds(local, local)], send, recv, place.beside, pieces_of(FRONT_ORDER, "h")))
        }
        for i, (name, w, at, count, order) in enumerate(items):
            plans[name] = gather_stages(place, order, given[w], fulls[w], at, count, *sems[3 * i : 3 * i + 3])
        stores = [pltpu.make_async_copy(src, dst, out_sem.at[i]) for i, (src, dst) in enumerate(zip((rows_s, q_s, k_s, v_s), outs))]
        stores.append(pltpu.make_async_copy(mix_s, mixed, out_sem.at[5]))

        def turn(i):
            for t in range(2):
                w = near[i][t].reshape(width, half).T
                for j in range(pairs // 2):
                    mix_s[j, t, i * 128 : (i + 1) * 128] = w[j * 128 : (j + 1) * 128]

        def project(full, dst, bias, scale):
            def block(i, _):
                r = pl.ds(pl.multiple_of(i * 256, 256), 256)
                for t in range(2):
                    v = nn(rows_s[r], full[t].reshape(width, half))
                    if bias is not None:
                        v = v + bias[:, t * half : (t + 1) * half]
                    dst[r, t * half : (t + 1) * half] = (v * scale).astype(BF16)
                return 0
            lax.fori_loop(0, rows // 256, block, 0)

        @pl.when(step == 0)
        def _():
            keep.start()
            place.greet(place.near)
            run(plans, FRONT_ORDER[0])
            keep.wait()
            project(near[0], q_s, bq_ref[...].reshape(1, width), 0.125)
            run(plans, FRONT_ORDER[1])
            project(near[1], k_s, None, 1.0)
            run(plans, FRONT_ORDER[2])
            project(near[2], v_s, bv_ref[...].reshape(1, width), 1.0)
            for i in range(3):
                turn(i)
            for store in stores:
                store.start()

        def hook(block, blocks):
            for i in range(pairs):
                for part in range(2):
                    if FRONT_ORDER[3 + 2 * i + part]:
                        @pl.when((step == 1 + i) & (block == part * (blocks // 2)))
                        def _():
                            run(plans, FRONT_ORDER[3 + 2 * i + part])

        @pl.when(step > 0)
        def _():
            cols = pl.ds(pl.multiple_of((step - 1) * 128, 128), 128)
            forward_pair(bq, hook, len_ref, q_s.at[:, cols], k_s.at[:, cols], v_s.at[:, cols], o_ref, lse_ref)

        @pl.when(step == pairs)
        def _():
            run(plans, FRONT_ORDER[3 + 2 * pairs])
            for store in stores:
                store.wait()

    spec = pl.BlockSpec((rows, 128), lambda i: (0, jnp.maximum(i - 1, 0)))
    flat = S((rows, width), BF16)
    full = [S((2, 4, 2, 2) + s.shape, BF16) for s in shards]
    V = pltpu.VMEM
    return pl.pallas_call(
        kernel,
        grid=(1 + pairs,),
        in_specs=[LENGTHS, HBM] + [HBM] * n + [whole((width,))] * 2,
        out_specs=[spec, spec] + [HBM] * (2 + n),
        out_shape=[flat, S((rows, width), F32), flat, flat, flat, flat] + full[3:] + [S((pairs // 2, 2, half, width), BF16)],
        scratch_shapes=[V((rows, width), BF16)] * 4 + [V(f.shape, BF16) for f in full[:3]] + [V((pairs // 2, 2, half, width), BF16), DMA((4,)), DMA((4,)), DMA((6,))]
        + [s for _ in items for s in (DMA((7,)), DMA((7,)), DMA)],
        cost_estimate=pl.CostEstimate(flops=10 * rows * rows * width, bytes_accessed=40 << 20, transcendentals=rows * rows * 12),
        compiler_params=pltpu.CompilerParams(collective_id=1, has_side_effects=True, vmem_limit_bytes=56 << 20),
        name="front",
    )(length, hidden, *shards, b_query, b_value)


def backward_pair(bk, hook, len_ref, q_ref, k_ref, v_ref, d_ref, o_ref, lse_ref, dq_ref, dk_ref, dv_ref, qa_s, ka_s, va_s, da_s, acc):
    rows = q_ref.shape[0]
    lane = lax.broadcasted_iota(jnp.int32, (1, 128), 1)
    kbias = jnp.where(live_rows(len_ref, rows), 0.0, -1e9)
    d = d_ref[...].astype(F32)
    prod = d * o_ref[...].astype(F32)
    hi, mid, lo = split3(-lse_ref[...])
    for h in range(2):
        own = lane // DH == h
        sp = DH * (1 - h)
        def pick(a, b, c, e):
            return jnp.where(lane == sp, a, jnp.where(lane == sp + 1, b, jnp.where(lane == sp + 2, c, jnp.where(lane == sp + 3, e, 0.0))))
        dh, dm, dl = split3(-jnp.sum(jnp.where(own, prod, 0.0), axis=1, keepdims=True))
        qa_s[h] = jnp.where(own, q_ref[...].astype(F32), pick(hi, mid, lo, 1.0)).astype(BF16)
        ka_s[h] = jnp.where(own, k_ref[...].astype(F32), pick(1.0, 1.0, 1.0, kbias)).astype(BF16)
        da_s[h] = jnp.where(own, d, pick(dh, dm, dl, 0.0)).astype(BF16)
        va_s[h] = jnp.where(own, v_ref[...].astype(F32), pick(1.0, 1.0, 1.0, 0.0)).astype(BF16)
    first = lane < DH
    upper = lax.broadcasted_iota(jnp.int32, (128, 1), 0) < DH
    acc[...] = jnp.zeros_like(acc)

    def block(b, _):
        hook(b, rows // bk)
        r = pl.ds(b * bk, bk)
        dks, dvs, dqs = [], [], []
        for h in range(2):
            p = jnp.exp(nt(ka_s[h, r], qa_s[h]))
            ds = (p * nt(va_s[h, r], da_s[h])).astype(BF16)
            dvs.append(nn(p.astype(BF16), d_ref[...]))
            dks.append(nn(ds, q_ref[...]))
            dqs.append(tn(k_ref[r], ds))
        dk_ref[r] = jnp.where(first, dks[0], dks[1]).astype(BF16)
        dv_ref[r] = jnp.where(first, dvs[0], dvs[1]).astype(BF16)
        acc[...] += jnp.where(upper, dqs[0], dqs[1])
        return 0

    for b in range(rows // bk):
        block(b, 0)
    dq_ref[...] = (acc[...].T * 0.125).astype(BF16)


def pair_scratch(rows):
    aug = pltpu.VMEM((2, rows, 128), BF16)
    return [aug, aug, aug, aug, pltpu.VMEM((128, rows), F32)]


def attend_backward(length, q, k, v, d, o, lse, bk=512):
    rows, width = q.shape
    spec = pl.BlockSpec((rows, 128), lambda i: (0, i))
    return pl.pallas_call(
        functools.partial(backward_pair, bk, lambda i, n: None),
        grid=(width // 128,),
        in_specs=[LENGTHS] + [spec] * 6,
        out_specs=[spec] * 3,
        out_shape=[S((rows, width), BF16)] * 3,
        scratch_shapes=pair_scratch(rows),
        compiler_params=pltpu.CompilerParams(vmem_limit_bytes=56 << 20),
        name="attend_backward",
    )(length, q, k, v, d, o, lse)


def back(length, q, k, v, d, o, lse, rows_in, mixed, grad_one, small, grads, bk=512):
    n = len(grads)
    rows, width = q.shape
    half, pairs = width // 2, width // 128
    pieces = pairs // 2
    shards = [(grads[0].shape[4], half)] * pieces + [g.shape[4:] for g in grads]
    items = []
    for name, (w, i, parts, order) in BACK_ITEMS.items():
        items.append((name, w, shards[w][1] // parts * i, shards[w][1] // parts, order))
    vb = small.shape[0] - 4

    def kernel(*refs):
        main_in, rows_ref, mixed_ref, one_ref, small_ref, given = refs[:7], refs[7], refs[8], refs[9], refs[10], refs[11 : 11 + n]
        refs = refs[11 + n :]
        pair_ref, sum_ref, outs = refs[0], refs[1], refs[2 : 2 + pieces + n]
        refs = refs[2 + pieces + n :]
        cat, rT, total, gr_s, own = refs[:5]
        refs = refs[5:]
        part, got, fold_send, fold_recv, send, recv, local_sem = refs[:7]
        main_scratch, scratch = refs[7:12], refs[12:]
        step = pl.program_id(0)
        place = Place()
        local = rows // 2
        keep = pltpu.make_async_copy(gr_s.at[pl.ds(0, local)], pair_ref.at[place.t], local_sem)
        plans = {
            f"r{i}": plan
            for i, plan in enumerate(swap(gr_s.at[pl.ds(local, local)], pair_ref.at[place.t], send, recv, place.beside, pieces_of(BACK_ORDER, "r")))
        }
        plans["sm"] = fold_stages(place, part, got, fold_send, fold_recv)
        sources = [own.at[p] for p in range(pieces)] + list(given)
        for i, (name, w, at, count, order) in enumerate(items):
            plans[name] = reduce_stages(place, order, sources[w], at, count, outs[w], scratch[9 * i : 9 * i + 9])

        @pl.when(step == 0)
        def _():
            place.greet(place.near + (place.corner, place.opposite))
            part[...] = small_ref[...]
            total[...] = one_ref[...]
            rT[...] = rows_ref[...].T

        def at(i, j):
            return 2 * i + j + i // 2

        def hook(block, blocks):
            for i in range(pairs):
                for j in range(2):
                    if BACK_ORDER[at(i, j)]:
                        if block == j * (blocks // 2):
                            @pl.when(step == i)
                            def _():
                                run(plans, BACK_ORDER[at(i, j)])

        t = step % 2
        backward_pair(bk, hook, *main_in, cat.at[t, :, pl.ds(0, 128)], cat.at[t, :, pl.ds(128, 128)], cat.at[t, :, pl.ds(256, 128)], *main_scratch)

        def gather_rows(p, first):
            r = slice(first, first + local)
            v = total[r] + (nn(cat[0, r], mixed_ref[p, 0]) + nn(cat[1, r], mixed_ref[p, 1]))
            total[r] = v
            gr_s[r] = v.astype(BF16)

        @pl.when(step % 2 == 1)
        def _():
            p = step // 2
            last = step == pairs - 1
            gather_rows(p, local)

            @pl.when(last)
            def _():
                run(plans, BACK_ORDER[-3])

            def weigh(t, _):
                own[p, t] = nn(rT[...], cat[t]).astype(BF16).reshape(own.shape[2:])
                sums = colsum(cat[t].astype(F32))
                lanes = pl.ds(pl.multiple_of(t * half + p * 128, 128), 128)
                part[vb : vb + 1, lanes] = sums[:, :128]
                part[vb + 1 : vb + 2, lanes] = sums[:, 256:]
                return 0
            weigh(0, 0)
            weigh(1, 0)
            for i in range(pieces - 1):
                @pl.when(step == 2 * i + 1)
                def _():
                    run(plans, BACK_ORDER[at(2 * i + 1, 2)])

            @pl.when(last)
            def _():
                run(plans, BACK_ORDER[-2])
            gather_rows(p, 0)

        @pl.when(step == pairs - 1)
        def _():
            keep.start()
            run(plans, BACK_ORDER[-1])
            sum_ref[...] = part[...]
            keep.wait()

    spec = pl.BlockSpec((rows, 128), lambda i: (0, i % 2 * (pairs // 2) + i // 2))
    V = pltpu.VMEM
    outs = [S(s, F32) for s in shards]
    return pl.pallas_call(
        kernel,
        grid=(pairs,),
        in_specs=[LENGTHS] + [spec] * 6 + [whole((rows, width)), whole(mixed.shape), whole((rows, width)), whole(small.shape)] + [HBM] * n,
        out_specs=[HBM, whole(small.shape)] + [whole(s) for s in shards],
        out_shape=[S((2, rows // 2, width), BF16), S(small.shape, F32)] + outs,
        scratch_shapes=[V((2, rows, half), BF16), V((width, rows), BF16), V((rows, width), F32), V((rows, width), BF16)]
        + [V((pieces, 2, 4, 2, 2) + shards[0], BF16)]
        + [V(small.shape, F32), V((7,) + small.shape, F32), DMA((7,)), DMA((7,)), DMA((4,)), DMA((4,)), DMA]
        + pair_scratch(rows)
        + [s for _, w, f, c, o in items for s in reduce_scratch(o, shards[w][0], c)],
        cost_estimate=pl.CostEstimate(flops=20 * rows * rows * width, bytes_accessed=60 << 20, transcendentals=rows * rows * 12),
        compiler_params=pltpu.CompilerParams(collective_id=2, has_side_effects=True, vmem_limit_bytes=63 << 20),
        name="back",
    )(length, q, k, v, d, o, lse, rows_in, mixed, grad_one, small, *grads)


def finish(near_out, came_out, grad_hidden, owned):
    local, width = near_out.shape
    pieces = 3

    def kernel(*refs):
        near_ref, came_ref, grad_ref = refs[:3]
        given, (out_ref, hid_ref), outs, sem = refs[3:9], refs[9:11], refs[11:17], refs[17]
        t = lax.axis_index("tensor")
        moves = [(near_ref, out_ref.at[t]), (came_ref, out_ref.at[1 - t]), (grad_ref, hid_ref)]
        moves += list(zip(given[pieces:], outs[3:]))
        for i in range(3):
            for p in range(pieces):
                moves.append((given[p].at[:, pl.ds(i * 128, 128)], outs[i].at[:, pl.ds(p * 128, 128)]))
        copies = [pltpu.make_async_copy(a, b, sem.at[i]) for i, (a, b) in enumerate(moves)]
        for copy in copies:
            copy.start()
        for copy in copies:
            copy.wait()

    return pl.pallas_call(
        kernel,
        in_specs=[pl.BlockSpec(memory_space=pltpu.VMEM)] * 9,
        out_specs=[HBM] * 8,
        out_shape=[S((2, local, width), BF16)] * 2 + [S(o.shape, F32) for o in owned],
        scratch_shapes=[DMA((15,))],
        name="finish",
    )(near_out, came_out, grad_hidden, *owned)


def norm_parts(v):
    c = v - jnp.mean(v, axis=-1, keepdims=True)
    r = lax.rsqrt(jnp.mean(c * c, axis=-1, keepdims=True) + 1e-5)
    return c * r, r


def norm_back(n, r, dyg):
    return r * (dyg - jnp.mean(dyg, axis=-1, keepdims=True) - n * jnp.mean(dyg * n, axis=-1, keepdims=True))


def colsum(v):
    return jnp.sum(v, axis=0, keepdims=True)


def mlp_up_kernel(chunk, a_ref, h_ref, wo_ref, wi_ref, wb_ref, *refs):
    vec_refs, (bi_ref, near_ref, far_ref, mid_ref, v1_ref, v2_ref, act, gp, b2) = refs[:6], refs[6:]
    half, inner = wo_ref.shape[2], wi_ref.shape[2]
    b_out, b_back, gain_one, shift_one, gain_two, shift_two = [ref[...].reshape(1, -1) for ref in vec_refs]
    v1 = h_ref[...].astype(F32) + (nt(a_ref[:, :half], wo_ref[0]) + nt(a_ref[:, half:], wo_ref[1])) + b_out
    v1_ref[...] = v1
    n1, r1 = norm_parts(v1)
    normed = n1 * gain_one + shift_one
    mid = normed.astype(BF16)
    mid_ref[...] = mid
    b2[...] = normed + b_back

    def up(i, _):
        t = i // (inner // chunk)
        cols = pl.ds(pl.multiple_of(i % (inner // chunk) * chunk, chunk), chunk)
        hp = nn(mid, wi_ref[t, :, cols]) + bi_ref[t, :, cols]
        half_up = 0.5 + 0.5 * lax.erf(hp * math.sqrt(0.5))
        a = (hp * half_up).astype(BF16)
        act[t, :, cols] = a
        gp[t, :, cols] = (half_up + hp * (jnp.exp(hp * hp * -0.5) * (1.0 / math.sqrt(2 * math.pi)))).astype(BF16)
        b2[...] += nt(a, wb_ref[t, :, cols])
        return 0

    lax.fori_loop(0, 2 * inner // chunk, up, 0)
    v2_ref[...] = b2[...]
    n2, r2 = norm_parts(b2[...])
    out = (n2 * gain_two + shift_two).astype(BF16)
    step, steps = pl.program_id(0), pl.num_programs(0)

    @pl.when(step < steps // 2)
    def _():
        near_ref[...] = out

    @pl.when(step >= steps // 2)
    def _():
        far_ref[...] = out


def mlp_up(a, h, wo, wi, wb, vec, bi, rows=256, chunk=1536):
    total, width = a.shape
    inner = wi.shape[2]
    row = pl.BlockSpec((rows, width), lambda i: (i, 0))
    wide = pl.BlockSpec((2, rows, inner), lambda i: (0, i, 0))
    return pl.pallas_call(
        functools.partial(mlp_up_kernel, chunk),
        grid=(total // rows,),
        in_specs=[row, row] + [whole(s.shape) for s in (wo, wi, wb, *vec, bi)],
        out_specs=[
            pl.BlockSpec((rows, width), lambda i: (jnp.minimum(i, total // rows // 2 - 1), 0)),
            pl.BlockSpec((rows, width), lambda i: (jnp.maximum(i - total // rows // 2, 0), 0)),
            row, row, row, wide, wide,
        ],
        out_shape=[S((total // 2, width), BF16), S((total // 2, width), BF16), S((total, width), BF16), S((total, width), F32), S((total, width), F32), S((2, total, inner), BF16), S((2, total, inner), BF16)],
        scratch_shapes=[pltpu.VMEM((rows, width), F32)],
        cost_estimate=pl.CostEstimate(flops=total * width * (8 * inner + 2 * width), bytes_accessed=40 << 20, transcendentals=4 * total * inner),
        compiler_params=pltpu.CompilerParams(vmem_limit_bytes=60 << 20),
        name="mlp_up",
    )(a, h, wo, wi, wb, *vec, bi)


def mlp_down_kernel(len_ref, a_ref, mid_ref, cot_ref, far_ref, v1_ref, v2_ref, wo_ref, *refs):
    vec_refs, (wi_ref, wb_ref, act_ref, gp_ref) = refs[:6], refs[6:10]
    g1_ref, ga_ref, gwo_ref, gwi_ref, gwb_ref, small_ref, back, btT, midT, gn, sums_s = refs[10:]
    step = pl.program_id(0)
    rows, half, chunk, block = a_ref.shape[0], wo_ref.shape[2], wi_ref.shape[2], 256
    width = a_ref.shape[1]
    b_out, b_back, gain_one, shift_one, gain_two, shift_two = [ref[...].reshape(1, -1) for ref in vec_refs]

    @pl.when(step == 0)
    def _():
        small_ref[...] = jnp.zeros_like(small_ref)
        midT[...] = mid_ref[...].T
        live = jnp.where(live_rows(len_ref, rows), 1.0, 0.0)
        near = cot_ref.at[lax.axis_index("tensor")]
        for b in range(rows // block):
            r = slice(b * block, (b + 1) * block)
            n2, r2 = norm_parts(v2_ref[r])
            at = (b * block) % (rows // 2)
            go = (near if b < rows // block // 2 else far_ref)[at : at + block].astype(F32) * live[r]
            grad_two = norm_back(n2, r2, go * gain_two)
            bt = grad_two.astype(BF16)
            back[r] = bt
            btT[:, r] = bt.T
            gn[r] = grad_two
            small_ref[1:2] += colsum(grad_two)
            small_ref[4:5] += colsum(go * n2)
            small_ref[5:6] += colsum(go)

    gb = (nn(back[...], wb_ref[0]) * gp_ref[0].astype(F32)).astype(BF16)
    sums = colsum(gb.astype(F32))
    gwb_ref[0] = nn(btT[...], act_ref[0]).astype(BF16)
    gwi_ref[0] = nn(midT[...], gb).astype(BF16)
    gn[...] += nt(gb, wi_ref[0])
    sums_s[...] = sums
    for j in range(half * 8 // chunk):
        @pl.when(step == j)
        def _():
            for at in range(j * chunk, (j + 1) * chunk, 128):
                small_ref[8 + at // width : 9 + at // width, at % width : at % width + 128] = sums_s[:, at - j * chunk : at - j * chunk + 128]

    @pl.when(step == pl.num_programs(0) - 1)
    def _():
        for b in range(rows // block):
            r = slice(b * block, (b + 1) * block)
            g = gn[r]
            n1, r1 = norm_parts(v1_ref[r])
            grad_one = norm_back(n1, r1, g * gain_one)
            bo = grad_one.astype(BF16)
            back[r] = bo
            g1_ref[r] = grad_one
            small_ref[0:1] += colsum(grad_one)
            small_ref[2:3] += colsum(g * n1)
            small_ref[3:4] += colsum(g)
            for t in range(2):
                ga_ref[r, t * half : (t + 1) * half] = nn(bo, wo_ref[t]).astype(BF16)
        btT[...] = back[...].T
        for t in range(2):
            gwo_ref[t] = nn(btT[...], a_ref[:, t * half : (t + 1) * half]).astype(BF16)


def mlp_down(length, a, mid, cot, far, v1, v2, wo, wi, wb, act, gp, vec, chunk=512):
    rows, width = a.shape
    inner = wi.shape[2]
    m = inner // chunk
    tall = pl.BlockSpec((1, rows, chunk), lambda i: (i // m, 0, i % m))
    weight = pl.BlockSpec((1, width, chunk), lambda i: (i // m, 0, i % m))
    V = pltpu.VMEM
    small = (12 + 2 * inner // width, width)
    return pl.pallas_call(
        mlp_down_kernel,
        grid=(2 * m,),
        in_specs=[LENGTHS] + [whole(s.shape) for s in (a, mid, cot, far, v1, v2, wo, *vec)] + [weight, weight, tall, tall],
        out_specs=[whole((rows, width)), whole((rows, width)), whole(wo.shape), weight, weight, whole(small)],
        out_shape=[S((rows, width), F32), S((rows, width), BF16), S(wo.shape, BF16), S(wi.shape, BF16), S(wb.shape, BF16), S(small, F32)],
        scratch_shapes=[V((rows, width), BF16), V((width, rows), BF16), V((width, rows), BF16), V((rows, width), F32), V((1, chunk), F32)],
        cost_estimate=pl.CostEstimate(flops=rows * width * (16 * inner + 4 * width), bytes_accessed=60 << 20, transcendentals=0),
        compiler_params=pltpu.CompilerParams(vmem_limit_bytes=62 << 20),
        name="mlp_down",
    )(length, a, mid, cot, far, v1, v2, wo, *vec, wi, wb, act, gp)


def per_device(
    hidden, lengths, cotangent, w_query, w_key, w_value, w_out, w_in, w_back,
    b_query, b_value, b_out, b_in, b_back, gain_one, shift_one, gain_two, shift_two,
):
    t = lax.axis_index("tensor")
    local = hidden.shape[1]
    width = b_query.shape[0]
    inner = b_in.shape[0]
    own_kernels = lax.axis_size("dp") == 16 and lax.axis_size("tensor") == 2
    flip = [(0, 1), (1, 0)]

    def mine(a):
        return lax.dynamic_index_in_dim(a, t, 0, keepdims=False)

    def take(a):
        other = lax.dynamic_index_in_dim(a, 1 - t, 0, keepdims=False)
        return jnp.concatenate([mine(a), lax.ppermute(other, "tensor", flip)], 0)

    def give(a):
        got = lax.ppermute(a[local:], "tensor", flip)
        first = t == 0
        return jnp.stack([jnp.where(first, a[:local], got), jnp.where(first, got, a[:local])], 0)

    def gather(w):
        return lax.all_gather(lax.all_gather(w, "dp", axis=0, tiled=True), "tensor", axis=0)

    def scatter(g):
        g = lax.psum_scatter(g, "dp", scatter_dimension=1, tiled=True)
        return lax.psum_scatter(g, "tensor", scatter_dimension=0, tiled=False).astype(F32)

    def flat(w):
        return w.reshape(2, width, -1)

    vec = (b_out, b_back, gain_one, shift_one, gain_two, shift_two)
    shards = (w_query, w_key, w_value, w_out, w_in, w_back)
    if own_kernels:
        attended, lse, rows, query, key, value, full_out, full_in, full_back, mixed = front(lengths, hidden, shards, b_query, b_value)
        full_out, full_in, full_back = flat(full_out), flat(full_in), flat(full_back)
        late_cotangent = lax.optimization_barrier((cotangent, attended))[0]
    else:
        late_cotangent = cotangent
        rows = take(hidden)
        full_query, full_key, full_value, full_out, full_in, full_back = [gather(w) for w in shards]

        def project(w):
            return jnp.concatenate([nn(rows, w[0]), nn(rows, w[1])], 1)

        query = ((project(full_query) + b_query) * 0.125).astype(BF16)
        key = project(full_key).astype(BF16)
        value = (project(full_value) + b_value).astype(BF16)
        attended, lse = attend_forward(lengths, query, key, value)
    bi = b_in.reshape(2, 1, inner // 2)
    far_cot = lax.ppermute(lax.dynamic_index_in_dim(late_cotangent, 1 - t, 0, keepdims=False), "tensor", flip)
    near_out, far_out, mid, v1, v2, act, gp = mlp_up(attended, rows, full_out, full_in, full_back, vec, bi)
    came_out = lax.ppermute(far_out, "tensor", flip)
    grad_one, grad_attended, g_out, g_in, g_back, small = mlp_down(
        lengths, attended, mid, cotangent, far_cot, v1, v2, full_out, full_in, full_back, act, gp, vec
    )
    def split(g):
        return g.reshape(2, 4, 2, 2, -1, g.shape[-1])
    vb = 8 + inner // width
    if own_kernels:
        grad_hidden, small, *owned = back(
            lengths, query, key, value, grad_attended, attended, lse, rows, mixed, grad_one, small, [split(g) for g in (g_out, g_in, g_back)]
        )
        output, grad_hidden, *owned = finish(near_out, came_out, grad_hidden, owned)
    else:
        d_query, d_key, d_value = attend_backward(lengths, query, key, value, grad_attended, attended, lse)
        total = grad_one
        grads = []
        for d, w in ((d_query, full_query), (d_key, full_key), (d_value, full_value)):
            total = total + nt(d, jnp.concatenate([w[0], w[1]], 1))
            g = tn(rows, d).astype(BF16)
            grads.append(jnp.stack([g[:, : width // 2], g[:, width // 2 :]]))
        small = small.at[vb].set(jnp.sum(d_query.astype(F32), 0)).at[vb + 1].set(jnp.sum(d_value.astype(F32), 0))
        first = t == 0
        output = jnp.stack([jnp.where(first, near_out, came_out), jnp.where(first, came_out, near_out)], 0)
        grad_hidden = give(total.astype(BF16))
        owned = [scatter(g) for g in grads + [g_out, g_in, g_back]]
        small = lax.psum(small, ("dp", "tensor"))
    return (
        output, grad_hidden, *owned,
        small[vb], small[vb + 1], small[0], small[8:vb].reshape(inner), small[1], small[2], small[3], small[4], small[5],
    )


def solution(mesh):
    rows = P(None, ("dp", "tensor"), None)
    weight = P("dp", "tensor")
    return jax.shard_map(
        per_device,
        mesh=mesh,
        in_specs=(rows, P(None, "dp"), rows) + (weight,) * 6 + (P(),) * 9,
        out_specs=(rows, rows) + (weight,) * 6 + (P(),) * 9,
        check_vma=False,
    )
```

```python
import functools
import math

import jax
import jax.numpy as jnp
from jax import lax
from jax.experimental import pallas as pl
from jax.experimental.pallas import tpu as pltpu
from jax.sharding import PartitionSpec as P

F32, BF16 = jnp.float32, jnp.bfloat16
DH = 64
S = jax.ShapeDtypeStruct
HBM = pl.BlockSpec(memory_space=pl.ANY)
LENGTHS = pl.BlockSpec(memory_space=pltpu.VMEM)
DMA = pltpu.SemaphoreType.DMA


def nt(a, b):
    return lax.dot_general(a, b, (((1,), (1,)), ((), ())), preferred_element_type=F32)


def nn(a, b):
    return lax.dot_general(a, b, (((1,), (0,)), ((), ())), preferred_element_type=F32)


def tn(a, b):
    return lax.dot_general(a, b, (((0,), (0,)), ((), ())), preferred_element_type=F32)


def split3(v):
    hi = v.astype(BF16).astype(F32)
    rest = v - hi
    mid = rest.astype(BF16).astype(F32)
    return hi, mid, rest - mid


class Place:
    def __init__(self):
        dp, t = lax.axis_index("dp"), lax.axis_index("tensor")
        z, x, c = dp // 4, (dp // 2) % 2, dp % 2
        self.z, self.x, self.c, self.t = z, x, c, t
        self.above, self.below, self.far = (z + 1) % 4, (z + 3) % 4, (z + 2) % 4
        at = lambda z, x, c, t: ((z * 2 + x) * 2 + c, t)
        self.up, self.down = at(self.above, x, c, t), at(self.below, x, c, t)
        self.across, self.beside, self.twin = at(z, 1 - x, c, t), at(z, x, c, 1 - t), at(z, x, 1 - c, t)
        self.corner, self.opposite = at(z, 1 - x, c, 1 - t), at(self.far, x, c, t)
        self.near = (self.up, self.down, self.across, self.beside, self.twin)

    def greet(self, peers):
        barrier = pltpu.get_barrier_semaphore()
        for peer in peers:
            pl.semaphore_signal(barrier, inc=1, device_id=peer, device_id_type=pl.DeviceIdType.MESH)
        pl.semaphore_wait(barrier, len(peers))


def remote(src, dst, send, recv, peer):
    return pltpu.make_async_remote_copy(src, dst, send, recv, device_id=peer, device_id_type=pl.DeviceIdType.MESH)


def gather_stages(place, order, shard, full, first, count, send, recv, local):
    z, x, c, t = place.z, place.x, place.c, place.t
    lanes = pl.ds(first, count)
    part = count // 256 * 128
    low, high = pl.ds(first, part), pl.ds(first + part, count - part)
    own = full.at[t, z, x, c, :, lanes]
    here = shard.at[:, lanes]
    def move(i, view, peer, src=None):
        return remote(view if src is None else src, view, send.at[i], recv.at[i], peer)
    keep = pltpu.make_async_copy(here, own, local)
    everything = move(6, full.at[:, :, :, c, :, lanes], place.twin)
    if order[0] == "z":
        first_up, first_down = move(0, own, place.up, here), move(1, own, place.down, here)
        next_up = move(2, full.at[t, place.below, x, c, :, low], place.up)
        next_down = move(3, full.at[t, place.above, x, c, :, high], place.down)
        if order == "zxy":
            four, five = move(4, full.at[t, :, x, c, :, lanes], place.across), move(5, full.at[t, :, :, c, :, lanes], place.beside)
        else:
            four, five = move(4, full.at[t, :, x, c, :, lanes], place.beside), move(5, full.at[:, :, x, c, :, lanes], place.across)
        copies = [first_up, first_down, next_up, next_down, four, five, everything]
        def s0(): keep.start(); first_up.start(); first_down.start()
        def s1(): first_up.wait_recv(); next_up.start(); first_down.wait_recv(); next_down.start()
        def s2(): next_up.wait_recv(); next_down.wait_recv(); keep.wait(); four.start()
        def s3(): four.wait_recv(); five.start()
        def s4(): five.wait_recv(); everything.start()
    else:
        if order == "xyz":
            one, two = move(0, own, place.across, here), move(1, full.at[t, z, :, c, :, lanes], place.beside)
        else:
            one, two = move(0, own, place.beside, here), move(1, full.at[:, z, x, c, :, lanes], place.across)
        first_up, first_down = move(2, full.at[:, z, :, c, :, lanes], place.up), move(3, full.at[:, z, :, c, :, lanes], place.down)
        next_up = move(4, full.at[0, place.below, :, c, :, lanes], place.up)
        next_down = move(5, full.at[1, place.above, :, c, :, lanes], place.down)
        copies = [one, two, first_up, first_down, next_up, next_down, everything]
        def s0(): keep.start(); one.start()
        def s1(): one.wait_recv(); keep.wait(); two.start()
        def s2(): two.wait_recv(); first_up.start(); first_down.start()
        def s3(): first_up.wait_recv(); next_up.start(); first_down.wait_recv(); next_down.start()
        def s4(): next_up.wait_recv(); next_down.wait_recv(); everything.start()
    def s5():
        everything.wait_recv()
        for copy in copies: copy.wait_send()
    return [s0, s1, s2, s3, s4, s5]


def add_blocks(count, dst, *srcs):
    def body(i, _):
        ref = dst(i)
        total = ref[...].astype(F32)
        for s in srcs: total = total + s(i)[...].astype(F32)
        ref[...] = total.astype(ref.dtype)
        return 0
    lax.fori_loop(0, count, body, 0)


def reduce_scratch(order, rows, lanes):
    V = lambda *s: pltpu.VMEM(s + (rows, lanes), BF16)
    base = [V(2, 4, 2), V(2, 4, 2)]
    if order == "wide": base += [V(3, 4), V(3), V(), V()]
    elif order == "yxz": base += [V(4, 2), V(4), V(), V(2)]
    elif order == "xyz": base += [V(2, 4), V(4), V(), V(2)]
    else: base += [V(2, 2), V(2, 2, 2), V(2), V()]
    return base + [pltpu.SemaphoreType.DMA((7,)), pltpu.SemaphoreType.DMA((7,)), pltpu.SemaphoreType.DMA]


def wide_stages(place, load, c0, held, r0, r1, r2, out, lanes, move):
    z, x, t = place.z, place.x, place.t
    flat = [
        move(1, held.at[t, :, 1 - x], r1.at[0], place.across),
        move(2, held.at[1 - t, :, x], r1.at[1], place.beside),
        move(3, held.at[1 - t, :, 1 - x], r1.at[2], place.corner),
    ]
    tall = [
        move(4, held.at[t, place.above, x], r2.at[0], place.up),
        move(5, held.at[t, place.below, x], r2.at[1], place.down),
        move(6, held.at[t, place.far, x], r2.at[2], place.opposite),
    ]
    def block(ref): return lambda i: ref.at[i // 8, (i // 2) % 4, i % 2]
    def s0(): load.start(); c0.start()
    def s1():
        load.wait(); c0.wait_recv(); add_blocks(16, block(held), block(r0))
        for copy in flat: copy.start()
    def s2():
        for copy in flat: copy.wait_recv()
        add_blocks(4, lambda k: held.at[t, k, x], *[lambda k, i=i: r1.at[i, k] for i in range(3)])
        for copy in tall: copy.start()
    def s3():
        for copy in tall: copy.wait_recv()
        out[:, lanes] = (held[t, z, x].astype(F32) + r2[2].astype(F32)) + (r2[0].astype(F32) + r2[1].astype(F32))
        for copy in [c0] + flat + tall: copy.wait_send()
    return [s0, s1, s2, s3]


def reduce_stages(place, order, grad, first, count, out, scratch):
    held, r0, r1, r2, r3, r4, send, recv, local = scratch
    z, x, c, t = place.z, place.x, place.c, place.t
    lanes = pl.ds(first, count)
    part = count // 256 * 128
    if part:
        low, high = (slice(None), pl.ds(0, part)), (slice(None), pl.ds(part, count - part))
    else:
        low, high = (pl.ds(0, 16), slice(None)), (pl.ds(16, held.shape[3] - 16), slice(None))
    load = pltpu.make_async_copy(grad.at[:, :, :, c, :, lanes], held, local)
    def move(i, src, dst, peer):
        return remote(src, dst, send.at[i], recv.at[i], peer)
    c0 = move(0, grad.at[:, :, :, 1 - c, :, lanes], r0, place.twin)
    if order == "wide":
        return wide_stages(place, load, c0, held, r0, r1, r2, out, lanes, move)
    at3 = lambda ref: (lambda i: ref.at[i // 8, (i // 2) % 4, i % 2])
    def s0(): load.start(); c0.start()
    if order[0] != "z":
        if order == "yxz":
            c1, c2 = move(1, held.at[1 - t], r1, place.beside), move(2, held.at[t, :, 1 - x], r2, place.across)
            def add1(): add_blocks(8, lambda i: held.at[t, i // 2, i % 2], lambda i: r1.at[i // 2, i % 2])
        else:
            c1, c2 = move(1, held.at[:, :, 1 - x], r1, place.across), move(2, held.at[1 - t, :, x], r2, place.beside)
            def add1(): add_blocks(8, lambda i: held.at[i // 4, i % 4, x], lambda i: r1.at[i // 4, i % 4])
        mine = lambda k: held.at[t, k, x]
        c3 = move(3, held.at[(t, place.far, x) + low], r3.at[low], place.up)
        c4 = move(4, held.at[(t, place.far, x) + high], r3.at[high], place.down)
        c5, c6 = move(5, mine(place.above), r4.at[0], place.up), move(6, mine(place.below), r4.at[1], place.down)
        def s1(): load.wait(); c0.wait_recv(); add_blocks(16, at3(held), at3(r0)); c1.start()
        def s2(): c1.wait_recv(); add1(); c2.start()
        def s3(): c2.wait_recv(); add_blocks(4, mine, lambda k: r2.at[k]); c3.start(); c4.start()
        def s4():
            c3.wait_recv()
            v = held.at[(t, place.above, x) + low]; v[...] = (v[...].astype(F32) + r3[low].astype(F32)).astype(BF16)
            c5.start()
            c4.wait_recv()
            v = held.at[(t, place.below, x) + high]; v[...] = (v[...].astype(F32) + r3[high].astype(F32)).astype(BF16)
            c6.start()
        def s5():
            c5.wait_recv(); c6.wait_recv()
            out[:, lanes] = mine(z)[...].astype(F32) + r4[0].astype(F32) + r4[1].astype(F32)
            for copy in (c0, c1, c2, c3, c4, c5, c6): copy.wait_send()
    else:
        c1, c2 = move(1, held.at[0, place.far], r1.at[0], place.up), move(2, held.at[1, place.far], r1.at[1], place.down)
        c3, c4 = move(3, held.at[:, place.above], r2.at[0], place.up), move(4, held.at[:, place.below], r2.at[1], place.down)
        if order == "zyx":
            c5, c6 = move(5, held.at[1 - t, z], r3, place.beside), move(6, held.at[t, z, 1 - x], r4, place.across)
            def add5(): add_blocks(2, lambda k: held.at[t, z, k], lambda k: r3.at[k])
        else:
            c5, c6 = move(5, held.at[:, z, 1 - x], r3, place.across), move(6, held.at[1 - t, z, x], r4, place.beside)
            def add5(): add_blocks(2, lambda k: held.at[k, z, x], lambda k: r3.at[k])
        def s1(): load.wait(); c0.wait_recv(); add_blocks(16, at3(held), at3(r0)); c1.start(); c2.start()
        def s2():
            c1.wait_recv(); add_blocks(2, lambda k: held.at[0, place.above, k], lambda k: r1.at[0, k]); c3.start()
            c2.wait_recv(); add_blocks(2, lambda k: held.at[1, place.below, k], lambda k: r1.at[1, k]); c4.start()
        def s3():
            c3.wait_recv(); c4.wait_recv()
            add_blocks(4, lambda k: held.at[k // 2, z, k % 2], lambda k: r2.at[0, k // 2, k % 2], lambda k: r2.at[1, k // 2, k % 2])
            c5.start()
        def s4(): c5.wait_recv(); add5(); c6.start()
        def s5():
            c6.wait_recv()
            out[:, lanes] = held[t, z, x].astype(F32) + r4[...].astype(F32)
            for copy in (c0, c1, c2, c3, c4, c5, c6): copy.wait_send()
    return [s0, s1, s2, s3, s4, s5]


FRONT_ITEMS = {
    "q": (0, 0, 1, "zyx"),
    "k": (1, 0, 1, "zyx"),
    "v": (2, 0, 1, "yxz"),
    "o0": (3, 0, 1, "xyz"),
    "i0": (4, 0, 2, "zxy"),
    "i1": (4, 1, 2, "xyz"),
    "b0": (5, 0, 4, "zyx"),
    "b1": (5, 1, 4, "zxy"),
    "b2": (5, 2, 4, "zyx"),
    "b3": (5, 3, 4, "zyx"),
}
BACK_ITEMS = {
    "m0": (0, 0, 1, "xyz"),
    "m1": (1, 0, 1, "yxz"),
    "mq": (2, 0, 3, "zxy"),
    "mk": (2, 1, 3, "zxy"),
    "mv": (2, 2, 3, "yxz"),
    "o0": (3, 0, 1, "zxy"),
    "i0": (4, 0, 2, "zxy"),
    "i1": (4, 1, 2, "xyz"),
    "b0": (5, 0, 2, "yxz"),
    "b1": (5, 1, 2, "xyz"),
}
FRONT_ORDER = (
    (("v", 0), ("q", 0), ("h1", 0), ("k", 0), ("b0", 0), ("v", 1), ("q", 1), ("k", 1), ("v", 2), ("b0", 1), ("i0", 0), ("q", 2), ("k", 2), ("h0", 0), ("i1", 0), ("b1", 0), ("o0", 0), ("h1", 1), ("b2", 0), ("b3", 0), ("q", 3), ("i1", 1), ("v", 3), ("o0", 1), ("b0", 2), ("k", 3), ("i0", 1), ("b1", 1), ("b2", 1), ("q", 4), ("b3", 1), ("h0", 1), ("q", 5),),
    (("v", 4), ("i0", 2), ("i1", 2), ("k", 4), ("b1", 2), ("b2", 2), ("o0", 2), ("b3", 2), ("v", 5), ("k", 5),),
    (),
    (("b0", 3),),
    (("b2", 3), ("i0", 3),),
    (("b1", 3), ("b3", 3),),
    (("i1", 3),),
    (),
    (("b0", 4),),
    (("o0", 3),),
    (("b2", 4), ("b0", 5), ("i0", 4),),
    (("i1", 4),),
    (("b2", 5), ("i0", 5), ("b3", 4), ("o0", 4),),
    (("i1", 5), ("b1", 4),),
    (("o0", 5), ("b3", 5),),
    (("b1", 5),),
)
BACK_ORDER = (
    (("i0", 0), ("i1", 0), ("b1", 0),),
    (("b0", 0),),
    (("i0", 1), ("i1", 1),),
    (("b0", 1), ("b1", 1),),
    (("i0", 2), ("m0", 0),),
    (),
    (("i1", 2), ("m0", 1),),
    (("b0", 2), ("o0", 0),),
    (),
    (("o0", 1), ("i1", 3), ("i0", 3), ("b1", 2), ("m1", 0),),
    (),
    (("o0", 2), ("m1", 1), ("m0", 2),),
    (("b0", 3), ("i1", 4), ("b1", 3),),
    (("i0", 4),),
    (("b0", 4), ("r2", 0), ("o0", 3), ("i1", 5), ("m1", 2), ("m0", 3),),
    (("mv", 0), ("i0", 5), ("b1", 4), ("mq", 0), ("mk", 0), ("o0", 4),),
    (("b0", 5), ("m0", 4), ("mv", 1), ("r2", 1), ("sm", 0), ("mq", 1), ("mk", 1), ("m1", 3), ("r0", 0), ("o0", 5), ("b1", 5), ("sm", 1), ("m0", 5), ("mv", 2), ("mq", 2), ("r1", 0), ("r3", 0), ("mk", 2), ("m1", 4), ("r0", 1), ("mv", 3), ("mq", 3), ("sm", 2), ("mk", 3), ("mq", 4), ("m1", 5), ("mv", 4), ("r1", 1), ("mk", 4), ("sm", 3), ("mv", 5), ("r3", 1), ("mq", 5), ("mk", 5),),
)


def fold_stages(place, part, got, send, recv):
    peers = (place.twin, place.across, place.beside, place.corner, place.up, place.down, place.opposite)
    copies = [remote(part, got.at[i], send.at[i], recv.at[i], peer) for i, peer in enumerate(peers)]
    def hop(first, last, old):
        for copy in copies[old:first]: copy.wait()
        if first == 1: part[...] = part[...] + got[0]
        elif first == 4: part[...] = (part[...] + got[1]) + (got[2] + got[3])
        elif first == 7: part[...] = (part[...] + got[6]) + (got[4] + got[5])
        for copy in copies[first:last]: copy.start()
    return [lambda: hop(0, 1, 0), lambda: hop(1, 4, 0), lambda: hop(4, 7, 1), lambda: hop(7, 7, 4)]


def swap(away, into, send, recv, peer, parts):
    size = away.shape[0] // parts
    plans = []
    for i in range(parts):
        r = pl.ds(i * size, size)
        give = remote(away.at[r], into.at[r], send.at[i], recv.at[i], peer)
        plans.append([give.start, give.wait])
    return plans


def whole(s):
    return pl.BlockSpec(s, lambda i: (0,) * len(s), pipeline_mode=pl.Buffered(1))


def live_rows(len_ref, rows):
    t = lax.axis_index("tensor")
    place = lax.broadcasted_iota(jnp.int32, (rows, 1), 0)
    length = jnp.where(t == 0, len_ref[0:1], len_ref[1:2])
    return (place + t * (rows // 2)) % rows < length


def forward_pair(bq, hook, len_ref, q_ref, k_ref, v_ref, o_ref, lse_ref):
    rows = q_ref.shape[0]
    lane = lax.broadcasted_iota(jnp.int32, (1, 128), 1)
    kbias = jnp.where(live_rows(len_ref, rows), 0.0, -1e9)
    first = lane < DH

    def block(i, _):
        hook(i, rows // bq)
        place = pl.ds(pl.multiple_of(i * bq, bq), bq)
        q = q_ref[place].astype(F32)
        k, v = k_ref[...].astype(F32), v_ref[...]
        os_, ls = [], []
        for h in range(2):
            own, spare = lane // DH == h, lane == DH * (1 - h)
            qa = jnp.where(own, q, jnp.where(spare, 1.0, 0.0)).astype(BF16)
            ka = jnp.where(own, k, jnp.where(spare, kbias, 0.0)).astype(BF16)
            s = nt(qa, ka)
            m = jnp.max(s, axis=1, keepdims=True)
            p = jnp.exp(s - m)
            l = jnp.sum(p, axis=1, keepdims=True)
            os_.append(nn(p.astype(BF16), v) * (1.0 / l))
            ls.append(m + jnp.log(l))
        o_ref[place] = jnp.where(first, os_[0], os_[1]).astype(BF16)
        lse_ref[place] = jnp.where(first, ls[1], ls[0])
        return 0

    lax.fori_loop(0, rows // bq, block, 0)


def attend_forward(length, q, k, v, bq=512):
    rows, width = q.shape
    spec = pl.BlockSpec((rows, 128), lambda i: (0, i))
    return pl.pallas_call(
        functools.partial(forward_pair, bq, lambda i, n: None),
        grid=(width // 128,),
        in_specs=[LENGTHS, spec, spec, spec],
        out_specs=[spec, spec],
        out_shape=[S((rows, width), BF16), S((rows, width), F32)],
        compiler_params=pltpu.CompilerParams(vmem_limit_bytes=56 << 20),
        name="attend_forward",
    )(length, q, k, v)


def pieces_of(order, letter):
    return len({name for phase in order for name, _ in phase if name[0] == letter})


def run(plans, events):
    for name, stage in events:
        plans[name][stage]()


def front(length, hidden, shards, b_query, b_value, bq=512):
    n = len(shards)
    rows, width = 2 * hidden.shape[1], hidden.shape[2]
    half, pairs = width // 2, width // 128
    items = [(name, w, shards[w].shape[1] // parts * i, shards[w].shape[1] // parts, order) for name, (w, i, parts, order) in FRONT_ITEMS.items()]

    def kernel(*refs):
        len_ref, pair_ref, given, bq_ref, bv_ref = refs[0], refs[1], refs[2 : 2 + n], refs[2 + n], refs[3 + n]
        refs = refs[4 + n :]
        o_ref, lse_ref, outs, far_outs, mixed = refs[0], refs[1], refs[2:6], refs[6 : 3 + n], refs[3 + n]
        refs = refs[4 + n :]
        rows_s, q_s, k_s, v_s, near, mix_s, (send, recv, out_sem), sems = refs[0], refs[1], refs[2], refs[3], refs[4:7], refs[7], refs[8:11], refs[11:]
        step = pl.program_id(0)
        place = Place()
        fulls = list(near) + list(far_outs)
        local = rows // 2
        keep = pltpu.make_async_copy(pair_ref.at[place.t], rows_s.at[pl.ds(0, local)], out_sem.at[4])
        plans = {
            f"h{i}": plan
            for i, plan in enumerate(swap(pair_ref.at[1 - place.t], rows_s.at[pl.ds(local, local)], send, recv, place.beside, pieces_of(FRONT_ORDER, "h")))
        }
        for i, (name, w, at, count, order) in enumerate(items):
            plans[name] = gather_stages(place, order, given[w], fulls[w], at, count, *sems[3 * i : 3 * i + 3])
        stores = [pltpu.make_async_copy(src, dst, out_sem.at[i]) for i, (src, dst) in enumerate(zip((rows_s, q_s, k_s, v_s), outs))]
        stores.append(pltpu.make_async_copy(mix_s, mixed, out_sem.at[5]))

        def turn(i):
            for t in range(2):
                w = near[i][t].reshape(width, half).T
                for j in range(pairs // 2):
                    mix_s[j, t, i * 128 : (i + 1) * 128] = w[j * 128 : (j + 1) * 128]

        def project(full, dst, bias, scale):
            def block(i, _):
                r = pl.ds(pl.multiple_of(i * 256, 256), 256)
                for t in range(2):
                    v = nn(rows_s[r], full[t].reshape(width, half))
                    if bias is not None:
                        v = v + bias[:, t * half : (t + 1) * half]
                    dst[r, t * half : (t + 1) * half] = (v * scale).astype(BF16)
                return 0
            lax.fori_loop(0, rows // 256, block, 0)

        @pl.when(step == 0)
        def _():
            keep.start()
            place.greet(place.near)
            run(plans, FRONT_ORDER[0])
            keep.wait()
            project(near[0], q_s, bq_ref[...].reshape(1, width), 0.125)
            run(plans, FRONT_ORDER[1])
            project(near[1], k_s, None, 1.0)
            run(plans, FRONT_ORDER[2])
            project(near[2], v_s, bv_ref[...].reshape(1, width), 1.0)
            for i in range(3):
                turn(i)
            for store in stores:
                store.start()

        def hook(block, blocks):
            for i in range(pairs):
                for part in range(2):
                    if FRONT_ORDER[3 + 2 * i + part]:
                        @pl.when((step == 1 + i) & (block == part * (blocks // 2)))
                        def _():
                            run(plans, FRONT_ORDER[3 + 2 * i + part])

        @pl.when(step > 0)
        def _():
            cols = pl.ds(pl.multiple_of((step - 1) * 128, 128), 128)
            forward_pair(bq, hook, len_ref, q_s.at[:, cols], k_s.at[:, cols], v_s.at[:, cols], o_ref, lse_ref)

        @pl.when(step == pairs)
        def _():
            run(plans, FRONT_ORDER[3 + 2 * pairs])
            for store in stores:
                store.wait()

    spec = pl.BlockSpec((rows, 128), lambda i: (0, jnp.maximum(i - 1, 0)))
    flat = S((rows, width), BF16)
    full = [S((2, 4, 2, 2) + s.shape, BF16) for s in shards]
    V = pltpu.VMEM
    return pl.pallas_call(
        kernel,
        grid=(1 + pairs,),
        in_specs=[LENGTHS, HBM] + [HBM] * n + [whole((width,))] * 2,
        out_specs=[spec, spec] + [HBM] * (2 + n),
        out_shape=[flat, S((rows, width), F32), flat, flat, flat, flat] + full[3:] + [S((pairs // 2, 2, half, width), BF16)],
        scratch_shapes=[V((rows, width), BF16)] * 4 + [V(f.shape, BF16) for f in full[:3]] + [V((pairs // 2, 2, half, width), BF16), DMA((4,)), DMA((4,)), DMA((6,))]
        + [s for _ in items for s in (DMA((7,)), DMA((7,)), DMA)],
        cost_estimate=pl.CostEstimate(flops=10 * rows * rows * width, bytes_accessed=40 << 20, transcendentals=rows * rows * 12),
        compiler_params=pltpu.CompilerParams(collective_id=1, has_side_effects=True, vmem_limit_bytes=56 << 20),
        name="front",
    )(length, hidden, *shards, b_query, b_value)


def backward_pair(bk, hook, len_ref, q_ref, k_ref, v_ref, d_ref, o_ref, lse_ref, dq_ref, dk_ref, dv_ref, qa_s, ka_s, va_s, da_s, acc):
    rows = q_ref.shape[0]
    lane = lax.broadcasted_iota(jnp.int32, (1, 128), 1)
    kbias = jnp.where(live_rows(len_ref, rows), 0.0, -1e9)
    d = d_ref[...].astype(F32)
    prod = d * o_ref[...].astype(F32)
    hi, mid, lo = split3(-lse_ref[...])
    for h in range(2):
        own = lane // DH == h
        sp = DH * (1 - h)
        def pick(a, b, c, e):
            return jnp.where(lane == sp, a, jnp.where(lane == sp + 1, b, jnp.where(lane == sp + 2, c, jnp.where(lane == sp + 3, e, 0.0))))
        dh, dm, dl = split3(-jnp.sum(jnp.where(own, prod, 0.0), axis=1, keepdims=True))
        qa_s[h] = jnp.where(own, q_ref[...].astype(F32), pick(hi, mid, lo, 1.0)).astype(BF16)
        ka_s[h] = jnp.where(own, k_ref[...].astype(F32), pick(1.0, 1.0, 1.0, kbias)).astype(BF16)
        da_s[h] = jnp.where(own, d, pick(dh, dm, dl, 0.0)).astype(BF16)
        va_s[h] = jnp.where(own, v_ref[...].astype(F32), pick(1.0, 1.0, 1.0, 0.0)).astype(BF16)
    first = lane < DH
    upper = lax.broadcasted_iota(jnp.int32, (128, 1), 0) < DH
    acc[...] = jnp.zeros_like(acc)

    def block(b, _):
        hook(b, rows // bk)
        r = pl.ds(b * bk, bk)
        dks, dvs, dqs = [], [], []
        for h in range(2):
            p = jnp.exp(nt(ka_s[h, r], qa_s[h]))
            ds = (p * nt(va_s[h, r], da_s[h])).astype(BF16)
            dvs.append(nn(p.astype(BF16), d_ref[...]))
            dks.append(nn(ds, q_ref[...]))
            dqs.append(tn(k_ref[r], ds))
        dk_ref[r] = jnp.where(first, dks[0], dks[1]).astype(BF16)
        dv_ref[r] = jnp.where(first, dvs[0], dvs[1]).astype(BF16)
        acc[...] += jnp.where(upper, dqs[0], dqs[1])
        return 0

    for b in range(rows // bk):
        block(b, 0)
    dq_ref[...] = (acc[...].T * 0.125).astype(BF16)


def pair_scratch(rows):
    aug = pltpu.VMEM((2, rows, 128), BF16)
    return [aug, aug, aug, aug, pltpu.VMEM((128, rows), F32)]


def attend_backward(length, q, k, v, d, o, lse, bk=512):
    rows, width = q.shape
    spec = pl.BlockSpec((rows, 128), lambda i: (0, i))
    return pl.pallas_call(
        functools.partial(backward_pair, bk, lambda i, n: None),
        grid=(width // 128,),
        in_specs=[LENGTHS] + [spec] * 6,
        out_specs=[spec] * 3,
        out_shape=[S((rows, width), BF16)] * 3,
        scratch_shapes=pair_scratch(rows),
        compiler_params=pltpu.CompilerParams(vmem_limit_bytes=56 << 20),
        name="attend_backward",
    )(length, q, k, v, d, o, lse)


def back(length, q, k, v, d, o, lse, rows_in, mixed, grad_one, small, grads, bk=512):
    n = len(grads)
    rows, width = q.shape
    half, pairs = width // 2, width // 128
    pieces = pairs // 2
    shards = [(grads[0].shape[4], half)] * pieces + [g.shape[4:] for g in grads]
    items = []
    for name, (w, i, parts, order) in BACK_ITEMS.items():
        items.append((name, w, shards[w][1] // parts * i, shards[w][1] // parts, order))
    vb = small.shape[0] - 4

    def kernel(*refs):
        main_in, rows_ref, mixed_ref, one_ref, small_ref, given = refs[:7], refs[7], refs[8], refs[9], refs[10], refs[11 : 11 + n]
        refs = refs[11 + n :]
        pair_ref, sum_ref, outs = refs[0], refs[1], refs[2 : 2 + pieces + n]
        refs = refs[2 + pieces + n :]
        cat, rT, total, gr_s, own, rows_s, mix_s, load_sem = refs[:8]
        refs = refs[8:]
        part, got, fold_send, fold_recv, send, recv, local_sem = refs[:7]
        main_scratch, scratch = refs[7:12], refs[12:]
        step = pl.program_id(0)
        place = Place()
        local = rows // 2
        loads = [
            pltpu.make_async_copy(src, dst, load_sem.at[i])
            for i, (src, dst) in enumerate(((rows_ref, rows_s), (one_ref, total), (mixed_ref, mix_s)))
        ]
        keep = pltpu.make_async_copy(gr_s.at[pl.ds(0, local)], pair_ref.at[place.t], local_sem)
        plans = {
            f"r{i}": plan
            for i, plan in enumerate(swap(gr_s.at[pl.ds(local, local)], pair_ref.at[place.t], send, recv, place.beside, pieces_of(BACK_ORDER, "r")))
        }
        plans["sm"] = fold_stages(place, part, got, fold_send, fold_recv)
        sources = [own.at[p] for p in range(pieces)] + list(given)
        for i, (name, w, at, count, order) in enumerate(items):
            plans[name] = reduce_stages(place, order, sources[w], at, count, outs[w], scratch[9 * i : 9 * i + 9])

        @pl.when(step == 0)
        def _():
            place.greet(place.near + (place.corner, place.opposite))
            part[...] = small_ref[...]
            for load in loads:
                load.start()

        def at(i, j):
            return 2 * i + j + i // 2

        def hook(block, blocks):
            for i in range(pairs):
                for j in range(2):
                    if BACK_ORDER[at(i, j)]:
                        if block == j * (blocks // 2):
                            @pl.when(step == i)
                            def _():
                                run(plans, BACK_ORDER[at(i, j)])

        t = step % 2
        backward_pair(bk, hook, *main_in, cat.at[t, :, pl.ds(0, 128)], cat.at[t, :, pl.ds(128, 128)], cat.at[t, :, pl.ds(256, 128)], *main_scratch)

        def gather_rows(p, first):
            r = slice(first, first + local)
            v = total[r] + (nn(cat[0, r], mix_s[p, 0]) + nn(cat[1, r], mix_s[p, 1]))
            total[r] = v
            gr_s[r] = v.astype(BF16)

        @pl.when(step == 1)
        def _():
            for load in loads:
                load.wait()
            rT[...] = rows_s[...].T

        @pl.when(step % 2 == 1)
        def _():
            p = step // 2
            last = step == pairs - 1
            gather_rows(p, local)

            @pl.when(last)
            def _():
                run(plans, BACK_ORDER[-3])

            def weigh(t, _):
                own[p, t] = nn(rT[...], cat[t]).astype(BF16).reshape(own.shape[2:])
                sums = colsum(cat[t].astype(F32))
                lanes = pl.ds(pl.multiple_of(t * half + p * 128, 128), 128)
                part[vb : vb + 1, lanes] = sums[:, :128]
                part[vb + 1 : vb + 2, lanes] = sums[:, 256:]
                return 0
            weigh(0, 0)
            weigh(1, 0)
            for i in range(pieces - 1):
                @pl.when(step == 2 * i + 1)
                def _():
                    run(plans, BACK_ORDER[at(2 * i + 1, 2)])

            @pl.when(last)
            def _():
                run(plans, BACK_ORDER[-2])
            gather_rows(p, 0)

        @pl.when(step == pairs - 1)
        def _():
            keep.start()
            run(plans, BACK_ORDER[-1])
            sum_ref[...] = part[...]
            keep.wait()

    spec = pl.BlockSpec((rows, 128), lambda i: (0, i % 2 * (pairs // 2) + i // 2))
    V = pltpu.VMEM
    outs = [S(s, F32) for s in shards]
    return pl.pallas_call(
        kernel,
        grid=(pairs,),
        in_specs=[LENGTHS] + [spec] * 6 + [HBM, HBM, HBM, whole(small.shape)] + [HBM] * n,
        out_specs=[HBM, whole(small.shape)] + [whole(s) for s in shards],
        out_shape=[S((2, rows // 2, width), BF16), S(small.shape, F32)] + outs,
        scratch_shapes=[V((2, rows, half), BF16), V((width, rows), BF16), V((rows, width), F32), V((rows, width), BF16)]
        + [V((pieces, 2, 4, 2, 2) + shards[0], BF16), V((rows, width), BF16), V(mixed.shape, BF16), DMA((3,))]
        + [V(small.shape, F32), V((7,) + small.shape, F32), DMA((7,)), DMA((7,)), DMA((4,)), DMA((4,)), DMA]
        + pair_scratch(rows)
        + [s for _, w, f, c, o in items for s in reduce_scratch(o, shards[w][0], c)],
        cost_estimate=pl.CostEstimate(flops=20 * rows * rows * width, bytes_accessed=60 << 20, transcendentals=rows * rows * 12),
        compiler_params=pltpu.CompilerParams(collective_id=2, has_side_effects=True, vmem_limit_bytes=63 << 20),
        name="back",
    )(length, q, k, v, d, o, lse, rows_in, mixed, grad_one, small, *grads)


def finish(near_out, came_out, grad_hidden, owned):
    local, width = near_out.shape
    pieces = 3

    def kernel(*refs):
        near_ref, came_ref, grad_ref = refs[:3]
        given, (out_ref, hid_ref), outs, sem = refs[3:9], refs[9:11], refs[11:17], refs[17]
        t = lax.axis_index("tensor")
        moves = [(near_ref, out_ref.at[t]), (came_ref, out_ref.at[1 - t]), (grad_ref, hid_ref)]
        moves += list(zip(given[pieces:], outs[3:]))
        for i in range(3):
            for p in range(pieces):
                moves.append((given[p].at[:, pl.ds(i * 128, 128)], outs[i].at[:, pl.ds(p * 128, 128)]))
        copies = [pltpu.make_async_copy(a, b, sem.at[i]) for i, (a, b) in enumerate(moves)]
        for copy in copies:
            copy.start()
        for copy in copies:
            copy.wait()

    return pl.pallas_call(
        kernel,
        in_specs=[pl.BlockSpec(memory_space=pltpu.VMEM)] * 9,
        out_specs=[HBM] * 8,
        out_shape=[S((2, local, width), BF16)] * 2 + [S(o.shape, F32) for o in owned],
        scratch_shapes=[DMA((15,))],
        name="finish",
    )(near_out, came_out, grad_hidden, *owned)


def norm_parts(v):
    c = v - jnp.mean(v, axis=-1, keepdims=True)
    r = lax.rsqrt(jnp.mean(c * c, axis=-1, keepdims=True) + 1e-5)
    return c * r, r


def norm_back(n, r, dyg):
    return r * (dyg - jnp.mean(dyg, axis=-1, keepdims=True) - n * jnp.mean(dyg * n, axis=-1, keepdims=True))


def colsum(v):
    return jnp.sum(v, axis=0, keepdims=True)


def mlp_up_kernel(chunk, a_ref, h_ref, wo_ref, wi_ref, wb_ref, *refs):
    vec_refs, (bi_ref, near_ref, far_ref, mid_ref, v1_ref, v2_ref, act, gp, b2) = refs[:6], refs[6:]
    half, inner = wo_ref.shape[2], wi_ref.shape[2]
    b_out, b_back, gain_one, shift_one, gain_two, shift_two = [ref[...].reshape(1, -1) for ref in vec_refs]
    v1 = h_ref[...].astype(F32) + (nt(a_ref[:, :half], wo_ref[0]) + nt(a_ref[:, half:], wo_ref[1])) + b_out
    v1_ref[...] = v1
    n1, r1 = norm_parts(v1)
    normed = n1 * gain_one + shift_one
    mid = normed.astype(BF16)
    mid_ref[...] = mid
    b2[...] = normed + b_back

    def up(i, _):
        t = i // (inner // chunk)
        cols = pl.ds(pl.multiple_of(i % (inner // chunk) * chunk, chunk), chunk)
        hp = nn(mid, wi_ref[t, :, cols]) + bi_ref[t, :, cols]
        half_up = 0.5 + 0.5 * lax.erf(hp * math.sqrt(0.5))
        a = (hp * half_up).astype(BF16)
        act[t, :, cols] = a
        gp[t, :, cols] = (half_up + hp * (jnp.exp(hp * hp * -0.5) * (1.0 / math.sqrt(2 * math.pi)))).astype(BF16)
        b2[...] += nt(a, wb_ref[t, :, cols])
        return 0

    lax.fori_loop(0, 2 * inner // chunk, up, 0)
    v2_ref[...] = b2[...]
    n2, r2 = norm_parts(b2[...])
    out = (n2 * gain_two + shift_two).astype(BF16)
    step, steps = pl.program_id(0), pl.num_programs(0)

    @pl.when(step < steps // 2)
    def _():
        near_ref[...] = out

    @pl.when(step >= steps // 2)
    def _():
        far_ref[...] = out


def mlp_up(a, h, wo, wi, wb, vec, bi, rows=256, chunk=1536):
    total, width = a.shape
    inner = wi.shape[2]
    row = pl.BlockSpec((rows, width), lambda i: (i, 0))
    wide = pl.BlockSpec((2, rows, inner), lambda i: (0, i, 0))
    return pl.pallas_call(
        functools.partial(mlp_up_kernel, chunk),
        grid=(total // rows,),
        in_specs=[row, row] + [whole(s.shape) for s in (wo, wi, wb, *vec, bi)],
        out_specs=[
            pl.BlockSpec((rows, width), lambda i: (jnp.minimum(i, total // rows // 2 - 1), 0)),
            pl.BlockSpec((rows, width), lambda i: (jnp.maximum(i - total // rows // 2, 0), 0)),
            row, row, row, wide, wide,
        ],
        out_shape=[S((total // 2, width), BF16), S((total // 2, width), BF16), S((total, width), BF16), S((total, width), F32), S((total, width), F32), S((2, total, inner), BF16), S((2, total, inner), BF16)],
        scratch_shapes=[pltpu.VMEM((rows, width), F32)],
        cost_estimate=pl.CostEstimate(flops=total * width * (8 * inner + 2 * width), bytes_accessed=40 << 20, transcendentals=4 * total * inner),
        compiler_params=pltpu.CompilerParams(vmem_limit_bytes=60 << 20),
        name="mlp_up",
    )(a, h, wo, wi, wb, *vec, bi)


def mlp_down_kernel(len_ref, a_hbm, mid_ref, cot_ref, far_ref, v1_hbm, v2_ref, wo_hbm, *refs):
    vec_refs, (wi_ref, wb_ref, act_ref, gp_ref) = refs[:6], refs[6:10]
    g1_ref, ga_ref, gwo_ref, gwi_ref, gwb_ref, small_ref, back, btT, midT, gn, sums_s, a_ref, v1_ref, wo_ref, load_sem = refs[10:]
    loads = [pltpu.make_async_copy(src, dst, load_sem.at[i]) for i, (src, dst) in enumerate(((a_hbm, a_ref), (v1_hbm, v1_ref), (wo_hbm, wo_ref)))]
    step = pl.program_id(0)
    rows, half, chunk, block = a_ref.shape[0], wo_ref.shape[2], wi_ref.shape[2], 256
    width = a_ref.shape[1]
    b_out, b_back, gain_one, shift_one, gain_two, shift_two = [ref[...].reshape(1, -1) for ref in vec_refs]

    @pl.when(step == 0)
    def _():
        for load in loads:
            load.start()
        small_ref[...] = jnp.zeros_like(small_ref)
        midT[...] = mid_ref[...].T
        live = jnp.where(live_rows(len_ref, rows), 1.0, 0.0)
        near = cot_ref.at[lax.axis_index("tensor")]
        for b in range(rows // block):
            r = slice(b * block, (b + 1) * block)
            n2, r2 = norm_parts(v2_ref[r])
            at = (b * block) % (rows // 2)
            go = (near if b < rows // block // 2 else far_ref)[at : at + block].astype(F32) * live[r]
            grad_two = norm_back(n2, r2, go * gain_two)
            bt = grad_two.astype(BF16)
            back[r] = bt
            btT[:, r] = bt.T
            gn[r] = grad_two
            small_ref[1:2] += colsum(grad_two)
            small_ref[4:5] += colsum(go * n2)
            small_ref[5:6] += colsum(go)

    gb = (nn(back[...], wb_ref[0]) * gp_ref[0].astype(F32)).astype(BF16)
    sums = colsum(gb.astype(F32))
    gwb_ref[0] = nn(btT[...], act_ref[0]).astype(BF16)
    gwi_ref[0] = nn(midT[...], gb).astype(BF16)
    gn[...] += nt(gb, wi_ref[0])
    sums_s[...] = sums
    for j in range(half * 8 // chunk):
        @pl.when(step == j)
        def _():
            for at in range(j * chunk, (j + 1) * chunk, 128):
                small_ref[8 + at // width : 9 + at // width, at % width : at % width + 128] = sums_s[:, at - j * chunk : at - j * chunk + 128]

    @pl.when(step == pl.num_programs(0) - 1)
    def _():
        for load in loads:
            load.wait()
        for b in range(rows // block):
            r = slice(b * block, (b + 1) * block)
            g = gn[r]
            n1, r1 = norm_parts(v1_ref[r])
            grad_one = norm_back(n1, r1, g * gain_one)
            bo = grad_one.astype(BF16)
            back[r] = bo
            g1_ref[r] = grad_one
            small_ref[0:1] += colsum(grad_one)
            small_ref[2:3] += colsum(g * n1)
            small_ref[3:4] += colsum(g)
            for t in range(2):
                ga_ref[r, t * half : (t + 1) * half] = nn(bo, wo_ref[t]).astype(BF16)
        btT[...] = back[...].T
        for t in range(2):
            gwo_ref[t] = nn(btT[...], a_ref[:, t * half : (t + 1) * half]).astype(BF16)


def mlp_down(length, a, mid, cot, far, v1, v2, wo, wi, wb, act, gp, vec, chunk=512):
    rows, width = a.shape
    inner = wi.shape[2]
    m = inner // chunk
    tall = pl.BlockSpec((1, rows, chunk), lambda i: (i // m, 0, i % m))
    weight = pl.BlockSpec((1, width, chunk), lambda i: (i // m, 0, i % m))
    V = pltpu.VMEM
    small = (12 + 2 * inner // width, width)
    return pl.pallas_call(
        mlp_down_kernel,
        grid=(2 * m,),
        in_specs=[LENGTHS, HBM] + [whole(s.shape) for s in (mid, cot, far)] + [HBM, whole(v2.shape), HBM] + [whole(s.shape) for s in vec] + [weight, weight, tall, tall],
        out_specs=[whole((rows, width)), whole((rows, width)), whole(wo.shape), weight, weight, whole(small)],
        out_shape=[S((rows, width), F32), S((rows, width), BF16), S(wo.shape, BF16), S(wi.shape, BF16), S(wb.shape, BF16), S(small, F32)],
        scratch_shapes=[V((rows, width), BF16), V((width, rows), BF16), V((width, rows), BF16), V((rows, width), F32), V((1, chunk), F32)]
        + [V(a.shape, BF16), V(v1.shape, F32), V(wo.shape, BF16), DMA((3,))],
        cost_estimate=pl.CostEstimate(flops=rows * width * (16 * inner + 4 * width), bytes_accessed=60 << 20, transcendentals=0),
        compiler_params=pltpu.CompilerParams(vmem_limit_bytes=62 << 20),
        name="mlp_down",
    )(length, a, mid, cot, far, v1, v2, wo, *vec, wi, wb, act, gp)


def per_device(
    hidden, lengths, cotangent, w_query, w_key, w_value, w_out, w_in, w_back,
    b_query, b_value, b_out, b_in, b_back, gain_one, shift_one, gain_two, shift_two,
):
    t = lax.axis_index("tensor")
    local = hidden.shape[1]
    width = b_query.shape[0]
    inner = b_in.shape[0]
    own_kernels = lax.axis_size("dp") == 16 and lax.axis_size("tensor") == 2
    flip = [(0, 1), (1, 0)]

    def mine(a):
        return lax.dynamic_index_in_dim(a, t, 0, keepdims=False)

    def take(a):
        other = lax.dynamic_index_in_dim(a, 1 - t, 0, keepdims=False)
        return jnp.concatenate([mine(a), lax.ppermute(other, "tensor", flip)], 0)

    def give(a):
        got = lax.ppermute(a[local:], "tensor", flip)
        first = t == 0
        return jnp.stack([jnp.where(first, a[:local], got), jnp.where(first, got, a[:local])], 0)

    def gather(w):
        return lax.all_gather(lax.all_gather(w, "dp", axis=0, tiled=True), "tensor", axis=0)

    def scatter(g):
        g = lax.psum_scatter(g, "dp", scatter_dimension=1, tiled=True)
        return lax.psum_scatter(g, "tensor", scatter_dimension=0, tiled=False).astype(F32)

    def flat(w):
        return w.reshape(2, width, -1)

    vec = (b_out, b_back, gain_one, shift_one, gain_two, shift_two)
    shards = (w_query, w_key, w_value, w_out, w_in, w_back)
    if own_kernels:
        attended, lse, rows, query, key, value, full_out, full_in, full_back, mixed = front(lengths, hidden, shards, b_query, b_value)
        full_out, full_in, full_back = flat(full_out), flat(full_in), flat(full_back)
        late_cotangent = lax.optimization_barrier((cotangent, attended))[0]
    else:
        late_cotangent = cotangent
        rows = take(hidden)
        full_query, full_key, full_value, full_out, full_in, full_back = [gather(w) for w in shards]

        def project(w):
            return jnp.concatenate([nn(rows, w[0]), nn(rows, w[1])], 1)

        query = ((project(full_query) + b_query) * 0.125).astype(BF16)
        key = project(full_key).astype(BF16)
        value = (project(full_value) + b_value).astype(BF16)
        attended, lse = attend_forward(lengths, query, key, value)
    bi = b_in.reshape(2, 1, inner // 2)
    far_cot = lax.ppermute(lax.dynamic_index_in_dim(late_cotangent, 1 - t, 0, keepdims=False), "tensor", flip)
    near_out, far_out, mid, v1, v2, act, gp = mlp_up(attended, rows, full_out, full_in, full_back, vec, bi)
    came_out = lax.ppermute(far_out, "tensor", flip)
    grad_one, grad_attended, g_out, g_in, g_back, small = mlp_down(
        lengths, attended, mid, cotangent, far_cot, v1, v2, full_out, full_in, full_back, act, gp, vec
    )
    def split(g):
        return g.reshape(2, 4, 2, 2, -1, g.shape[-1])
    vb = 8 + inner // width
    if own_kernels:
        grad_hidden, small, *owned = back(
            lengths, query, key, value, grad_attended, attended, lse, rows, mixed, grad_one, small, [split(g) for g in (g_out, g_in, g_back)]
        )
        output, grad_hidden, *owned = finish(near_out, came_out, grad_hidden, owned)
    else:
        d_query, d_key, d_value = attend_backward(lengths, query, key, value, grad_attended, attended, lse)
        total = grad_one
        grads = []
        for d, w in ((d_query, full_query), (d_key, full_key), (d_value, full_value)):
            total = total + nt(d, jnp.concatenate([w[0], w[1]], 1))
            g = tn(rows, d).astype(BF16)
            grads.append(jnp.stack([g[:, : width // 2], g[:, width // 2 :]]))
        small = small.at[vb].set(jnp.sum(d_query.astype(F32), 0)).at[vb + 1].set(jnp.sum(d_value.astype(F32), 0))
        first = t == 0
        output = jnp.stack([jnp.where(first, near_out, came_out), jnp.where(first, came_out, near_out)], 0)
        grad_hidden = give(total.astype(BF16))
        owned = [scatter(g) for g in grads + [g_out, g_in, g_back]]
        small = lax.psum(small, ("dp", "tensor"))
    return (
        output, grad_hidden, *owned,
        small[vb], small[vb + 1], small[0], small[8:vb].reshape(inner), small[1], small[2], small[3], small[4], small[5],
    )


def solution(mesh):
    rows = P(None, ("dp", "tensor"), None)
    weight = P("dp", "tensor")
    return jax.shard_map(
        per_device,
        mesh=mesh,
        in_specs=(rows, P(None, "dp"), rows) + (weight,) * 6 + (P(),) * 9,
        out_specs=(rows, rows) + (weight,) * 6 + (P(),) * 9,
        check_vma=False,
    )
```

```python
import functools
import math

import jax
import jax.numpy as jnp
from jax import lax
from jax.experimental import pallas as pl
from jax.experimental.pallas import tpu as pltpu
from jax.sharding import PartitionSpec as P

F32, BF16 = jnp.float32, jnp.bfloat16
DH = 64
S = jax.ShapeDtypeStruct
HBM = pl.BlockSpec(memory_space=pl.ANY)
LENGTHS = pl.BlockSpec(memory_space=pltpu.VMEM)
DMA = pltpu.SemaphoreType.DMA


def nt(a, b):
    return lax.dot_general(a, b, (((1,), (1,)), ((), ())), preferred_element_type=F32)


def nn(a, b):
    return lax.dot_general(a, b, (((1,), (0,)), ((), ())), preferred_element_type=F32)


def tn(a, b):
    return lax.dot_general(a, b, (((0,), (0,)), ((), ())), preferred_element_type=F32)


def split3(v):
    hi = v.astype(BF16).astype(F32)
    rest = v - hi
    mid = rest.astype(BF16).astype(F32)
    return hi, mid, rest - mid


class Place:
    def __init__(self):
        dp, t = lax.axis_index("dp"), lax.axis_index("tensor")
        z, x, c = dp // 4, (dp // 2) % 2, dp % 2
        self.z, self.x, self.c, self.t = z, x, c, t
        self.above, self.below, self.far = (z + 1) % 4, (z + 3) % 4, (z + 2) % 4
        at = lambda z, x, c, t: ((z * 2 + x) * 2 + c, t)
        self.up, self.down = at(self.above, x, c, t), at(self.below, x, c, t)
        self.across, self.beside, self.twin = at(z, 1 - x, c, t), at(z, x, c, 1 - t), at(z, x, 1 - c, t)
        self.corner, self.opposite = at(z, 1 - x, c, 1 - t), at(self.far, x, c, t)
        self.near = (self.up, self.down, self.across, self.beside, self.twin)

    def greet(self, peers):
        barrier = pltpu.get_barrier_semaphore()
        for peer in peers:
            pl.semaphore_signal(barrier, inc=1, device_id=peer, device_id_type=pl.DeviceIdType.MESH)
        pl.semaphore_wait(barrier, len(peers))


def remote(src, dst, send, recv, peer):
    return pltpu.make_async_remote_copy(src, dst, send, recv, device_id=peer, device_id_type=pl.DeviceIdType.MESH)


def gather_stages(place, order, shard, full, first, count, send, recv, local):
    z, x, c, t = place.z, place.x, place.c, place.t
    lanes = pl.ds(first, count)
    part = count // 256 * 128
    low, high = pl.ds(first, part), pl.ds(first + part, count - part)
    own = full.at[t, z, x, c, :, lanes]
    here = shard.at[:, lanes]
    def move(i, view, peer, src=None):
        return remote(view if src is None else src, view, send.at[i], recv.at[i], peer)
    keep = pltpu.make_async_copy(here, own, local)
    everything = move(6, full.at[:, :, :, c, :, lanes], place.twin)
    if order[0] == "z":
        first_up, first_down = move(0, own, place.up, here), move(1, own, place.down, here)
        next_up = move(2, full.at[t, place.below, x, c, :, low], place.up)
        next_down = move(3, full.at[t, place.above, x, c, :, high], place.down)
        if order == "zxy":
            four, five = move(4, full.at[t, :, x, c, :, lanes], place.across), move(5, full.at[t, :, :, c, :, lanes], place.beside)
        else:
            four, five = move(4, full.at[t, :, x, c, :, lanes], place.beside), move(5, full.at[:, :, x, c, :, lanes], place.across)
        copies = [first_up, first_down, next_up, next_down, four, five, everything]
        def s0(): keep.start(); first_up.start(); first_down.start()
        def s1(): first_up.wait_recv(); next_up.start(); first_down.wait_recv(); next_down.start()
        def s2(): next_up.wait_recv(); next_down.wait_recv(); keep.wait(); four.start()
        def s3(): four.wait_recv(); five.start()
        def s4(): five.wait_recv(); everything.start()
    else:
        if order == "xyz":
            one, two = move(0, own, place.across, here), move(1, full.at[t, z, :, c, :, lanes], place.beside)
        else:
            one, two = move(0, own, place.beside, here), move(1, full.at[:, z, x, c, :, lanes], place.across)
        first_up, first_down = move(2, full.at[:, z, :, c, :, lanes], place.up), move(3, full.at[:, z, :, c, :, lanes], place.down)
        next_up = move(4, full.at[0, place.below, :, c, :, lanes], place.up)
        next_down = move(5, full.at[1, place.above, :, c, :, lanes], place.down)
        copies = [one, two, first_up, first_down, next_up, next_down, everything]
        def s0(): keep.start(); one.start()
        def s1(): one.wait_recv(); keep.wait(); two.start()
        def s2(): two.wait_recv(); first_up.start(); first_down.start()
        def s3(): first_up.wait_recv(); next_up.start(); first_down.wait_recv(); next_down.start()
        def s4(): next_up.wait_recv(); next_down.wait_recv(); everything.start()
    def s5():
        everything.wait_recv()
        for copy in copies: copy.wait_send()
    return [s0, s1, s2, s3, s4, s5]


def add_blocks(count, dst, *srcs):
    def body(i, _):
        ref = dst(i)
        total = ref[...].astype(F32)
        for s in srcs: total = total + s(i)[...].astype(F32)
        ref[...] = total.astype(ref.dtype)
        return 0
    lax.fori_loop(0, count, body, 0)


def reduce_scratch(order, rows, lanes):
    V = lambda *s: pltpu.VMEM(s + (rows, lanes), BF16)
    base = [V(2, 4, 2), V(2, 4, 2)]
    if order == "wide": base += [V(3, 4), V(3), V(), V()]
    elif order == "yxz": base += [V(4, 2), V(4), V(), V(2)]
    elif order == "xyz": base += [V(2, 4), V(4), V(), V(2)]
    else: base += [V(2, 2), V(2, 2, 2), V(2), V()]
    return base + [pltpu.SemaphoreType.DMA((7,)), pltpu.SemaphoreType.DMA((7,)), pltpu.SemaphoreType.DMA]


def wide_stages(place, load, c0, held, r0, r1, r2, out, lanes, move):
    z, x, t = place.z, place.x, place.t
    flat = [
        move(1, held.at[t, :, 1 - x], r1.at[0], place.across),
        move(2, held.at[1 - t, :, x], r1.at[1], place.beside),
        move(3, held.at[1 - t, :, 1 - x], r1.at[2], place.corner),
    ]
    tall = [
        move(4, held.at[t, place.above, x], r2.at[0], place.up),
        move(5, held.at[t, place.below, x], r2.at[1], place.down),
        move(6, held.at[t, place.far, x], r2.at[2], place.opposite),
    ]
    def block(ref): return lambda i: ref.at[i // 8, (i // 2) % 4, i % 2]
    def s0(): load.start(); c0.start()
    def s1():
        load.wait(); c0.wait_recv(); add_blocks(16, block(held), block(r0))
        for copy in flat: copy.start()
    def s2():
        for copy in flat: copy.wait_recv()
        add_blocks(4, lambda k: held.at[t, k, x], *[lambda k, i=i: r1.at[i, k] for i in range(3)])
        for copy in tall: copy.start()
    def s3():
        for copy in tall: copy.wait_recv()
        out[:, lanes] = (held[t, z, x].astype(F32) + r2[2].astype(F32)) + (r2[0].astype(F32) + r2[1].astype(F32))
        for copy in [c0] + flat + tall: copy.wait_send()
    return [s0, s1, s2, s3]


def reduce_stages(place, order, grad, first, count, out, scratch):
    held, r0, r1, r2, r3, r4, send, recv, local = scratch
    z, x, c, t = place.z, place.x, place.c, place.t
    lanes = pl.ds(first, count)
    part = count // 256 * 128
    if part:
        low, high = (slice(None), pl.ds(0, part)), (slice(None), pl.ds(part, count - part))
    else:
        low, high = (pl.ds(0, 16), slice(None)), (pl.ds(16, held.shape[3] - 16), slice(None))
    load = pltpu.make_async_copy(grad.at[:, :, :, c, :, lanes], held, local)
    def move(i, src, dst, peer):
        return remote(src, dst, send.at[i], recv.at[i], peer)
    c0 = move(0, grad.at[:, :, :, 1 - c, :, lanes], r0, place.twin)
    if order == "wide":
        return wide_stages(place, load, c0, held, r0, r1, r2, out, lanes, move)
    at3 = lambda ref: (lambda i: ref.at[i // 8, (i // 2) % 4, i % 2])
    def s0(): load.start(); c0.start()
    if order[0] != "z":
        if order == "yxz":
            c1, c2 = move(1, held.at[1 - t], r1, place.beside), move(2, held.at[t, :, 1 - x], r2, place.across)
            def add1(): add_blocks(8, lambda i: held.at[t, i // 2, i % 2], lambda i: r1.at[i // 2, i % 2])
        else:
            c1, c2 = move(1, held.at[:, :, 1 - x], r1, place.across), move(2, held.at[1 - t, :, x], r2, place.beside)
            def add1(): add_blocks(8, lambda i: held.at[i // 4, i % 4, x], lambda i: r1.at[i // 4, i % 4])
        mine = lambda k: held.at[t, k, x]
        c3 = move(3, held.at[(t, place.far, x) + low], r3.at[low], place.up)
        c4 = move(4, held.at[(t, place.far, x) + high], r3.at[high], place.down)
        c5, c6 = move(5, mine(place.above), r4.at[0], place.up), move(6, mine(place.below), r4.at[1], place.down)
        def s1(): load.wait(); c0.wait_recv(); add_blocks(16, at3(held), at3(r0)); c1.start()
        def s2(): c1.wait_recv(); add1(); c2.start()
        def s3(): c2.wait_recv(); add_blocks(4, mine, lambda k: r2.at[k]); c3.start(); c4.start()
        def s4():
            c3.wait_recv()
            v = held.at[(t, place.above, x) + low]; v[...] = (v[...].astype(F32) + r3[low].astype(F32)).astype(BF16)
            c5.start()
            c4.wait_recv()
            v = held.at[(t, place.below, x) + high]; v[...] = (v[...].astype(F32) + r3[high].astype(F32)).astype(BF16)
            c6.start()
        def s5():
            c5.wait_recv(); c6.wait_recv()
            out[:, lanes] = mine(z)[...].astype(F32) + r4[0].astype(F32) + r4[1].astype(F32)
            for copy in (c0, c1, c2, c3, c4, c5, c6): copy.wait_send()
    else:
        c1, c2 = move(1, held.at[0, place.far], r1.at[0], place.up), move(2, held.at[1, place.far], r1.at[1], place.down)
        c3, c4 = move(3, held.at[:, place.above], r2.at[0], place.up), move(4, held.at[:, place.below], r2.at[1], place.down)
        if order == "zyx":
            c5, c6 = move(5, held.at[1 - t, z], r3, place.beside), move(6, held.at[t, z, 1 - x], r4, place.across)
            def add5(): add_blocks(2, lambda k: held.at[t, z, k], lambda k: r3.at[k])
        else:
            c5, c6 = move(5, held.at[:, z, 1 - x], r3, place.across), move(6, held.at[1 - t, z, x], r4, place.beside)
            def add5(): add_blocks(2, lambda k: held.at[k, z, x], lambda k: r3.at[k])
        def s1(): load.wait(); c0.wait_recv(); add_blocks(16, at3(held), at3(r0)); c1.start(); c2.start()
        def s2():
            c1.wait_recv(); add_blocks(2, lambda k: held.at[0, place.above, k], lambda k: r1.at[0, k]); c3.start()
            c2.wait_recv(); add_blocks(2, lambda k: held.at[1, place.below, k], lambda k: r1.at[1, k]); c4.start()
        def s3():
            c3.wait_recv(); c4.wait_recv()
            add_blocks(4, lambda k: held.at[k // 2, z, k % 2], lambda k: r2.at[0, k // 2, k % 2], lambda k: r2.at[1, k // 2, k % 2])
            c5.start()
        def s4(): c5.wait_recv(); add5(); c6.start()
        def s5():
            c6.wait_recv()
            out[:, lanes] = held[t, z, x].astype(F32) + r4[...].astype(F32)
            for copy in (c0, c1, c2, c3, c4, c5, c6): copy.wait_send()
    return [s0, s1, s2, s3, s4, s5]


FRONT_ITEMS = {
    "q": (0, 0, 1, "zyx"),
    "k": (1, 0, 1, "zyx"),
    "v": (2, 0, 1, "yxz"),
    "o0": (3, 0, 1, "xyz"),
    "i0": (4, 0, 2, "zxy"),
    "i1": (4, 1, 2, "xyz"),
    "b0": (5, 0, 4, "zyx"),
    "b1": (5, 1, 4, "zxy"),
    "b2": (5, 2, 4, "zyx"),
    "b3": (5, 3, 4, "zyx"),
}
BACK_ITEMS = {
    "m0": (0, 0, 1, "xyz"),
    "m1": (1, 0, 1, "yxz"),
    "mq": (2, 0, 3, "zxy"),
    "mk": (2, 1, 3, "zxy"),
    "mv": (2, 2, 3, "yxz"),
    "o0": (3, 0, 1, "zxy"),
    "i0": (4, 0, 2, "zxy"),
    "i1": (4, 1, 2, "xyz"),
    "b0": (5, 0, 2, "yxz"),
    "b1": (5, 1, 2, "xyz"),
}
FRONT_ORDER = (
    (("v", 0), ("q", 0), ("h1", 0), ("k", 0), ("b0", 0), ("v", 1), ("q", 1), ("k", 1), ("v", 2), ("b0", 1), ("i0", 0), ("q", 2), ("k", 2), ("h0", 0), ("i1", 0), ("b1", 0), ("o0", 0), ("h1", 1), ("b2", 0), ("b3", 0), ("q", 3), ("i1", 1), ("v", 3), ("o0", 1), ("b0", 2), ("k", 3), ("i0", 1), ("b1", 1), ("b2", 1), ("q", 4), ("b3", 1), ("h0", 1), ("q", 5),),
    (("v", 4), ("i0", 2), ("i1", 2), ("k", 4), ("b1", 2), ("b2", 2), ("o0", 2), ("b3", 2), ("v", 5), ("k", 5),),
    (),
    (("b0", 3),),
    (("b2", 3), ("i0", 3),),
    (("b1", 3), ("b3", 3),),
    (("i1", 3),),
    (),
    (("b0", 4),),
    (("o0", 3),),
    (("b2", 4), ("b0", 5), ("i0", 4),),
    (("i1", 4),),
    (("b2", 5), ("i0", 5), ("b3", 4), ("o0", 4),),
    (("i1", 5), ("b1", 4),),
    (("o0", 5), ("b3", 5),),
    (("b1", 5),),
)
BACK_ORDER = (
    (("i0", 0), ("i1", 0), ("b1", 0),),
    (("b0", 0),),
    (("i0", 1), ("i1", 1),),
    (("b0", 1), ("b1", 1),),
    (("i0", 2), ("m0", 0),),
    (),
    (("i1", 2), ("m0", 1),),
    (("b0", 2), ("o0", 0),),
    (),
    (("o0", 1), ("i1", 3), ("i0", 3), ("b1", 2), ("m1", 0),),
    (),
    (("o0", 2), ("m1", 1), ("m0", 2),),
    (("b0", 3), ("i1", 4), ("b1", 3),),
    (("i0", 4),),
    (("b0", 4), ("r2", 0), ("o0", 3), ("i1", 5), ("m1", 2), ("m0", 3),),
    (("mv", 0), ("i0", 5), ("b1", 4), ("mq", 0), ("mk", 0), ("o0", 4),),
    (("b0", 5), ("m0", 4), ("mv", 1), ("r2", 1), ("sm", 0), ("mq", 1), ("mk", 1), ("m1", 3), ("r0", 0), ("o0", 5), ("b1", 5), ("sm", 1), ("m0", 5), ("mv", 2), ("mq", 2), ("r1", 0), ("r3", 0), ("mk", 2), ("m1", 4), ("r0", 1), ("mv", 3), ("mq", 3), ("sm", 2), ("mk", 3), ("mq", 4), ("m1", 5), ("mv", 4), ("r1", 1), ("mk", 4), ("sm", 3), ("mv", 5), ("r3", 1), ("mq", 5), ("mk", 5),),
)


def fold_stages(place, part, got, send, recv):
    peers = (place.twin, place.across, place.beside, place.corner, place.up, place.down, place.opposite)
    copies = [remote(part, got.at[i], send.at[i], recv.at[i], peer) for i, peer in enumerate(peers)]
    def hop(first, last, old):
        for copy in copies[old:first]: copy.wait()
        if first == 1: part[...] = part[...] + got[0]
        elif first == 4: part[...] = (part[...] + got[1]) + (got[2] + got[3])
        elif first == 7: part[...] = (part[...] + got[6]) + (got[4] + got[5])
        for copy in copies[first:last]: copy.start()
    return [lambda: hop(0, 1, 0), lambda: hop(1, 4, 0), lambda: hop(4, 7, 1), lambda: hop(7, 7, 4)]


def swap(away, into, send, recv, peer, parts):
    size = away.shape[0] // parts
    plans = []
    for i in range(parts):
        r = pl.ds(i * size, size)
        give = remote(away.at[r], into.at[r], send.at[i], recv.at[i], peer)
        plans.append([give.start, give.wait])
    return plans


def whole(s):
    return pl.BlockSpec(s, lambda i: (0,) * len(s), pipeline_mode=pl.Buffered(1))


def live_rows(len_ref, rows):
    t = lax.axis_index("tensor")
    place = lax.broadcasted_iota(jnp.int32, (rows, 1), 0)
    length = jnp.where(t == 0, len_ref[0:1], len_ref[1:2])
    return (place + t * (rows // 2)) % rows < length


def forward_pair(bq, hook, len_ref, q_ref, k_ref, v_ref, o_ref, lse_ref):
    rows = q_ref.shape[0]
    lane = lax.broadcasted_iota(jnp.int32, (1, 128), 1)
    kbias = jnp.where(live_rows(len_ref, rows), 0.0, -1e9)
    first = lane < DH

    def block(i, _):
        hook(i, rows // bq)
        place = pl.ds(pl.multiple_of(i * bq, bq), bq)
        q = q_ref[place].astype(F32)
        k, v = k_ref[...].astype(F32), v_ref[...]
        os_, ls = [], []
        for h in range(2):
            own, spare = lane // DH == h, lane == DH * (1 - h)
            qa = jnp.where(own, q, jnp.where(spare, 1.0, 0.0)).astype(BF16)
            ka = jnp.where(own, k, jnp.where(spare, kbias, 0.0)).astype(BF16)
            s = nt(qa, ka)
            m = jnp.max(s, axis=1, keepdims=True)
            p = jnp.exp(s - m)
            l = jnp.sum(p, axis=1, keepdims=True)
            os_.append(nn(p.astype(BF16), v) * (1.0 / l))
            ls.append(m + jnp.log(l))
        o_ref[place] = jnp.where(first, os_[0], os_[1]).astype(BF16)
        lse_ref[place] = jnp.where(first, ls[1], ls[0])
        return 0

    lax.fori_loop(0, rows // bq, block, 0)


def attend_forward(length, q, k, v, bq=512):
    rows, width = q.shape
    spec = pl.BlockSpec((rows, 128), lambda i: (0, i))
    return pl.pallas_call(
        functools.partial(forward_pair, bq, lambda i, n: None),
        grid=(width // 128,),
        in_specs=[LENGTHS, spec, spec, spec],
        out_specs=[spec, spec],
        out_shape=[S((rows, width), BF16), S((rows, width), F32)],
        compiler_params=pltpu.CompilerParams(vmem_limit_bytes=56 << 20),
        name="attend_forward",
    )(length, q, k, v)


def pieces_of(order, letter):
    return len({name for phase in order for name, _ in phase if name[0] == letter})


def run(plans, events):
    for name, stage in events:
        plans[name][stage]()


def front(length, hidden, shards, b_query, b_value, bq=512):
    n = len(shards)
    rows, width = 2 * hidden.shape[1], hidden.shape[2]
    half, pairs = width // 2, width // 128
    items = [(name, w, shards[w].shape[1] // parts * i, shards[w].shape[1] // parts, order) for name, (w, i, parts, order) in FRONT_ITEMS.items()]

    def kernel(*refs):
        len_ref, pair_ref, given, bq_ref, bv_ref = refs[0], refs[1], refs[2 : 2 + n], refs[2 + n], refs[3 + n]
        refs = refs[4 + n :]
        o_ref, lse_ref, outs, far_outs, mixed = refs[0], refs[1], refs[2:6], refs[6 : 3 + n], refs[3 + n]
        refs = refs[4 + n :]
        rows_s, q_s, k_s, v_s, near, mix_s, (send, recv, out_sem), sems = refs[0], refs[1], refs[2], refs[3], refs[4:7], refs[7], refs[8:11], refs[11:]
        step = pl.program_id(0)
        place = Place()
        fulls = list(near) + list(far_outs)
        local = rows // 2
        keep = pltpu.make_async_copy(pair_ref.at[place.t], rows_s.at[pl.ds(0, local)], out_sem.at[4])
        plans = {
            f"h{i}": plan
            for i, plan in enumerate(swap(pair_ref.at[1 - place.t], rows_s.at[pl.ds(local, local)], send, recv, place.beside, pieces_of(FRONT_ORDER, "h")))
        }
        for i, (name, w, at, count, order) in enumerate(items):
            plans[name] = gather_stages(place, order, given[w], fulls[w], at, count, *sems[3 * i : 3 * i + 3])
        stores = [pltpu.make_async_copy(src, dst, out_sem.at[i]) for i, (src, dst) in enumerate(zip((rows_s, q_s, k_s, v_s), outs))]
        stores.append(pltpu.make_async_copy(mix_s, mixed, out_sem.at[5]))

        def turn(i):
            for t in range(2):
                w = near[i][t].reshape(width, half).T
                for j in range(pairs // 2):
                    mix_s[j, t, i * 128 : (i + 1) * 128] = w[j * 128 : (j + 1) * 128]

        def project(full, dst, bias, scale):
            def block(i, _):
                r = pl.ds(pl.multiple_of(i * 256, 256), 256)
                for t in range(2):
                    v = nn(rows_s[r], full[t].reshape(width, half))
                    if bias is not None:
                        v = v + bias[:, t * half : (t + 1) * half]
                    dst[r, t * half : (t + 1) * half] = (v * scale).astype(BF16)
                return 0
            lax.fori_loop(0, rows // 256, block, 0)

        @pl.when(step == 0)
        def _():
            keep.start()
            place.greet(place.near)
            run(plans, FRONT_ORDER[0])
            keep.wait()
            project(near[0], q_s, bq_ref[...].reshape(1, width), 0.125)
            run(plans, FRONT_ORDER[1])
            project(near[1], k_s, None, 1.0)
            run(plans, FRONT_ORDER[2])
            project(near[2], v_s, bv_ref[...].reshape(1, width), 1.0)
            for i in range(3):
                turn(i)
            for store in stores:
                store.start()

        def hook(block, blocks):
            for i in range(pairs):
                for part in range(2):
                    if FRONT_ORDER[3 + 2 * i + part]:
                        @pl.when((step == 1 + i) & (block == part * (blocks // 2)))
                        def _():
                            run(plans, FRONT_ORDER[3 + 2 * i + part])

        @pl.when(step > 0)
        def _():
            cols = pl.ds(pl.multiple_of((step - 1) * 128, 128), 128)
            forward_pair(bq, hook, len_ref, q_s.at[:, cols], k_s.at[:, cols], v_s.at[:, cols], o_ref, lse_ref)

        @pl.when(step == pairs)
        def _():
            run(plans, FRONT_ORDER[3 + 2 * pairs])
            for store in stores:
                store.wait()

    spec = pl.BlockSpec((rows, 128), lambda i: (0, jnp.maximum(i - 1, 0)))
    flat = S((rows, width), BF16)
    full = [S((2, 4, 2, 2) + s.shape, BF16) for s in shards]
    V = pltpu.VMEM
    return pl.pallas_call(
        kernel,
        grid=(1 + pairs,),
        in_specs=[LENGTHS, HBM] + [HBM] * n + [whole((width,))] * 2,
        out_specs=[spec, spec] + [HBM] * (2 + n),
        out_shape=[flat, S((rows, width), F32), flat, flat, flat, flat] + full[3:] + [S((pairs // 2, 2, half, width), BF16)],
        scratch_shapes=[V((rows, width), BF16)] * 4 + [V(f.shape, BF16) for f in full[:3]] + [V((pairs // 2, 2, half, width), BF16), DMA((4,)), DMA((4,)), DMA((6,))]
        + [s for _ in items for s in (DMA((7,)), DMA((7,)), DMA)],
        cost_estimate=pl.CostEstimate(flops=10 * rows * rows * width, bytes_accessed=40 << 20, transcendentals=rows * rows * 12),
        compiler_params=pltpu.CompilerParams(collective_id=1, has_side_effects=True, vmem_limit_bytes=56 << 20),
        name="front",
    )(length, hidden, *shards, b_query, b_value)


def backward_pair(bk, hook, len_ref, q_ref, k_ref, v_ref, d_ref, o_ref, lse_ref, dq_ref, dk_ref, dv_ref, qa_s, ka_s, va_s, da_s, acc):
    rows = q_ref.shape[0]
    lane = lax.broadcasted_iota(jnp.int32, (1, 128), 1)
    kbias = jnp.where(live_rows(len_ref, rows), 0.0, -1e9)
    d = d_ref[...].astype(F32)
    prod = d * o_ref[...].astype(F32)
    hi, mid, lo = split3(-lse_ref[...])
    for h in range(2):
        own = lane // DH == h
        sp = DH * (1 - h)
        def pick(a, b, c, e):
            return jnp.where(lane == sp, a, jnp.where(lane == sp + 1, b, jnp.where(lane == sp + 2, c, jnp.where(lane == sp + 3, e, 0.0))))
        dh, dm, dl = split3(-jnp.sum(jnp.where(own, prod, 0.0), axis=1, keepdims=True))
        qa_s[h] = jnp.where(own, q_ref[...].astype(F32), pick(hi, mid, lo, 1.0)).astype(BF16)
        ka_s[h] = jnp.where(own, k_ref[...].astype(F32), pick(1.0, 1.0, 1.0, kbias)).astype(BF16)
        da_s[h] = jnp.where(own, d, pick(dh, dm, dl, 0.0)).astype(BF16)
        va_s[h] = jnp.where(own, v_ref[...].astype(F32), pick(1.0, 1.0, 1.0, 0.0)).astype(BF16)
    first = lane < DH
    upper = lax.broadcasted_iota(jnp.int32, (128, 1), 0) < DH
    acc[...] = jnp.zeros_like(acc)

    def block(b, _):
        hook(b, rows // bk)
        r = pl.ds(b * bk, bk)
        dks, dvs, dqs = [], [], []
        for h in range(2):
            p = jnp.exp(nt(ka_s[h, r], qa_s[h]))
            ds = (p * nt(va_s[h, r], da_s[h])).astype(BF16)
            dvs.append(nn(p.astype(BF16), d_ref[...]))
            dks.append(nn(ds, q_ref[...]))
            dqs.append(tn(k_ref[r], ds))
        dk_ref[r] = jnp.where(first, dks[0], dks[1]).astype(BF16)
        dv_ref[r] = jnp.where(first, dvs[0], dvs[1]).astype(BF16)
        acc[...] += jnp.where(upper, dqs[0], dqs[1])
        return 0

    for b in range(rows // bk):
        block(b, 0)
    dq_ref[...] = (acc[...].T * 0.125).astype(BF16)


def pair_scratch(rows):
    aug = pltpu.VMEM((2, rows, 128), BF16)
    return [aug, aug, aug, aug, pltpu.VMEM((128, rows), F32)]


def attend_backward(length, q, k, v, d, o, lse, bk=512):
    rows, width = q.shape
    spec = pl.BlockSpec((rows, 128), lambda i: (0, i))
    return pl.pallas_call(
        functools.partial(backward_pair, bk, lambda i, n: None),
        grid=(width // 128,),
        in_specs=[LENGTHS] + [spec] * 6,
        out_specs=[spec] * 3,
        out_shape=[S((rows, width), BF16)] * 3,
        scratch_shapes=pair_scratch(rows),
        compiler_params=pltpu.CompilerParams(vmem_limit_bytes=56 << 20),
        name="attend_backward",
    )(length, q, k, v, d, o, lse)


def back(length, q, k, v, d, o, lse, rows_in, mixed, grad_one, small, grads, bk=512):
    n = len(grads)
    rows, width = q.shape
    half, pairs = width // 2, width // 128
    pieces = pairs // 2
    shards = [(grads[0].shape[4], half)] * pieces + [g.shape[4:] for g in grads]
    items = []
    for name, (w, i, parts, order) in BACK_ITEMS.items():
        items.append((name, w, shards[w][1] // parts * i, shards[w][1] // parts, order))
    vb = small.shape[0] - 4

    def kernel(*refs):
        main_in, rows_ref, mixed_ref, one_ref, small_ref, given = refs[:7], refs[7], refs[8], refs[9], refs[10], refs[11 : 11 + n]
        refs = refs[11 + n :]
        pair_ref, sum_ref, outs = refs[0], refs[1], refs[2 : 2 + pieces + n]
        refs = refs[2 + pieces + n :]
        cat, rT, total, gr_s, own, rows_s, mix_s, load_sem = refs[:8]
        refs = refs[8:]
        part, got, fold_send, fold_recv, send, recv, local_sem = refs[:7]
        main_scratch, scratch = refs[7:12], refs[12:]
        step = pl.program_id(0)
        place = Place()
        local = rows // 2
        loads = [
            pltpu.make_async_copy(src, dst, load_sem.at[i])
            for i, (src, dst) in enumerate(((rows_ref, rows_s), (one_ref, total), (mixed_ref, mix_s)))
        ]
        keep = pltpu.make_async_copy(gr_s.at[pl.ds(0, local)], pair_ref.at[place.t], local_sem)
        plans = {
            f"r{i}": plan
            for i, plan in enumerate(swap(gr_s.at[pl.ds(local, local)], pair_ref.at[place.t], send, recv, place.beside, pieces_of(BACK_ORDER, "r")))
        }
        plans["sm"] = fold_stages(place, part, got, fold_send, fold_recv)
        sources = [own.at[p] for p in range(pieces)] + list(given)
        for i, (name, w, at, count, order) in enumerate(items):
            plans[name] = reduce_stages(place, order, sources[w], at, count, outs[w], scratch[9 * i : 9 * i + 9])

        @pl.when(step == 0)
        def _():
            place.greet(place.near + (place.corner, place.opposite))
            part[...] = small_ref[...]
            for load in loads:
                load.start()

        def at(i, j):
            return 2 * i + j + i // 2

        def hook(block, blocks):
            for i in range(pairs):
                for j in range(2):
                    if BACK_ORDER[at(i, j)]:
                        if block == j * (blocks // 2):
                            @pl.when(step == i)
                            def _():
                                run(plans, BACK_ORDER[at(i, j)])

        t = step % 2
        backward_pair(bk, hook, *main_in, cat.at[t, :, pl.ds(0, 128)], cat.at[t, :, pl.ds(128, 128)], cat.at[t, :, pl.ds(256, 128)], *main_scratch)

        def gather_rows(p, first):
            r = slice(first, first + local)
            v = total[r] + (nn(cat[0, r], mix_s[p, 0]) + nn(cat[1, r], mix_s[p, 1]))
            total[r] = v
            gr_s[r] = v.astype(BF16)

        @pl.when(step == 1)
        def _():
            for load in loads:
                load.wait()
            rT[...] = rows_s[...].T

        @pl.when(step % 2 == 1)
        def _():
            p = step // 2
            last = step == pairs - 1
            gather_rows(p, local)

            @pl.when(last)
            def _():
                run(plans, BACK_ORDER[-3])

            def weigh(t, _):
                own[p, t] = nn(rT[...], cat[t]).astype(BF16).reshape(own.shape[2:])
                sums = colsum(cat[t].astype(F32))
                lanes = pl.ds(pl.multiple_of(t * half + p * 128, 128), 128)
                part[vb : vb + 1, lanes] = sums[:, :128]
                part[vb + 1 : vb + 2, lanes] = sums[:, 256:]
                return 0
            weigh(0, 0)
            weigh(1, 0)
            for i in range(pieces - 1):
                @pl.when(step == 2 * i + 1)
                def _():
                    run(plans, BACK_ORDER[at(2 * i + 1, 2)])

            @pl.when(last)
            def _():
                run(plans, BACK_ORDER[-2])
            gather_rows(p, 0)

        @pl.when(step == pairs - 1)
        def _():
            keep.start()
            run(plans, BACK_ORDER[-1])
            sum_ref[...] = part[...]
            keep.wait()

    spec = pl.BlockSpec((rows, 128), lambda i: (0, i % 2 * (pairs // 2) + i // 2))
    V = pltpu.VMEM
    outs = [S(s, F32) for s in shards]
    return pl.pallas_call(
        kernel,
        grid=(pairs,),
        in_specs=[LENGTHS] + [spec] * 6 + [HBM, HBM, HBM, whole(small.shape)] + [HBM] * n,
        out_specs=[HBM, whole(small.shape)] + [whole(s) for s in shards],
        out_shape=[S((2, rows // 2, width), BF16), S(small.shape, F32)] + outs,
        scratch_shapes=[V((2, rows, half), BF16), V((width, rows), BF16), V((rows, width), F32), V((rows, width), BF16)]
        + [V((pieces, 2, 4, 2, 2) + shards[0], BF16), V((rows, width), BF16), V(mixed.shape, BF16), DMA((3,))]
        + [V(small.shape, F32), V((7,) + small.shape, F32), DMA((7,)), DMA((7,)), DMA((4,)), DMA((4,)), DMA]
        + pair_scratch(rows)
        + [s for _, w, f, c, o in items for s in reduce_scratch(o, shards[w][0], c)],
        cost_estimate=pl.CostEstimate(flops=20 * rows * rows * width, bytes_accessed=60 << 20, transcendentals=rows * rows * 12),
        compiler_params=pltpu.CompilerParams(collective_id=2, has_side_effects=True, vmem_limit_bytes=63 << 20),
        name="back",
    )(length, q, k, v, d, o, lse, rows_in, mixed, grad_one, small, *grads)


def finish(near_out, came_out, grad_hidden, owned):
    local, width = near_out.shape
    pieces = 3

    def kernel(*refs):
        near_ref, came_ref, grad_ref = refs[:3]
        given, (out_ref, hid_ref), outs, sem = refs[3:9], refs[9:11], refs[11:17], refs[17]
        t = lax.axis_index("tensor")
        moves = [(near_ref, out_ref.at[t]), (came_ref, out_ref.at[1 - t]), (grad_ref, hid_ref)]
        moves += list(zip(given[pieces:], outs[3:]))
        for i in range(3):
            for p in range(pieces):
                moves.append((given[p].at[:, pl.ds(i * 128, 128)], outs[i].at[:, pl.ds(p * 128, 128)]))
        copies = [pltpu.make_async_copy(a, b, sem.at[i]) for i, (a, b) in enumerate(moves)]
        for copy in copies:
            copy.start()
        for copy in copies:
            copy.wait()

    return pl.pallas_call(
        kernel,
        in_specs=[pl.BlockSpec(memory_space=pltpu.VMEM)] * 9,
        out_specs=[HBM] * 8,
        out_shape=[S((2, local, width), BF16)] * 2 + [S(o.shape, F32) for o in owned],
        scratch_shapes=[DMA((15,))],
        name="finish",
    )(near_out, came_out, grad_hidden, *owned)


def norm_parts(v):
    c = v - jnp.mean(v, axis=-1, keepdims=True)
    r = lax.rsqrt(jnp.mean(c * c, axis=-1, keepdims=True) + 1e-5)
    return c * r, r


def norm_back(n, r, dyg):
    return r * (dyg - jnp.mean(dyg, axis=-1, keepdims=True) - n * jnp.mean(dyg * n, axis=-1, keepdims=True))


def colsum(v):
    return jnp.sum(v, axis=0, keepdims=True)


def mlp_up_kernel(chunk, a_ref, h_ref, wo_ref, wi_hbm, wb_hbm, *refs):
    vec_refs, (bi_ref, near_ref, far_ref, mid_ref, v1_ref, v2_ref, act, gp, b2, wi_ref, wb_ref, load_sem) = refs[:6], refs[6:]
    loads = [pltpu.make_async_copy(src, dst, load_sem.at[i]) for i, (src, dst) in enumerate(((wi_hbm, wi_ref), (wb_hbm, wb_ref)))]

    @pl.when(pl.program_id(0) == 0)
    def _():
        for load in loads:
            load.start()

    half, inner = wo_ref.shape[2], wi_ref.shape[2]
    b_out, b_back, gain_one, shift_one, gain_two, shift_two = [ref[...].reshape(1, -1) for ref in vec_refs]
    v1 = h_ref[...].astype(F32) + (nt(a_ref[:, :half], wo_ref[0]) + nt(a_ref[:, half:], wo_ref[1])) + b_out
    v1_ref[...] = v1
    n1, r1 = norm_parts(v1)
    normed = n1 * gain_one + shift_one
    mid = normed.astype(BF16)
    mid_ref[...] = mid
    b2[...] = normed + b_back

    @pl.when(pl.program_id(0) == 0)
    def _():
        for load in loads:
            load.wait()

    def up(i, _):
        t = i // (inner // chunk)
        cols = pl.ds(pl.multiple_of(i % (inner // chunk) * chunk, chunk), chunk)
        hp = nn(mid, wi_ref[t, :, cols]) + bi_ref[t, :, cols]
        half_up = 0.5 + 0.5 * lax.erf(hp * math.sqrt(0.5))
        a = (hp * half_up).astype(BF16)
        act[t, :, cols] = a
        gp[t, :, cols] = (half_up + hp * (jnp.exp(hp * hp * -0.5) * (1.0 / math.sqrt(2 * math.pi)))).astype(BF16)
        b2[...] += nt(a, wb_ref[t, :, cols])
        return 0

    lax.fori_loop(0, 2 * inner // chunk, up, 0)
    v2_ref[...] = b2[...]
    n2, r2 = norm_parts(b2[...])
    out = (n2 * gain_two + shift_two).astype(BF16)
    step, steps = pl.program_id(0), pl.num_programs(0)

    @pl.when(step < steps // 2)
    def _():
        near_ref[...] = out

    @pl.when(step >= steps // 2)
    def _():
        far_ref[...] = out


def mlp_up(a, h, wo, wi, wb, vec, bi, rows=256, chunk=1536):
    total, width = a.shape
    inner = wi.shape[2]
    row = pl.BlockSpec((rows, width), lambda i: (i, 0))
    wide = pl.BlockSpec((2, rows, inner), lambda i: (0, i, 0))
    return pl.pallas_call(
        functools.partial(mlp_up_kernel, chunk),
        grid=(total // rows,),
        in_specs=[row, row, whole(wo.shape), HBM, HBM] + [whole(s.shape) for s in (*vec, bi)],
        out_specs=[
            pl.BlockSpec((rows, width), lambda i: (jnp.minimum(i, total // rows // 2 - 1), 0)),
            pl.BlockSpec((rows, width), lambda i: (jnp.maximum(i - total // rows // 2, 0), 0)),
            row, row, row, wide, wide,
        ],
        out_shape=[S((total // 2, width), BF16), S((total // 2, width), BF16), S((total, width), BF16), S((total, width), F32), S((total, width), F32), S((2, total, inner), BF16), S((2, total, inner), BF16)],
        scratch_shapes=[pltpu.VMEM((rows, width), F32), pltpu.VMEM(wi.shape, BF16), pltpu.VMEM(wb.shape, BF16), DMA((2,))],
        cost_estimate=pl.CostEstimate(flops=total * width * (8 * inner + 2 * width), bytes_accessed=40 << 20, transcendentals=4 * total * inner),
        compiler_params=pltpu.CompilerParams(vmem_limit_bytes=60 << 20),
        name="mlp_up",
    )(a, h, wo, wi, wb, *vec, bi)


def mlp_down_kernel(len_ref, a_hbm, mid_ref, cot_ref, far_ref, v1_hbm, v2_ref, wo_hbm, *refs):
    vec_refs, (wi_ref, wb_ref, act_ref, gp_ref) = refs[:6], refs[6:10]
    g1_ref, ga_ref, gwo_ref, gwi_ref, gwb_ref, small_ref, back, btT, midT, gn, sums_s, a_ref, v1_ref, wo_ref, load_sem = refs[10:]
    loads = [pltpu.make_async_copy(src, dst, load_sem.at[i]) for i, (src, dst) in enumerate(((a_hbm, a_ref), (v1_hbm, v1_ref), (wo_hbm, wo_ref)))]
    step = pl.program_id(0)
    rows, half, chunk, block = a_ref.shape[0], wo_ref.shape[2], wi_ref.shape[2], 256
    width = a_ref.shape[1]
    b_out, b_back, gain_one, shift_one, gain_two, shift_two = [ref[...].reshape(1, -1) for ref in vec_refs]

    @pl.when(step == 0)
    def _():
        for load in loads:
            load.start()
        small_ref[...] = jnp.zeros_like(small_ref)
        midT[...] = mid_ref[...].T
        live = jnp.where(live_rows(len_ref, rows), 1.0, 0.0)
        near = cot_ref.at[lax.axis_index("tensor")]
        for b in range(rows // block):
            r = slice(b * block, (b + 1) * block)
            n2, r2 = norm_parts(v2_ref[r])
            at = (b * block) % (rows // 2)
            go = (near if b < rows // block // 2 else far_ref)[at : at + block].astype(F32) * live[r]
            grad_two = norm_back(n2, r2, go * gain_two)
            bt = grad_two.astype(BF16)
            back[r] = bt
            btT[:, r] = bt.T
            gn[r] = grad_two
            small_ref[1:2] += colsum(grad_two)
            small_ref[4:5] += colsum(go * n2)
            small_ref[5:6] += colsum(go)

    gb = (nn(back[...], wb_ref[0]) * gp_ref[0].astype(F32)).astype(BF16)
    sums = colsum(gb.astype(F32))
    gwb_ref[0] = nn(btT[...], act_ref[0]).astype(BF16)
    gwi_ref[0] = nn(midT[...], gb).astype(BF16)
    gn[...] += nt(gb, wi_ref[0])
    sums_s[...] = sums
    for j in range(half * 8 // chunk):
        @pl.when(step == j)
        def _():
            for at in range(j * chunk, (j + 1) * chunk, 128):
                small_ref[8 + at // width : 9 + at // width, at % width : at % width + 128] = sums_s[:, at - j * chunk : at - j * chunk + 128]

    @pl.when(step == pl.num_programs(0) - 1)
    def _():
        for load in loads:
            load.wait()
        for b in range(rows // block):
            r = slice(b * block, (b + 1) * block)
            g = gn[r]
            n1, r1 = norm_parts(v1_ref[r])
            grad_one = norm_back(n1, r1, g * gain_one)
            bo = grad_one.astype(BF16)
            back[r] = bo
            g1_ref[r] = grad_one
            small_ref[0:1] += colsum(grad_one)
            small_ref[2:3] += colsum(g * n1)
            small_ref[3:4] += colsum(g)
            for t in range(2):
                ga_ref[r, t * half : (t + 1) * half] = nn(bo, wo_ref[t]).astype(BF16)
        btT[...] = back[...].T
        for t in range(2):
            gwo_ref[t] = nn(btT[...], a_ref[:, t * half : (t + 1) * half]).astype(BF16)


def mlp_down(length, a, mid, cot, far, v1, v2, wo, wi, wb, act, gp, vec, chunk=512):
    rows, width = a.shape
    inner = wi.shape[2]
    m = inner // chunk
    tall = pl.BlockSpec((1, rows, chunk), lambda i: (i // m, 0, i % m))
    weight = pl.BlockSpec((1, width, chunk), lambda i: (i // m, 0, i % m))
    V = pltpu.VMEM
    small = (12 + 2 * inner // width, width)
    return pl.pallas_call(
        mlp_down_kernel,
        grid=(2 * m,),
        in_specs=[LENGTHS, HBM] + [whole(s.shape) for s in (mid, cot, far)] + [HBM, whole(v2.shape), HBM] + [whole(s.shape) for s in vec] + [weight, weight, tall, tall],
        out_specs=[whole((rows, width)), whole((rows, width)), whole(wo.shape), weight, weight, whole(small)],
        out_shape=[S((rows, width), F32), S((rows, width), BF16), S(wo.shape, BF16), S(wi.shape, BF16), S(wb.shape, BF16), S(small, F32)],
        scratch_shapes=[V((rows, width), BF16), V((width, rows), BF16), V((width, rows), BF16), V((rows, width), F32), V((1, chunk), F32)]
        + [V(a.shape, BF16), V(v1.shape, F32), V(wo.shape, BF16), DMA((3,))],
        cost_estimate=pl.CostEstimate(flops=rows * width * (16 * inner + 4 * width), bytes_accessed=60 << 20, transcendentals=0),
        compiler_params=pltpu.CompilerParams(vmem_limit_bytes=62 << 20),
        name="mlp_down",
    )(length, a, mid, cot, far, v1, v2, wo, *vec, wi, wb, act, gp)


def per_device(
    hidden, lengths, cotangent, w_query, w_key, w_value, w_out, w_in, w_back,
    b_query, b_value, b_out, b_in, b_back, gain_one, shift_one, gain_two, shift_two,
):
    t = lax.axis_index("tensor")
    local = hidden.shape[1]
    width = b_query.shape[0]
    inner = b_in.shape[0]
    own_kernels = lax.axis_size("dp") == 16 and lax.axis_size("tensor") == 2
    flip = [(0, 1), (1, 0)]

    def mine(a):
        return lax.dynamic_index_in_dim(a, t, 0, keepdims=False)

    def take(a):
        other = lax.dynamic_index_in_dim(a, 1 - t, 0, keepdims=False)
        return jnp.concatenate([mine(a), lax.ppermute(other, "tensor", flip)], 0)

    def give(a):
        got = lax.ppermute(a[local:], "tensor", flip)
        first = t == 0
        return jnp.stack([jnp.where(first, a[:local], got), jnp.where(first, got, a[:local])], 0)

    def gather(w):
        return lax.all_gather(lax.all_gather(w, "dp", axis=0, tiled=True), "tensor", axis=0)

    def scatter(g):
        g = lax.psum_scatter(g, "dp", scatter_dimension=1, tiled=True)
        return lax.psum_scatter(g, "tensor", scatter_dimension=0, tiled=False).astype(F32)

    def flat(w):
        return w.reshape(2, width, -1)

    vec = (b_out, b_back, gain_one, shift_one, gain_two, shift_two)
    shards = (w_query, w_key, w_value, w_out, w_in, w_back)
    if own_kernels:
        attended, lse, rows, query, key, value, full_out, full_in, full_back, mixed = front(lengths, hidden, shards, b_query, b_value)
        full_out, full_in, full_back = flat(full_out), flat(full_in), flat(full_back)
        late_cotangent = lax.optimization_barrier((cotangent, attended))[0]
    else:
        late_cotangent = cotangent
        rows = take(hidden)
        full_query, full_key, full_value, full_out, full_in, full_back = [gather(w) for w in shards]

        def project(w):
            return jnp.concatenate([nn(rows, w[0]), nn(rows, w[1])], 1)

        query = ((project(full_query) + b_query) * 0.125).astype(BF16)
        key = project(full_key).astype(BF16)
        value = (project(full_value) + b_value).astype(BF16)
        attended, lse = attend_forward(lengths, query, key, value)
    bi = b_in.reshape(2, 1, inner // 2)
    far_cot = lax.ppermute(lax.dynamic_index_in_dim(late_cotangent, 1 - t, 0, keepdims=False), "tensor", flip)
    near_out, far_out, mid, v1, v2, act, gp = mlp_up(attended, rows, full_out, full_in, full_back, vec, bi)
    came_out = lax.ppermute(far_out, "tensor", flip)
    grad_one, grad_attended, g_out, g_in, g_back, small = mlp_down(
        lengths, attended, mid, cotangent, far_cot, v1, v2, full_out, full_in, full_back, act, gp, vec
    )
    def split(g):
        return g.reshape(2, 4, 2, 2, -1, g.shape[-1])
    vb = 8 + inner // width
    if own_kernels:
        grad_hidden, small, *owned = back(
            lengths, query, key, value, grad_attended, attended, lse, rows, mixed, grad_one, small, [split(g) for g in (g_out, g_in, g_back)]
        )
        output, grad_hidden, *owned = finish(near_out, came_out, grad_hidden, owned)
    else:
        d_query, d_key, d_value = attend_backward(lengths, query, key, value, grad_attended, attended, lse)
        total = grad_one
        grads = []
        for d, w in ((d_query, full_query), (d_key, full_key), (d_value, full_value)):
            total = total + nt(d, jnp.concatenate([w[0], w[1]], 1))
            g = tn(rows, d).astype(BF16)
            grads.append(jnp.stack([g[:, : width // 2], g[:, width // 2 :]]))
        small = small.at[vb].set(jnp.sum(d_query.astype(F32), 0)).at[vb + 1].set(jnp.sum(d_value.astype(F32), 0))
        first = t == 0
        output = jnp.stack([jnp.where(first, near_out, came_out), jnp.where(first, came_out, near_out)], 0)
        grad_hidden = give(total.astype(BF16))
        owned = [scatter(g) for g in grads + [g_out, g_in, g_back]]
        small = lax.psum(small, ("dp", "tensor"))
    return (
        output, grad_hidden, *owned,
        small[vb], small[vb + 1], small[0], small[8:vb].reshape(inner), small[1], small[2], small[3], small[4], small[5],
    )


def solution(mesh):
    rows = P(None, ("dp", "tensor"), None)
    weight = P("dp", "tensor")
    return jax.shard_map(
        per_device,
        mesh=mesh,
        in_specs=(rows, P(None, "dp"), rows) + (weight,) * 6 + (P(),) * 9,
        out_specs=(rows, rows) + (weight,) * 6 + (P(),) * 9,
        check_vma=False,
    )
```
